128 devices in a mesh: tx: 16 (over y, x), ty: 8 (over z, core).
Axes of the slice: x: 4, y: 4, z: 4, core: 2. Of those that a mesh axis runs over, the one named last changes fastest.
Arguments:
- potential: float32 [32768, 768], P(('tx', 'ty')), may hold values from -3 to 3
- gating: float32 [32768, 768], P(('tx', 'ty')), may hold values from -3 to 3
- ecs_start: float32 [512, 256, 32], P('tx', 'ty'), may hold values from -6 to 6
- templates: bfloat16 [10, 768, 768], replicated, may hold values from -0.21875 to 0.21875
- template_id: int32 [32768], P(('tx', 'ty')), may hold values from 0 to 9
- patch_src: int32 [131072], P(('tx', 'ty')), may hold values from 0 to 3071
- patch_dev: int32 [131072, 1], P(('tx', 'ty')), may hold values from 0 to 127; in each aligned block of 1024 rows (0 to 1023, 1024 to 2047, ...) at most 16 rows name the same one
- patch_dst: int32 [131072], P(('tx', 'ty')), may hold values from 0 to 3071
- patch_conduct: float32 [131072], P(('tx', 'ty')), may hold values from 0.5 to 2
- memb_point: int32 [393216], P(('tx', 'ty')), may hold values from 0 to 32767
Outputs:
- final_potential: float32 [32768, 768], P(('tx', 'ty'))
- final_ecs: float32 [512, 256, 32], P('tx', 'ty')
The draws below stay inside these ranges and needn't reach their ends.
Inputs may be any that keep to these rules, and one draw needn't show every extreme that they name: `patch_dev`: among the 1024 gap junctions listed on one device, at most 16 have their target on any one device, and some device receives exactly 16 from some device.
All inputs are finite; a program needn't handle non-finite values.
Results may differ from the reference program's by a relative error of at most 0.0003.
Values sent between devices are 32-bit elements; how exact they have to be, the bound alone decides.
No kernel may reach another device: no remote copies, remote signals or barrier semaphores. Data moves between devices by JAX's collectives and lax.ppermute only.
A program may use at most 128 MiB of HBM per device.

```python
import math
import jax
import jax.numpy as jnp
import numpy as np

NODES = 768
BLOCK = 64
TEMPLATES = 10
CELLS_DEV = 256
P_DEV = 1024
TILE = 32
SWEEPS = 4
STEPS = 2
NCELL = 32768
BLOCKS = 393216
PATCHES = 131072
CAP = 16
NX = 512
NY = 256
N_TY = 8
DEVICES = 128


def with_ends(drawn, key, smallest, top_value):
    extent = drawn.shape
    spot = [jax.random.randint(jax.random.fold_in(key, axis), (), 0, extent[axis]) for axis in range(len(extent))]
    drawn = drawn.at[tuple(spot)].set(smallest)
    longest = extent.index(max(extent))
    spot[longest] = (spot[longest] + 1) % extent[longest]
    return drawn.at[tuple(spot)].set(top_value)


def steps_of(stream_key, shape, cuts, low, top_value):
    def one(dim, parts):
        steps = jax.random.uniform(jax.random.fold_in(jax.random.fold_in(stream_key, 6), dim), (parts,), jnp.float32, low / len(cuts), top_value / len(cuts))
        return jnp.repeat(jnp.exp(steps), shape[dim] // parts).reshape((-1,) + (1,) * (len(shape) - dim - 1))

    level = one(*cuts[0])
    for cut in cuts[1:]:
        level = level * one(*cut)
    return level


def routed_block(own_key, own, number, rows, number_of, top, most, slope):
    order = jax.random.permutation(own_key, number_of)
    packed, ordinary = load_shares(number_of, rows * top, most, slope, True), load_shares(number_of, rows * top, most, slope, False)
    places = jnp.arange(number_of)

    def named(sizes, offset_by):
        used = int((sizes > 0).sum())
        fixed = max(1, used // 4)
        passed = fixed + (places - fixed + offset_by * (used - fixed)) % max(1, number_of - fixed)
        return jnp.zeros((number_of,), jnp.int32).at[order[jnp.where(places < fixed, places, passed)]].set(jnp.asarray(sizes, jnp.int32))

    sizes = jnp.where(number % 4 == 0, named(packed, number // 4), named(ordinary, number - number // 4 - 1))
    mixed = jax.random.permutation(jax.random.fold_in(own, 3), number_of)
    giver, taker = mixed[0:number_of // 2 * 2:2], mixed[1:number_of // 2 * 2:2]
    slack = jnp.minimum(sizes[giver] - 1, most - sizes[taker]) // 2
    slack = jnp.where((giver == order[0]) | (taker == order[0]) | (sizes[taker] == 0), 0, jnp.maximum(slack, 0))
    passed = jax.random.randint(jax.random.fold_in(own, 4), (number_of // 2,), 0, 1 << 20) % (slack + 1)
    sizes = sizes.at[giver].add(-passed).at[taker].add(passed)
    members = jnp.searchsorted(jnp.cumsum(sizes), jnp.arange(rows * top), side="right").astype(jnp.int32)
    listing = members.reshape(top, rows).T
    listing = listing[jax.random.permutation(jax.random.fold_in(own, 1), rows)]
    offset_by = jax.random.randint(jax.random.fold_in(own, 2), (rows, 1), 0, top)
    return jnp.take_along_axis(listing, (jnp.arange(top)[None, :] + offset_by) % top, axis=1)


def load_shares(amount, total, reach, slope, full):
    portions = [(1 << 20) // math.isqrt(grade ** slope) + 1 for grade in range(1, amount + 1)]
    largest = reach if full else min(reach, max(-(-total // amount), total * portions[0] // sum(portions)))
    least = 1 if total - largest >= amount - 1 else 0
    counts, rest = [largest] + [least] * (amount - 1), total - largest - least * (amount - 1)
    while rest > 0:
        movable = [i for i in range(1, amount) if counts[i] < largest] or [i for i in range(1, amount) if counts[i] < reach]
        mass, remaining = sum([portions[i] for i in movable]), rest
        for i in movable:
            extra = min(reach - counts[i], max(1, remaining * portions[i] // mass), rest)
            counts[i] = counts[i] + extra
            rest = rest - extra
    return np.array(counts)


def scatter_about(rng, extent, width, reach, cuts=(), held_as=jnp.bfloat16):
    entries = width * jax.random.normal(rng, extent, jnp.float32)
    if cuts:
        entries = entries * steps_of(rng, extent, cuts, -0.22, 0.18)
    return jnp.clip(entries, -reach, reach).astype(held_as)


def setup_inputs(seed: int = 0) -> dict:
    seeds = jax.random.split(jax.random.key(seed), 11)
    potential = scatter_about(seeds[0], (NCELL, NODES), 1.0, 3.0, ((0, 128),), jnp.float32)
    gating = scatter_about(seeds[1], (NCELL, NODES), 0.5, 3.0, ((0, 128),), jnp.float32)
    ecs_start = scatter_about(seeds[2], (NX, NY, TILE), 1.0, 6.0, ((0, 16), (1, 8)), jnp.float32)
    templates = scatter_about(seeds[3], (TEMPLATES, NODES, NODES), NODES ** -0.5, 0.21875)
    template_id = with_ends(jax.random.randint(seeds[4], (NCELL,), 0, TEMPLATES), jax.random.fold_in(seeds[4], 1), 0, TEMPLATES - 1).astype(jnp.int32)
    patch_src = with_ends(jax.random.randint(seeds[5], (PATCHES,), 0, CELLS_DEV * (NODES // BLOCK)), jax.random.fold_in(seeds[5], 1), 0, (CELLS_DEV * (NODES // BLOCK)) - 1).astype(jnp.int32)
    patch_dev_keys = jax.random.split(jax.random.fold_in(seeds[6], 1), PATCHES // P_DEV)
    patch_dev_turns = jax.random.permutation(jax.random.fold_in(seeds[6], 3), PATCHES // P_DEV)
    patch_dev = jax.vmap(lambda own, number: routed_block(jax.random.fold_in(seeds[6], 2), own, number, P_DEV, DEVICES, 1, CAP, 2))(patch_dev_keys, patch_dev_turns).reshape((PATCHES, 1))
    patch_dst = with_ends(jax.random.randint(seeds[7], (PATCHES,), 0, CELLS_DEV * (NODES // BLOCK)), jax.random.fold_in(seeds[7], 1), 0, (CELLS_DEV * (NODES // BLOCK)) - 1).astype(jnp.int32)
    patch_conduct = jnp.clip(jnp.exp(math.log(2.0) - 1.3862944 * jax.random.uniform(seeds[8], (PATCHES,), jnp.float32) ** steps_of(seeds[8], (PATCHES,), ((0, 128),), -0.2, 0.2)), 0.5, 2.0)
    memb_point = with_ends(jax.random.randint(seeds[9], (BLOCKS,), 0, TILE * TILE * TILE), jax.random.fold_in(seeds[9], 1), 0, (TILE * TILE * TILE) - 1).astype(jnp.int32)
    return {"potential": potential, "gating": gating, "ecs_start": ecs_start, "templates": templates, "template_id": template_id, "patch_src": patch_src, "patch_dev": patch_dev, "patch_dst": patch_dst, "patch_conduct": patch_conduct, "memb_point": memb_point}


def neighbours(phi):
    padded = jnp.pad(phi, 1)
    total = padded[2:, 1:-1, 1:-1] + padded[:-2, 1:-1, 1:-1]
    total = total + padded[1:-1, 2:, 1:-1] + padded[1:-1, :-2, 1:-1]
    return total + padded[1:-1, 1:-1, 2:] + padded[1:-1, 1:-1, :-2]


def reference(potential, gating, ecs_start, templates, template_id, patch_src, patch_dev, patch_dst, patch_conduct, memb_point):
    per_cell = NODES // BLOCK
    dev_blocks = CELLS_DEV * per_cell
    owner = (jnp.arange(PATCHES, dtype=jnp.int32) // P_DEV).astype(jnp.int32)
    source_ids = owner * dev_blocks + patch_src
    target_ids = patch_dev[:, 0] * dev_blocks + patch_dst
    block_ids = jnp.arange(BLOCKS, dtype=jnp.int32)
    device_ids = block_ids // dev_blocks
    grid_x = (device_ids // N_TY) * TILE + memb_point // (TILE * TILE)
    grid_y = (device_ids % N_TY) * TILE + (memb_point // TILE) % TILE
    grid_z = memb_point % TILE
    flat_point = ((grid_x * NY + grid_y) * TILE + grid_z).astype(jnp.int32)
    volt = potential
    recov = gating
    phi = ecs_start
    for step in range(STEPS):
        volt_bf = volt.astype(jnp.bfloat16)
        steklov = jnp.zeros((NCELL, NODES), jnp.float32)
        for index in range(TEMPLATES):
            masked = jnp.where((template_id == index)[:, None], volt_bf, jnp.zeros_like(volt_bf))
            steklov = steklov + jnp.dot(masked, templates[index], preferred_element_type=jnp.float32)
        ion = volt - volt * volt * volt / 3.0 - recov
        blocks = volt.reshape(BLOCKS, BLOCK)
        flux = patch_conduct[:, None] * (blocks[source_ids] - blocks[target_ids])
        gap = jax.ops.segment_sum(flux, target_ids, BLOCKS) - jax.ops.segment_sum(flux, source_ids, BLOCKS)
        current = steklov - ion - gap.reshape(NCELL, NODES)
        block_mean = jnp.mean(current.reshape(BLOCKS, BLOCK), axis=1)
        deposit = jax.ops.segment_sum(block_mean, flat_point, NX * NY * TILE).reshape(NX, NY, TILE)
        for sweep in range(SWEEPS):
            phi = (deposit + neighbours(phi)) / 6.5
        phi_block = phi.reshape(-1)[flat_point]
        phi_nodes = jnp.broadcast_to(phi_block[:, None], (BLOCKS, BLOCK)).reshape(NCELL, NODES)
        recov = recov + 0.05 * 0.08 * (volt + 0.7 - 0.8 * recov)
        volt = volt - 0.05 * (current + phi_nodes)
    return volt, phi
```

```python
import functools

import jax
import jax.numpy as jnp
from jax import lax
from jax.experimental import pallas as pl
from jax.experimental.pallas import tpu as pltpu
from jax.sharding import PartitionSpec as P

BLOCK = 64
SWEEPS = 4
STEPS = 2
CELLS = 256
NODES = 768
PER = 12
DEVS = 128
CAP = 16
TILE = 32
HALO = 4
F32 = jnp.float32
BF16 = jnp.bfloat16
I32 = jnp.int32
AXES = ("tx", "ty")
VMEM = pl.BlockSpec(memory_space=pltpu.VMEM)
SMEM = pl.BlockSpec(memory_space=pltpu.SMEM)


def iota(shape, dim):
    return lax.broadcasted_iota(I32, shape, dim)


def low_half(rows):
    return iota((rows, 128), 1) < 64


def regroup(number):
    value = number.astype(F32)
    cell = jnp.floor((value + 0.5) * (1.0 / PER))
    return (value - PER * cell) * CELLS + cell


def split2(x):
    hi = x.astype(BF16).astype(F32)
    return hi, x - hi


def tables(by_lane):
    def rows(at):
        hi = by_lane[16 * at : 16 * at + 16, :]
        lo = by_lane[16 * at + 16 : 16 * at + 32, :]
        return (hi * 64.0 + lo).astype(I32)

    conduct = by_lane[64:80, :] + by_lane[80:96, :] + by_lane[96:112, :]
    return rows(0), rows(2), conduct


def setup_kernel(dev_ref, src_ref, dst_ref, conduct_ref, table_ref, own_ref, own_conduct_ref):
    device = iota((128, 128), 0)
    before = (device < iota((128, 128), 1)).astype(F32).astype(BF16)
    slots = iota((16, 128), 0)
    count = jnp.zeros((128, 1), F32)
    table = jnp.zeros((128, 128), F32)
    for q in range(8):
        hit = (dev_ref[q : q + 1, :] == device).astype(F32)
        hit_bf = hit.astype(BF16)
        running = jnp.dot(hit_bf, before, preferred_element_type=F32) + count
        rank = jnp.sum(hit * running, axis=0, keepdims=True)
        count = count + jnp.sum(hit, axis=1, keepdims=True)
        here = rank.astype(I32) == slots
        parts = []
        for ref in (dst_ref, src_ref):
            number = regroup(ref[q : q + 1, :])
            hi = jnp.floor(number * (1.0 / 64.0))
            parts += [hi, number - 64.0 * hi]
        first, rest = split2(conduct_ref[q : q + 1, :])
        second, third = split2(rest)
        parts += [first, second, third, jnp.zeros((1, 128), F32)]
        values = jnp.concatenate([jnp.where(here, part, 0.0) for part in parts], axis=0)
        table = table + lax.dot_general(
            hit_bf, values.astype(BF16), (((1,), (1,)), ((), ())), preferred_element_type=F32
        )
    table_ref[...] = table
    _, own, conduct = tables(table.T)
    own_ref[...] = own
    own_conduct_ref[...] = conduct


def doubled(volt, rows_ref):
    low = low_half(CELLS)
    for j in range(PER // 2):
        pair = volt[:, 128 * j : 128 * j + 128]
        turned = pltpu.roll(pair, 64, 1)
        rows_ref[512 * j : 512 * j + 256, :] = jnp.where(low, pair, turned)
        rows_ref[512 * j + 256 : 512 * j + 512, :] = jnp.where(low, turned, pair)


def gather_rows(rows_ref, index_ref, conduct_ref, out_ref, offset, stride):
    low = low_half(1)

    def body(d, carry):
        for p in range(8):
            a = index_ref[2 * p, d]
            b = index_ref[2 * p + 1, d]
            scale = jnp.where(low, conduct_ref[2 * p, d], conduct_ref[2 * p + 1, d])
            row = jnp.where(low, rows_ref[pl.ds(a, 1), :], rows_ref[pl.ds(b, 1), :])
            out_ref[pl.ds(d * stride + offset + p, 1), :] = row * scale
        return carry

    lax.fori_loop(0, DEVS, body, 0)


def first_gather_kernel(own_ref, conduct_ref, volt_ref, out_ref, rows_ref):
    doubled(volt_ref[...], rows_ref)
    gather_rows(rows_ref, own_ref, conduct_ref, out_ref, 0, 8)


def second_gather_kernel(
    table_ref, volt_ref, sent_ref, out_ref, into_ref, into_conduct_ref, rows_ref, index_sm, conduct_sm, sem
):
    into, _, conduct = tables(table_ref[...].T)
    into_ref[...] = into
    into_conduct_ref[...] = conduct
    one = pltpu.make_async_copy(into_ref, index_sm, sem.at[0])
    two = pltpu.make_async_copy(into_conduct_ref, conduct_sm, sem.at[1])
    one.start()
    two.start()
    doubled(volt_ref[...], rows_ref)
    for d in range(DEVS):
        out_ref[16 * d : 16 * d + 8, :] = sent_ref[8 * d : 8 * d + 8, :]
    one.wait()
    two.wait()
    gather_rows(rows_ref, index_sm, conduct_sm, out_ref, 8, 16)


def degree_kernel(into_ref, into_conduct_ref, own_ref, own_conduct_ref, out_ref):
    cell = iota((CELLS, 128), 0)
    kind = iota((16, 128), 0)
    total = jnp.zeros((CELLS, 48), F32)
    for index_ref, conduct_ref in ((into_ref, into_conduct_ref), (own_ref, own_conduct_ref)):
        for s in range(CAP):
            number = index_ref[s : s + 1, :]
            hit = ((number & 255) == cell).astype(F32).astype(BF16)
            here = (number >> 8) == kind
            first, rest = split2(conduct_ref[s : s + 1, :])
            second, third = split2(rest)
            values = jnp.concatenate([jnp.where(here, x, 0.0) for x in (first, second, third)], axis=0)
            total = total + lax.dot_general(
                hit, values.astype(BF16), (((1,), (1,)), ((), ())), preferred_element_type=F32
            )
    out_ref[...] = total[:, 0:16] + total[:, 16:32] + total[:, 32:48]


def base_kernel(volt_ref, recov_ref, id_ref, degree_ref, template_ref, out_ref, volt_bf):
    index = pl.program_id(0)

    @pl.when(index == 0)
    def _():
        volt_bf[...] = volt_ref[...].astype(BF16)
        out_ref[...] = jnp.zeros_like(out_ref)

    masked = jnp.where(id_ref[...] == index, volt_bf[...], jnp.zeros((), BF16))
    out_ref[...] += jnp.dot(masked, template_ref[0], preferred_element_type=F32)

    @pl.when(index == pl.num_programs(0) - 1)
    def _():
        low = low_half(CELLS)
        for j in range(PER // 2):
            cut = slice(128 * j, 128 * j + 128)
            volt = volt_ref[:, cut]
            ion = volt - volt * volt * volt * (1.0 / 3.0) - recov_ref[:, cut]
            degree = jnp.where(low, degree_ref[:, 2 * j : 2 * j + 1], degree_ref[:, 2 * j + 1 : 2 * j + 2])
            out_ref[:, cut] += degree * volt - ion


def grid_row(point):
    return ((point >> 7) & 7) * TILE + (point >> 10)


def gap_kernel(
    into_ref,
    own_ref,
    got_ref,
    base_ref,
    point_col_ref,
    point_row_ref,
    phi_ref,
    current_ref,
    deposit_ref,
    x_low_ref,
    x_high_ref,
    y_low_ref,
    y_high_ref,
    ll_ref,
    lh_ref,
    hl_ref,
    hh_ref,
    even_in,
    odd_in,
    even_out,
    odd_out,
):
    for ref in (even_in, odd_in, even_out, odd_out):
        ref[...] = jnp.zeros_like(ref)

    def body(d, carry):
        for p in range(8):
            row = got_ref[pl.ds(d * 16 + p, 1), :]
            back = got_ref[pl.ds(d * 16 + 8 + p, 1), :]
            even_in[pl.ds(into_ref[2 * p, d], 1), :] += row
            odd_in[pl.ds(into_ref[2 * p + 1, d], 1), :] += row
            even_out[pl.ds(own_ref[2 * p, d], 1), :] += back
            odd_out[pl.ds(own_ref[2 * p + 1, d], 1), :] += back
        return carry

    lax.fori_loop(0, DEVS, body, 0)

    low = low_half(CELLS)
    lane = iota((CELLS, 128), 1)
    row_of = iota((CELLS, CELLS), 0)
    total = jnp.zeros((CELLS, 256), F32)
    for j in range(PER // 2):
        sums = []
        for k in (2 * j, 2 * j + 1):
            cut = slice(CELLS * k, CELLS * k + CELLS)
            even = even_in[cut, :] + even_out[cut, :]
            odd = odd_in[cut, :] + odd_out[cut, :]
            both = jnp.where(low, even, odd)
            sums.append(both + pltpu.roll(both, 64, 1))
        cut = slice(128 * j, 128 * j + 128)
        current = base_ref[:, cut] - jnp.where(low, sums[0], sums[1])
        current_ref[:, cut] = current
        for k, part in ((2 * j, jnp.where(low, current, 0.0)), (2 * j + 1, jnp.where(low, 0.0, current))):
            mean = jnp.sum(part, axis=1, keepdims=True) * (1.0 / BLOCK)
            hi, lo = split2(mean)
            here = (point_col_ref[:, k : k + 1] & 127) == lane
            spread = jnp.concatenate([jnp.where(here, hi, 0.0), jnp.where(here, lo, 0.0)], axis=1)
            hit = (grid_row(point_row_ref[k : k + 1, :]) == row_of).astype(F32).astype(BF16)
            total = total + jnp.dot(hit, spread.astype(BF16), preferred_element_type=F32)
    total = total[:, 0:128] + total[:, 128:256]
    for t in range(8):
        deposit_ref[:, 128 * t : 128 * t + 128] = total[TILE * t : TILE * t + TILE, :]
    far = TILE - HALO
    for array, at in ((phi_ref, 0), (deposit_ref, HALO)):
        x_low_ref[at : at + HALO, :] = array[0:HALO, :]
        x_high_ref[at : at + HALO, :] = array[far:TILE, :]
        y_low_ref[8 * at : 8 * at + TILE, :] = array[:, 0:128]
        y_high_ref[8 * at : 8 * at + TILE, :] = array[:, 896:1024]
        ll_ref[at : at + HALO, :] = array[0:HALO, 0:128]
        lh_ref[at : at + HALO, :] = array[0:HALO, 896:1024]
        hl_ref[at : at + HALO, :] = array[far:TILE, 0:128]
        hh_ref[at : at + HALO, :] = array[far:TILE, 896:1024]


def sweep_kernel(last, *refs):
    (
        place_ref,
        phi_ref,
        deposit_ref,
        x_before_ref,
        x_after_ref,
        y_before_ref,
        y_after_ref,
        bb_ref,
        ba_ref,
        ab_ref,
        aa_ref,
        current_ref,
        volt_ref,
        point_col_ref,
    ) = refs[:14]
    if last:
        volt_out, phi_out, wide_phi, wide_deposit = refs[14:]
    else:
        (
            recov_ref,
            into_ref,
            into_conduct_ref,
            own_ref,
            own_conduct_ref,
            volt_out,
            phi_out,
            recov_out,
            send_out,
            wide_phi,
            wide_deposit,
            rows_ref,
        ) = refs[14:]
    high = TILE + HALO
    for wide, at in ((wide_phi, 0), (wide_deposit, HALO)):
        wide[0:HALO, 128:1152] = x_before_ref[at : at + HALO, :]
        wide[high : high + HALO, 128:1152] = x_after_ref[at : at + HALO, :]
        wide[HALO:high, 0:128] = y_before_ref[8 * at : 8 * at + TILE, :]
        wide[HALO:high, 1152:1280] = y_after_ref[8 * at : 8 * at + TILE, :]
        wide[0:HALO, 0:128] = bb_ref[at : at + HALO, :]
        wide[0:HALO, 1152:1280] = ba_ref[at : at + HALO, :]
        wide[high : high + HALO, 0:128] = ab_ref[at : at + HALO, :]
        wide[high : high + HALO, 1152:1280] = aa_ref[at : at + HALO, :]
    wide_phi[HALO:high, 128:1152] = phi_ref[...]
    wide_deposit[HALO:high, 128:1152] = deposit_ref[...]
    shape = (TILE + 2 * HALO, 1280)
    row = iota(shape, 0)
    lane = iota(shape, 1)
    first_row = jnp.where(place_ref[0] == 0, HALO, 0)
    last_row = jnp.where(place_ref[0] == place_ref[2] - 1, high, high + HALO)
    first_lane = jnp.where(place_ref[1] == 0, 128, 0)
    last_lane = jnp.where(place_ref[1] == place_ref[3] - 1, 1152, 1280)
    inside = (row >= first_row) & (row < last_row) & (lane >= first_lane) & (lane < last_lane)
    depth = lane & (TILE - 1)
    wide_phi[...] = jnp.where(inside, wide_phi[...], 0.0)
    for sweep in range(SWEEPS):
        phi = wide_phi[...]
        total = wide_deposit[...] + pltpu.roll(phi, 1, 0) + pltpu.roll(phi, shape[0] - 1, 0)
        total = total + pltpu.roll(phi, 32, 1) + pltpu.roll(phi, shape[1] - 32, 1)
        total = total + jnp.where(depth == 0, 0.0, pltpu.roll(phi, 1, 1))
        total = total + jnp.where(depth == TILE - 1, 0.0, pltpu.roll(phi, shape[1] - 1, 1))
        wide_phi[...] = jnp.where(inside, total * (1.0 / 6.5), 0.0)
    phi = wide_phi[HALO:high, 128:1152]
    phi_out[...] = phi
    stacked = jnp.concatenate([phi[:, 128 * t : 128 * t + 128] for t in range(8)], axis=0)
    hi, lo = split2(stacked)
    pieces = jnp.concatenate([hi, lo], axis=1).astype(BF16)
    low = low_half(CELLS)
    lane = iota((CELLS, 128), 1)
    column = iota((CELLS, CELLS), 1)
    for j in range(PER // 2):
        at_patch = []
        for k in (2 * j, 2 * j + 1):
            point = point_col_ref[:, k : k + 1]
            hit = (grid_row(point) == column).astype(F32).astype(BF16)
            found = jnp.dot(hit, pieces, preferred_element_type=F32)
            found = found[:, 0:128] + found[:, 128:256]
            at_patch.append(jnp.sum(jnp.where((point & 127) == lane, found, 0.0), axis=1, keepdims=True))
        cut = slice(128 * j, 128 * j + 128)
        volt = volt_ref[:, cut]
        fresh = volt - 0.05 * (current_ref[:, cut] + jnp.where(low, at_patch[0], at_patch[1]))
        volt_out[:, cut] = fresh
        if not last:
            recov = recov_ref[:, cut]
            recov_out[:, cut] = recov + 0.05 * 0.08 * (volt + 0.7 - 0.8 * recov)
            turned = pltpu.roll(fresh, 64, 1)
            rows_ref[512 * j : 512 * j + 256, :] = jnp.where(low, fresh, turned)
            rows_ref[512 * j + 256 : 512 * j + 512, :] = jnp.where(low, turned, fresh)
    if not last:
        gather_rows(rows_ref, own_ref, own_conduct_ref, send_out, 0, 16)
        gather_rows(rows_ref, into_ref, into_conduct_ref, send_out, 8, 16)


def shaped(*shape, dtype=F32):
    return jax.ShapeDtypeStruct(shape, dtype)


def exchange(x):
    return lax.all_to_all(x, AXES, split_axis=0, concat_axis=0, tiled=True)


def send(x, by_x, by_y):
    size_x = lax.axis_size("tx")
    size_y = lax.axis_size("ty")
    if by_y == 0:
        return lax.ppermute(x, "tx", [(i, (i + by_x) % size_x) for i in range(size_x)])
    if by_x == 0:
        return lax.ppermute(x, "ty", [(i, (i + by_y) % size_y) for i in range(size_y)])
    moves = [
        (i * size_y + j, (i + by_x) % size_x * size_y + (j + by_y) % size_y)
        for i in range(size_x)
        for j in range(size_y)
    ]
    return lax.ppermute(x, AXES, moves)


def on_device(
    potential,
    gating,
    ecs_start,
    templates,
    template_id,
    patch_src,
    patch_dev,
    patch_dst,
    patch_conduct,
    memb_point,
):
    flat = (8, 128)
    table, own, own_conduct = pl.pallas_call(
        setup_kernel,
        out_shape=(shaped(128, 128), shaped(CAP, 128, dtype=I32), shaped(CAP, 128)),
        in_specs=[VMEM] * 4,
        out_specs=(VMEM,) * 3,
        name="setup",
    )(
        patch_dev.reshape(flat),
        patch_src.reshape(flat),
        patch_dst.reshape(flat),
        patch_conduct.reshape(flat),
    )
    got_table = exchange(table)
    rows_scratch = pltpu.VMEM((PER * CELLS, 128), F32)
    sent = pl.pallas_call(
        first_gather_kernel,
        out_shape=shaped(DEVS * 8, 128),
        in_specs=[SMEM, SMEM, VMEM],
        out_specs=VMEM,
        scratch_shapes=[rows_scratch],
        name="gather_source",
    )(own, own_conduct, potential)
    outgoing, into, into_conduct = pl.pallas_call(
        second_gather_kernel,
        out_shape=(shaped(DEVS * 16, 128), shaped(CAP, 128, dtype=I32), shaped(CAP, 128)),
        in_specs=[VMEM] * 3,
        out_specs=(VMEM,) * 3,
        scratch_shapes=[
            rows_scratch,
            pltpu.SMEM((CAP, 128), I32),
            pltpu.SMEM((CAP, 128), F32),
            pltpu.SemaphoreType.DMA((2,)),
        ],
        name="gather_target",
    )(got_table, potential, sent)
    degree = pl.pallas_call(
        degree_kernel,
        out_shape=shaped(CELLS, 16),
        in_specs=[VMEM] * 4,
        out_specs=VMEM,
        name="degree",
    )(into, into_conduct, own, own_conduct)

    place = jnp.stack([lax.axis_index("tx"), lax.axis_index("ty"), lax.axis_size("tx"), lax.axis_size("ty")])
    place = place.astype(I32)
    point_col = memb_point.reshape(CELLS, PER)
    point_row = point_col.T
    id_col = template_id.reshape(CELLS, 1)
    volt = potential
    recov = gating
    phi = ecs_start.reshape(TILE, TILE * TILE)
    whole = lambda *shape: pl.BlockSpec(shape, lambda i: (0,) * len(shape))
    for step in range(STEPS):
        last = step == STEPS - 1
        got = exchange(outgoing.reshape(DEVS, 16, 128)).reshape(DEVS * 16, 128)
        base = pl.pallas_call(
            base_kernel,
            grid=(templates.shape[0],),
            out_shape=shaped(CELLS, NODES),
            in_specs=[
                whole(CELLS, NODES),
                whole(CELLS, NODES),
                whole(CELLS, 1),
                whole(CELLS, 16),
                pl.BlockSpec((1, NODES, NODES), lambda i: (i, 0, 0)),
            ],
            out_specs=whole(CELLS, NODES),
            scratch_shapes=[pltpu.VMEM((CELLS, NODES), BF16)],
            cost_estimate=pl.CostEstimate(flops=3_000_000_000, bytes_accessed=14_000_000, transcendentals=0),
            name="base",
        )(volt, recov, id_col, degree, templates)
        accumulator = pltpu.VMEM((PER * CELLS, 128), F32)
        slabs = (shaped(8, 1024),) * 2 + (shaped(64, 128),) * 2 + (shaped(8, 128),) * 4
        current, deposit, *edges = pl.pallas_call(
            gap_kernel,
            out_shape=(shaped(CELLS, NODES), shaped(TILE, 1024)) + slabs,
            in_specs=[SMEM] * 2 + [VMEM] * 5,
            out_specs=(VMEM,) * 10,
            scratch_shapes=[accumulator] * 4,
            name="gap",
        )(into, own, got, base, point_col, point_row, phi)
        ways = ((-1, 0), (1, 0), (0, -1), (0, 1), (-1, -1), (-1, 1), (1, -1), (1, 1))
        came = [send(edge, *way) for edge, way in zip(edges, ways)]
        x_after, x_before, y_after, y_before, aa, ab, ba, bb = came
        operands = [place, phi, deposit, x_before, x_after, y_before, y_after, bb, ba, ab, aa, current, volt, point_col]
        specs = [SMEM] + [VMEM] * 13
        wide = [pltpu.VMEM((TILE + 2 * HALO, 1280), F32)] * 2
        outs = (shaped(CELLS, NODES), shaped(TILE, 1024))
        if last:
            volt, phi = pl.pallas_call(
                functools.partial(sweep_kernel, True),
                out_shape=outs,
                in_specs=specs,
                out_specs=(VMEM,) * 2,
                scratch_shapes=wide,
                name="sweep_last",
            )(*operands)
        else:
            volt, phi, recov, outgoing = pl.pallas_call(
                functools.partial(sweep_kernel, False),
                out_shape=outs + (shaped(CELLS, NODES), shaped(DEVS * 16, 128)),
                in_specs=specs + [VMEM] + [SMEM] * 4,
                out_specs=(VMEM,) * 4,
                scratch_shapes=wide + [rows_scratch],
                name="sweep",
            )(*operands, recov, into, into_conduct, own, own_conduct)
    return (volt, phi.reshape(TILE, TILE, TILE))


def solution(mesh):
    return jax.shard_map(
        on_device,
        mesh=mesh,
        in_specs=(
            P(("tx", "ty"), None),
            P(("tx", "ty"), None),
            P("tx", "ty", None),
            P(),
            P(("tx", "ty")),
            P(("tx", "ty")),
            P(("tx", "ty"), None),
            P(("tx", "ty")),
            P(("tx", "ty")),
            P(("tx", "ty")),
        ),
        out_specs=(P(("tx", "ty"), None), P("tx", "ty", None)),
        check_vma=False,
    )
```

```python
import functools

import jax
import jax.numpy as jnp
from jax import lax
from jax.experimental import pallas as pl
from jax.experimental.pallas import tpu as pltpu
from jax.sharding import PartitionSpec as P

BLOCK = 64
SWEEPS = 4
STEPS = 2
CELLS = 256
NODES = 768
PER = 12
DEVS = 128
CAP = 16
TILE = 32
HALO = 4
TILES = 8
F32 = jnp.float32
BF16 = jnp.bfloat16
I32 = jnp.int32
AXES = ("tx", "ty")
VMEM = pl.BlockSpec(memory_space=pltpu.VMEM)
SMEM = pl.BlockSpec(memory_space=pltpu.SMEM)
NT = (((1,), (1,)), ((), ()))
TN = (((0,), (0,)), ((), ()))


def iota(shape, dim):
    return lax.broadcasted_iota(I32, shape, dim)


def low_half(rows):
    return iota((rows, 128), 1) < 64


def flag(condition):
    return condition.astype(F32).astype(BF16)


def regroup(number):
    value = number.astype(F32)
    cell = jnp.floor((value + 0.5) * (1.0 / PER))
    return (value - PER * cell) * CELLS + cell


def split2(x):
    hi = x.astype(BF16).astype(F32)
    return hi, x - hi


def setup_kernel(dev_ref, src_ref, dst_ref, conduct_ref, table_ref):
    device = iota((128, 128), 0)
    before = flag(device < iota((128, 128), 1))
    slots = iota((16, 128), 0)
    count = jnp.zeros((128, 1), F32)
    table = jnp.zeros((128, 128), F32)
    for q in range(8):
        hit = (dev_ref[q : q + 1, :] == device).astype(F32)
        hit_bf = hit.astype(BF16)
        running = jnp.dot(hit_bf, before, preferred_element_type=F32) + count
        rank = jnp.sum(hit * running, axis=0, keepdims=True)
        count = count + jnp.sum(hit, axis=1, keepdims=True)
        here = rank.astype(I32) == slots
        parts = []
        for ref in (dst_ref, src_ref):
            number = regroup(ref[q : q + 1, :])
            hi = jnp.floor(number * (1.0 / 64.0))
            parts += [hi, number - 64.0 * hi]
        first, rest = split2(conduct_ref[q : q + 1, :])
        second, third = split2(rest)
        parts += [first, second, third, jnp.zeros((1, 128), F32)]
        values = jnp.concatenate([jnp.where(here, part, 0.0) for part in parts], axis=0)
        table = table + lax.dot_general(hit_bf, values.astype(BF16), NT, preferred_element_type=F32)
    table_ref[...] = table


def decode(table, first_lane, scratch):
    scratch[...] = table
    lane = iota((16, 128), 1)
    out = jnp.zeros((16, 128), F32)
    for dl in range(8):
        rows = scratch[pl.ds(dl, 16, stride=8), :]
        out = jnp.where((lane >> 4) == dl, pltpu.roll(rows, (16 * dl - first_lane) % 128, 1), out)
    return out


def doubled(volt, rows_ref):
    low = low_half(CELLS)
    for j in range(PER // 2):
        pair = volt[:, 128 * j : 128 * j + 128]
        turned = pltpu.roll(pair, 64, 1)
        rows_ref[512 * j : 512 * j + 256, :] = jnp.where(low, pair, turned)
        rows_ref[512 * j + 256 : 512 * j + 512, :] = jnp.where(low, turned, pair)


def gather_rows(rows_ref, index_ref, scale_ref, out_ref, offset, stride):
    low = low_half(1)

    def body(r, carry):
        scale_base = pl.multiple_of(r * 64, 64)
        out_base = pl.multiple_of(r * (8 * stride), 8 * stride)
        for m in range(64):
            a = index_ref[r, 2 * m]
            b = index_ref[r, 2 * m + 1]
            row = jnp.where(low, rows_ref[pl.ds(a, 1), :], rows_ref[pl.ds(b, 1), :])
            place = (m // 8) * stride + offset + m % 8
            out_ref[pl.ds(out_base + place, 1), :] = row * scale_ref[pl.ds(scale_base + m, 1), :]
        return carry

    lax.fori_loop(0, DEVS // 8, body, 0)


def gather_kernel(incoming, *refs):
    if incoming:
        table_ref, volt_ref, sent_ref, out_ref = refs[:4]
    else:
        table_ref, volt_ref, out_ref = refs[:3]
    index_ref, conduct_ref, scale_ref, rows_ref, scratch, index_sm, sem = refs[-7:]
    table = table_ref[...]
    numbers = 64.0 * table + pltpu.roll(table, 112, 1)
    index_ref[...] = decode(numbers, 0 if incoming else 32, scratch).astype(I32)
    copy = pltpu.make_async_copy(index_ref, index_sm, sem)
    copy.start()
    conducts = table + pltpu.roll(table, 112, 1) + pltpu.roll(table, 96, 1)
    conduct_ref[...] = decode(conducts, 64, scratch)
    part = iota((128, 1024), 0)
    lane = iota((128, 1024), 1)
    spread = flag((part >= 64) & (part < 112) & ((part & 15) == (lane >> 6)))
    scale = jnp.dot(table.astype(BF16), spread, preferred_element_type=F32)
    for p in range(8):
        scale_ref[pl.ds(p, DEVS, stride=8), :] = scale[:, 128 * p : 128 * p + 128]
    doubled(volt_ref[...], rows_ref)
    if incoming:
        for d in range(DEVS):
            out_ref[16 * d : 16 * d + 8, :] = sent_ref[8 * d : 8 * d + 8, :]
    copy.wait()
    if incoming:
        gather_rows(rows_ref, index_sm, scale_ref, out_ref, 8, 16)
    else:
        gather_rows(rows_ref, index_sm, scale_ref, out_ref, 0, 8)


def expander(rows, j):
    return (iota((rows, 128), 0) & 15) == 2 * j + (iota((rows, 128), 1) >> 6)


def prepare_kernel(into_ref, into_conduct_ref, own_ref, own_conduct_ref, id_ref, ecs_ref, degree_ref, id_out, phi_out):
    cell = iota((CELLS, 128), 0)
    kind = iota((16, 128), 0)
    total = jnp.zeros((48, CELLS), F32)
    for index_ref, conduct_ref in ((into_ref, into_conduct_ref), (own_ref, own_conduct_ref)):
        for s in range(CAP):
            number = index_ref[s : s + 1, :]
            hit = flag((number & 255) == cell)
            here = (number >> 8) == kind
            first, rest = split2(conduct_ref[s : s + 1, :])
            second, third = split2(rest)
            values = jnp.concatenate([jnp.where(here, x, 0.0) for x in (first, second, third)], axis=0)
            total = total + lax.dot_general(values.astype(BF16), hit, NT, preferred_element_type=F32)
    total = total[0:16, :] + total[16:32, :] + total[32:48, :]
    first, rest = split2(total)
    second, third = split2(rest)
    pieces = jnp.concatenate([first, second, third], axis=0).astype(BF16)
    for j in range(PER // 2):
        degree_ref[:, 128 * j : 128 * j + 128] = lax.dot_general(
            pieces, flag(expander(48, j)), TN, preferred_element_type=F32
        )
    number = iota((16, 128), 0).astype(F32).astype(BF16)
    for half in range(2):
        hit = flag(id_ref[half : half + 1, :] == kind)
        id_out[128 * half : 128 * half + 128, :] = lax.dot_general(hit, number, TN, preferred_element_type=F32)
    for t in range(TILES):
        for y in range(4):
            rows = ecs_ref[pl.ds(4 * t + y, TILE, stride=TILE), :]
            phi_out[TILE * t : TILE * t + TILE, 32 * y : 32 * y + 32] = rows


def base_kernel(volt_ref, recov_ref, id_ref, degree_ref, template_ref, out_ref, volt_bf):
    index = pl.program_id(0)

    @pl.when(index == 0)
    def _():
        volt_bf[...] = volt_ref[...].astype(BF16)
        out_ref[...] = jnp.zeros_like(out_ref)

    mine = id_ref[...] == index.astype(F32)
    masked = jnp.concatenate(
        [
            jnp.where(mine, volt_bf[:, 128 * j : 128 * j + 128], jnp.zeros((), BF16))
            for j in range(PER // 2)
        ],
        axis=1,
    )
    out_ref[...] += jnp.dot(masked, template_ref[0], preferred_element_type=F32)

    @pl.when(index == pl.num_programs(0) - 1)
    def _():
        volt = volt_ref[...]
        ion = volt - volt * volt * volt * (1.0 / 3.0) - recov_ref[...]
        out_ref[...] += degree_ref[...] * volt - ion


def grid_row(point):
    return ((point >> 7) & 7) * TILE + (point >> 10)


def gap_kernel(
    into_ref,
    own_ref,
    got_ref,
    base_ref,
    point_ref,
    phi_ref,
    current_ref,
    deposit_ref,
    x_low_ref,
    x_high_ref,
    y_low_ref,
    y_high_ref,
    even_in,
    odd_in,
    even_out,
    odd_out,
):
    for ref in (even_in, odd_in, even_out, odd_out):
        ref[...] = jnp.zeros_like(ref)

    def body(r, carry):
        base = pl.multiple_of(r * 128, 128)
        for m in range(64):
            at = (m // 8) * 16 + m % 8
            row = got_ref[pl.ds(base + at, 1), :]
            back = got_ref[pl.ds(base + (at + 8), 1), :]
            even_in[pl.ds(into_ref[r, 2 * m], 1), :] += row
            odd_in[pl.ds(into_ref[r, 2 * m + 1], 1), :] += row
            even_out[pl.ds(own_ref[r, 2 * m], 1), :] += back
            odd_out[pl.ds(own_ref[r, 2 * m + 1], 1), :] += back
        return carry

    lax.fori_loop(0, DEVS // 8, body, 0)

    low = low_half(CELLS)
    means = jnp.zeros((16, CELLS), F32)
    for j in range(PER // 2):
        sums = []
        for k in (2 * j, 2 * j + 1):
            cut = slice(CELLS * k, CELLS * k + CELLS)
            even = even_in[cut, :] + even_out[cut, :]
            odd = odd_in[cut, :] + odd_out[cut, :]
            both = jnp.where(low, even, odd)
            sums.append(both + pltpu.roll(both, 64, 1))
        cut = slice(128 * j, 128 * j + 128)
        current = base_ref[:, cut] - jnp.where(low, sums[0], sums[1])
        current_ref[:, cut] = current
        weights = jnp.where(expander(16, j), 1.0 / BLOCK, 0.0).astype(BF16)
        for part in split2(current):
            means = means + lax.dot_general(weights, part.astype(BF16), NT, preferred_element_type=F32)
    mean_hi, mean_lo = split2(means)
    row_of = iota((CELLS, CELLS), 0)
    column_of = iota((128, CELLS), 0)
    total = jnp.zeros((CELLS, 256), F32)
    for k in range(PER):
        point = point_ref[k : k + 1, :]
        hit = flag(grid_row(point) == row_of)
        here = (point & 127) == column_of
        spread = [jnp.where(here, x[k : k + 1, :], 0.0) for x in (mean_hi, mean_lo)]
        spread = jnp.concatenate(spread, axis=0).astype(BF16)
        total = total + lax.dot_general(hit, spread, NT, preferred_element_type=F32)
    deposit_ref[...] = total[:, 0:128] + total[:, 128:256]
    for array, at, across in ((phi_ref, 0, 0), (deposit_ref, HALO, TILE)):
        for t in range(TILES):
            start = TILE * t
            x_low_ref[8 * t + at : 8 * t + at + HALO, :] = array[start : start + HALO, :]
            x_high_ref[8 * t + at : 8 * t + at + HALO, :] = array[start + TILE - HALO : start + TILE, :]
        y_low_ref[across : across + TILE, :] = array[0:TILE, :]
        y_high_ref[across : across + TILE, :] = array[TILE * (TILES - 1) :, :]


ROWS = TILE + 2 * HALO
LEAD = 8


def sweep_kernel(last, *refs):
    place_ref, phi_ref, deposit_ref, x_before_ref, x_after_ref, y_before_ref, y_after_ref = refs[:7]
    current_ref, volt_ref, point_ref = refs[7:10]
    if last:
        volt_out, phi_out, wide_phi, wide_deposit, found_ref = refs[10:]
    else:
        recov_ref, into_ref, into_scale_ref, own_ref, own_scale_ref = refs[10:15]
        volt_out, phi_out, recov_out, send_out, wide_phi, wide_deposit, found_ref, rows_ref = refs[15:]
    end = LEAD + ROWS
    high = LEAD + HALO + TILE
    for wide, array, at, across in ((wide_phi, phi_ref, 0, 0), (wide_deposit, deposit_ref, HALO, TILE)):
        for t in range(TILES):
            wide[t + 1, LEAD : LEAD + HALO, :] = x_before_ref[8 * t + at : 8 * t + at + HALO, :]
            wide[t + 1, LEAD + HALO : high, :] = array[TILE * t : TILE * t + TILE, :]
            wide[t + 1, high:end, :] = x_after_ref[8 * t + at : 8 * t + at + HALO, :]
        for t, came in ((0, y_before_ref), (TILES + 1, y_after_ref)):
            wide[t, LEAD : LEAD + HALO, :] = came[at : at + HALO, :]
            wide[t, LEAD + HALO : high, :] = came[8 + across : 8 + across + TILE, :]
            wide[t, high:end, :] = came[72 + at : 72 + at + HALO, :]
    shape = (ROWS, 128)
    row = iota(shape, 0)
    lane = iota(shape, 1)
    depth = lane & (TILE - 1)
    first_row = jnp.where(place_ref[0] == 0, HALO, 0)
    last_row = jnp.where(place_ref[0] == place_ref[2] - 1, HALO + TILE, ROWS)
    inside = (row >= first_row) & (row < last_row)
    first_tile = jnp.where(place_ref[1] == 0, 1, 0)
    last_tile = jnp.where(place_ref[1] == place_ref[3] - 1, TILES + 1, TILES + 2)
    scale = jnp.where(inside, 1.0 / 6.5, 0.0)
    side = [jnp.where((t >= first_tile) & (t < last_tile), 1.0, 0.0) for t in (0, TILES + 1)]
    edge = {0: scale * side[0], TILES + 1: scale * side[1]}
    for t in range(TILES + 2):
        wide_phi[t, 0:LEAD, :] = jnp.zeros((LEAD, 128), F32)
        wide_phi[t, end : end + 8, :] = jnp.zeros((8, 128), F32)
        keep = jnp.where(inside, side[0 if t == 0 else 1], 0.0) if t in edge else jnp.where(inside, 1.0, 0.0)
        wide_phi[t, LEAD:end, :] = jnp.where(keep > 0.0, wide_phi[t, LEAD:end, :], 0.0)
    nothing = jnp.zeros(shape, F32)
    for sweep in range(SWEEPS):
        middle = [wide_phi[t, LEAD:end, :] for t in range(TILES + 2)]
        fresh = []
        ups = [pltpu.roll(x, 32, 1) for x in middle]
        downs = [pltpu.roll(x, 96, 1) for x in middle]
        for t in range(TILES + 2):
            total = wide_deposit[t, LEAD:end, :]
            total = total + wide_phi[t, LEAD - 1 : end - 1, :] + wide_phi[t, LEAD + 1 : end + 1, :]
            total = total + jnp.where(lane < 32, ups[t - 1] if t else nothing, ups[t])
            total = total + jnp.where(lane >= 96, downs[t + 1] if t <= TILES else nothing, downs[t])
            total = total + jnp.where(depth == 0, 0.0, pltpu.roll(middle[t], 1, 1))
            total = total + jnp.where(depth == TILE - 1, 0.0, pltpu.roll(middle[t], 127, 1))
            fresh.append(jnp.where(edge.get(t, scale) > 0.0, total * (1.0 / 6.5), 0.0))
        for t in range(TILES + 2):
            wide_phi[t, LEAD:end, :] = fresh[t]
    tiles = [wide_phi[t + 1, LEAD + HALO : high, :] for t in range(TILES)]
    if last:
        for t in range(TILES):
            for y in range(4):
                turned = tiles[t] if y == 0 else pltpu.roll(tiles[t], 128 - 32 * y, 1)
                phi_out[pl.ds(4 * t + y, TILE, stride=TILE), :] = turned[:, 0:TILE]
    else:
        for t in range(TILES):
            phi_out[TILE * t : TILE * t + TILE, :] = tiles[t]
    turned = jnp.concatenate(tiles, axis=0).T
    pieces = jnp.concatenate(split2(turned), axis=0).astype(BF16)
    row_of = iota((CELLS, CELLS), 0)
    column_of = iota((128, CELLS), 0)
    found_ref[...] = jnp.zeros_like(found_ref)
    for k in range(PER):
        point = point_ref[k : k + 1, :]
        hit = flag(grid_row(point) == row_of)
        found = jnp.dot(pieces, hit, preferred_element_type=F32)
        found = found[0:128, :] + found[128:256, :]
        here = (point & 127) == column_of
        found_ref[k : k + 1, :] = jnp.sum(jnp.where(here, found, 0.0), axis=0, keepdims=True)
    found = jnp.concatenate(split2(found_ref[...]), axis=0).astype(BF16)
    low = low_half(CELLS)
    for j in range(PER // 2):
        cut = slice(128 * j, 128 * j + 128)
        at_node = lax.dot_general(found, flag(expander(32, j)), TN, preferred_element_type=F32)
        volt = volt_ref[:, cut]
        fresh = volt - 0.05 * (current_ref[:, cut] + at_node)
        volt_out[:, cut] = fresh
        if not last:
            recov = recov_ref[:, cut]
            recov_out[:, cut] = recov + 0.05 * 0.08 * (volt + 0.7 - 0.8 * recov)
            turned = pltpu.roll(fresh, 64, 1)
            rows_ref[512 * j : 512 * j + 256, :] = jnp.where(low, fresh, turned)
            rows_ref[512 * j + 256 : 512 * j + 512, :] = jnp.where(low, turned, fresh)
    if not last:
        gather_rows(rows_ref, own_ref, own_scale_ref, send_out, 0, 16)
        gather_rows(rows_ref, into_ref, into_scale_ref, send_out, 8, 16)


def shaped(*shape, dtype=F32):
    return jax.ShapeDtypeStruct(shape, dtype)


def exchange(x):
    return lax.all_to_all(x, AXES, split_axis=0, concat_axis=0, tiled=True)


def shift(x, axis, by):
    size = lax.axis_size(axis)
    return lax.ppermute(x, axis, [(i, (i + by) % size) for i in range(size)])


def on_device(
    potential,
    gating,
    ecs_start,
    templates,
    template_id,
    patch_src,
    patch_dev,
    patch_dst,
    patch_conduct,
    memb_point,
):
    flat = (8, 128)
    table = pl.pallas_call(
        setup_kernel,
        out_shape=shaped(128, 128),
        in_specs=[VMEM] * 4,
        out_specs=VMEM,
        name="setup",
    )(
        patch_dev.reshape(flat),
        patch_src.reshape(flat),
        patch_dst.reshape(flat),
        patch_conduct.reshape(flat),
    )
    got_table = exchange(table)
    rows_scratch = pltpu.VMEM((PER * CELLS, 128), F32)
    tables_out = (shaped(16, 128, dtype=I32), shaped(16, 128), shaped(DEVS * 8, 128))
    gather_scratch = [
        rows_scratch,
        pltpu.VMEM((128, 128), F32),
        pltpu.SMEM((16, 128), I32),
        pltpu.SemaphoreType.DMA,
    ]
    sent, own, own_conduct, own_scale = pl.pallas_call(
        functools.partial(gather_kernel, False),
        out_shape=(shaped(DEVS * 8, 128),) + tables_out,
        in_specs=[VMEM] * 2,
        out_specs=(VMEM,) * 4,
        scratch_shapes=gather_scratch,
        name="gather_source",
    )(table, potential)
    outgoing, into, into_conduct, into_scale = pl.pallas_call(
        functools.partial(gather_kernel, True),
        out_shape=(shaped(DEVS * 16, 128),) + tables_out,
        in_specs=[VMEM] * 3,
        out_specs=(VMEM,) * 4,
        scratch_shapes=gather_scratch,
        name="gather_target",
    )(got_table, potential, sent)
    degree, id_wide, phi = pl.pallas_call(
        prepare_kernel,
        out_shape=(shaped(CELLS, NODES), shaped(CELLS, 128), shaped(TILE * TILES, 128)),
        in_specs=[VMEM] * 6,
        out_specs=(VMEM,) * 3,
        name="prepare",
    )(into, into_conduct, own, own_conduct, template_id.reshape(2, 128), ecs_start.reshape(TILE * TILE, TILE))

    place = jnp.stack([lax.axis_index("tx"), lax.axis_index("ty"), lax.axis_size("tx"), lax.axis_size("ty")])
    place = place.astype(I32)
    points = memb_point.reshape(CELLS, PER).T
    volt = potential
    recov = gating
    whole = lambda *shape: pl.BlockSpec(shape, lambda i: (0,) * len(shape))
    for step in range(STEPS):
        last = step == STEPS - 1
        got = exchange(outgoing.reshape(DEVS, 16, 128)).reshape(DEVS * 16, 128)
        base = pl.pallas_call(
            base_kernel,
            grid=(templates.shape[0],),
            out_shape=shaped(CELLS, NODES),
            in_specs=[
                whole(CELLS, NODES),
                whole(CELLS, NODES),
                whole(CELLS, 128),
                whole(CELLS, NODES),
                pl.BlockSpec((1, NODES, NODES), lambda i: (i, 0, 0)),
            ],
            out_specs=whole(CELLS, NODES),
            scratch_shapes=[pltpu.VMEM((CELLS, NODES), BF16)],
            cost_estimate=pl.CostEstimate(flops=3_000_000_000, bytes_accessed=14_000_000, transcendentals=0),
            name="base",
        )(volt, recov, id_wide, degree, templates)
        accumulator = pltpu.VMEM((PER * CELLS, 128), F32)
        current, deposit, x_low, x_high, y_low, y_high = pl.pallas_call(
            gap_kernel,
            out_shape=(shaped(CELLS, NODES), shaped(TILE * TILES, 128)) + (shaped(64, 128),) * 4,
            in_specs=[SMEM] * 2 + [VMEM] * 4,
            out_specs=(VMEM,) * 6,
            scratch_shapes=[accumulator] * 4,
            name="gap",
        )(into, own, got, base, points, phi)
        x_before = shift(x_high, "tx", 1)
        x_after = shift(x_low, "tx", -1)
        y_low = jnp.concatenate([x_before[0:8], y_low, x_after[0:8]])
        y_high = jnp.concatenate([x_before[56:64], y_high, x_after[56:64]])
        y_before = shift(y_high, "ty", 1)
        y_after = shift(y_low, "ty", -1)
        operands = [place, phi, deposit, x_before, x_after, y_before, y_after, current, volt, points]
        specs = [SMEM] + [VMEM] * 9
        wide = [pltpu.VMEM((TILES + 2, LEAD + ROWS + 8, 128), F32)] * 2 + [pltpu.VMEM((16, CELLS), F32)]
        if last:
            volt, phi = pl.pallas_call(
                functools.partial(sweep_kernel, True),
                out_shape=(shaped(CELLS, NODES), shaped(TILE * TILE, TILE)),
                in_specs=specs,
                out_specs=(VMEM,) * 2,
                scratch_shapes=wide,
                name="sweep_last",
            )(*operands)
        else:
            volt, phi, recov, outgoing = pl.pallas_call(
                functools.partial(sweep_kernel, False),
                out_shape=(
                    shaped(CELLS, NODES),
                    shaped(TILE * TILES, 128),
                    shaped(CELLS, NODES),
                    shaped(DEVS * 16, 128),
                ),
                in_specs=specs + [VMEM, SMEM, VMEM, SMEM, VMEM],
                out_specs=(VMEM,) * 4,
                scratch_shapes=wide + [rows_scratch],
                name="sweep",
            )(*operands, recov, into, into_scale, own, own_scale)
    return (volt, phi.reshape(TILE, TILE, TILE))


def solution(mesh):
    return jax.shard_map(
        on_device,
        mesh=mesh,
        in_specs=(
            P(("tx", "ty"), None),
            P(("tx", "ty"), None),
            P("tx", "ty", None),
            P(),
            P(("tx", "ty")),
            P(("tx", "ty")),
            P(("tx", "ty"), None),
            P(("tx", "ty")),
            P(("tx", "ty")),
            P(("tx", "ty")),
        ),
        out_specs=(P(("tx", "ty"), None), P("tx", "ty", None)),
        check_vma=False,
    )
```

```python
import functools

import jax
import jax.numpy as jnp
from jax import lax
from jax.experimental import pallas as pl
from jax.experimental.pallas import tpu as pltpu
from jax.sharding import PartitionSpec as P

BLOCK = 64
SWEEPS = 4
STEPS = 2
CELLS = 256
NODES = 768
PER = 12
DEVS = 128
CAP = 16
TILE = 32
HALO = 4
TILES = 8
F32 = jnp.float32
BF16 = jnp.bfloat16
I32 = jnp.int32
AXES = ("tx", "ty")
VMEM = pl.BlockSpec(memory_space=pltpu.VMEM)
SMEM = pl.BlockSpec(memory_space=pltpu.SMEM)
NT = (((1,), (1,)), ((), ()))
TN = (((0,), (0,)), ((), ()))
PARAMS = pltpu.CompilerParams(vmem_limit_bytes=67_043_328)


def iota(shape, dim):
    return lax.broadcasted_iota(I32, shape, dim)


def low_half(rows):
    return iota((rows, 128), 1) < 64


def flag(condition):
    return condition.astype(F32).astype(BF16)


def regroup(number):
    value = number.astype(F32)
    cell = jnp.floor((value + 0.5) * (1.0 / PER))
    return (value - PER * cell) * CELLS + cell


def split2(x):
    hi = x.astype(BF16).astype(F32)
    return hi, x - hi


def setup_kernel(dev_ref, src_ref, dst_ref, conduct_ref, table_ref):
    device = iota((128, 128), 0)
    before = flag(device < iota((128, 128), 1))
    slots = iota((16, 128), 0)
    count = jnp.zeros((128, 1), F32)
    table = jnp.zeros((128, 128), F32)
    for q in range(8):
        hit = (dev_ref[q : q + 1, :] == device).astype(F32)
        hit_bf = hit.astype(BF16)
        running = jnp.dot(hit_bf, before, preferred_element_type=F32) + count
        rank = jnp.sum(hit * running, axis=0, keepdims=True)
        count = count + jnp.sum(hit, axis=1, keepdims=True)
        here = rank.astype(I32) == slots
        parts = []
        for ref in (dst_ref, src_ref):
            number = regroup(ref[q : q + 1, :])
            hi = jnp.floor(number * (1.0 / 64.0))
            parts += [hi, number - 64.0 * hi]
        first, rest = split2(conduct_ref[q : q + 1, :])
        second, third = split2(rest)
        parts += [first, second, third, jnp.zeros((1, 128), F32)]
        values = jnp.concatenate([jnp.where(here, part, 0.0) for part in parts], axis=0)
        table = table + lax.dot_general(hit_bf, values.astype(BF16), NT, preferred_element_type=F32)
    table_ref[...] = table


def decode(table, first_lane, scratch):
    scratch[...] = table
    lane = iota((16, 128), 1)
    out = jnp.zeros((16, 128), F32)
    for dl in range(8):
        rows = scratch[pl.ds(dl, 16, stride=8), :]
        out = jnp.where((lane >> 4) == dl, pltpu.roll(rows, (16 * dl - first_lane) % 128, 1), out)
    return out


def doubled(volt, rows_ref):
    low = low_half(CELLS)
    for j in range(PER // 2):
        pair = volt[:, 128 * j : 128 * j + 128]
        turned = pltpu.roll(pair, 64, 1)
        rows_ref[512 * j : 512 * j + 256, :] = jnp.where(low, pair, turned)
        rows_ref[512 * j + 256 : 512 * j + 512, :] = jnp.where(low, turned, pair)


def start_slots(index_ref, slots, sem):
    copies = [
        pltpu.make_async_copy(index_ref.at[pl.ds(s, 1), :], slot, sem.at[s]) for s, slot in enumerate(slots)
    ]
    for copy in copies:
        copy.start()
    return copies


def gather_rows(rows_ref, slots, scale_ref, out_ref, offset, stride):
    low = low_half(1)

    def body(i, carry):
        for u in range(2):
            d = 2 * i + u
            scale_base = pl.multiple_of(d * 8, 8)
            out_base = pl.multiple_of(d * stride, 8)
            for p in range(8):
                a = slots[p][0, d]
                b = slots[p + 8][0, d]
                row = jnp.where(low, rows_ref[pl.ds(a, 1), :], rows_ref[pl.ds(b, 1), :])
                out_ref[pl.ds(out_base + (offset + p), 1), :] = row * scale_ref[pl.ds(scale_base + p, 1), :]
        return carry

    lax.fori_loop(0, DEVS // 2, body, 0)


def gather_kernel(incoming, *refs):
    if incoming:
        table_ref, volt_ref, sent_ref, out_ref = refs[:4]
        refs = refs[4:]
    else:
        table_ref, volt_ref, out_ref = refs[:3]
        refs = refs[3:]
    index_ref, number_ref, conduct_ref, scale_ref, rows_ref, scratch = refs[:6]
    slots, sem = refs[6:22], refs[22]
    first = 0 if incoming else 32
    table = table_ref[...]
    numbers = 64.0 * table + pltpu.roll(table, 112, 1)
    index_ref[...] = numbers.T[first : first + 16, :].astype(I32)
    copies = start_slots(index_ref, slots, sem)
    number_ref[...] = decode(numbers, first, scratch).astype(I32)
    conducts = table + pltpu.roll(table, 112, 1) + pltpu.roll(table, 96, 1)
    conduct_ref[...] = decode(conducts, 64, scratch)
    part = iota((128, 1024), 0)
    lane = iota((128, 1024), 1)
    slot = (lane >> 7) + 8 * ((lane >> 6) & 1)
    spread = flag((part >= 64) & (part < 112) & ((part & 15) == slot))
    scale = jnp.dot(table.astype(BF16), spread, preferred_element_type=F32)
    for p in range(8):
        scale_ref[pl.ds(p, DEVS, stride=8), :] = scale[:, 128 * p : 128 * p + 128]
    doubled(volt_ref[...], rows_ref)
    if incoming:
        for d in range(DEVS):
            out_ref[16 * d : 16 * d + 8, :] = sent_ref[8 * d : 8 * d + 8, :]
    for copy in copies:
        copy.wait()
    if incoming:
        gather_rows(rows_ref, slots, scale_ref, out_ref, 8, 16)
    else:
        gather_rows(rows_ref, slots, scale_ref, out_ref, 0, 8)


def expander(rows, j):
    return (iota((rows, 128), 0) & 15) == 2 * j + (iota((rows, 128), 1) >> 6)


def grid_row(point):
    return ((point >> 7) & 7) * TILE + (point >> 10)


def prepare_kernel(
    into_ref,
    into_conduct_ref,
    own_ref,
    own_conduct_ref,
    id_ref,
    ecs_ref,
    point_ref,
    degree_ref,
    id_out,
    phi_out,
    slot_out,
    place_ref,
    found_ref,
):
    cell = iota((CELLS, 128), 0)
    kind = iota((16, 128), 0)
    place_ref[...] = jnp.zeros_like(place_ref)
    place_ref[0:PER, :] = grid_row(point_ref[...]).astype(F32)
    place_ref[16 : 16 + PER, :] = (point_ref[...] & 127).astype(F32)
    places = place_ref[...].astype(BF16)
    total = jnp.zeros((48, CELLS), F32)
    for side, (index_ref, conduct_ref) in enumerate(((into_ref, into_conduct_ref), (own_ref, own_conduct_ref))):
        for s in range(16):
            number = index_ref[s : s + 1, :]
            hit = flag((number & 255) == cell)
            here = (number >> 8) == kind
            first, rest = split2(conduct_ref[s : s + 1, :])
            second, third = split2(rest)
            values = jnp.concatenate([jnp.where(here, x, 0.0) for x in (first, second, third)], axis=0)
            total = total + lax.dot_general(values.astype(BF16), hit, NT, preferred_element_type=F32)
            found = jnp.dot(places, hit, preferred_element_type=F32)
            for part in range(2):
                picked = jnp.where(here, found[16 * part : 16 * part + 16, :], 0.0)
                at = 32 * part + 16 * side + s
                found_ref[at : at + 1, :] = jnp.sum(picked, axis=0, keepdims=True)
    upper = (iota((16, 128), 1) & 8) != 0
    for part in range(2):
        into = found_ref[32 * part : 32 * part + 16, :]
        own = found_ref[32 * part + 16 : 32 * part + 32, :]
        slot_out[32 * part : 32 * part + 16, :] = jnp.where(upper, pltpu.roll(own, 8, 1), into).astype(I32)
        slot_out[32 * part + 16 : 32 * part + 32, :] = jnp.where(upper, own, pltpu.roll(into, 120, 1)).astype(I32)
    total = total[0:16, :] + total[16:32, :] + total[32:48, :]
    first, rest = split2(total)
    second, third = split2(rest)
    pieces = jnp.concatenate([first, second, third], axis=0).astype(BF16)
    for j in range(PER // 2):
        degree_ref[:, 128 * j : 128 * j + 128] = lax.dot_general(
            pieces, flag(expander(48, j)), TN, preferred_element_type=F32
        )
    number = iota((16, 128), 0).astype(F32).astype(BF16)
    for half in range(2):
        hit = flag(id_ref[half : half + 1, :] == kind)
        id_out[128 * half : 128 * half + 128, :] = lax.dot_general(hit, number, TN, preferred_element_type=F32)
    for t in range(TILES):
        for y in range(4):
            rows = ecs_ref[pl.ds(4 * t + y, TILE, stride=TILE), :]
            phi_out[TILE * t : TILE * t + TILE, 32 * y : 32 * y + 32] = rows


def deposited(total, row, column, mean):
    hit = flag(row == iota((CELLS, CELLS), 0))
    here = column == iota((128, CELLS), 0)
    spread = jnp.concatenate([jnp.where(here, x, 0.0) for x in split2(mean)], axis=0)
    return total + lax.dot_general(hit, spread.astype(BF16), NT, preferred_element_type=F32)


def base_kernel(volt_ref, recov_ref, id_ref, degree_ref, point_ref, template_ref, out_ref, deposit_ref, volt_bf, held, sem):
    count = held.shape[0]
    copies = [pltpu.make_async_copy(template_ref.at[i], held.at[i], sem.at[i]) for i in range(count)]
    for copy in copies:
        copy.start()
    volt = volt_ref[...]
    volt_bf[...] = volt.astype(BF16)
    out_ref[...] = degree_ref[...] * volt - (volt - volt * volt * volt * (1.0 / 3.0) - recov_ref[...])

    def body(i, carry):
        parts = []
        for u in range(2):
            index = 2 * i + u
            pltpu.make_async_copy(template_ref.at[index], held.at[index], sem.at[index]).wait()
            mine = id_ref[...] == index.astype(F32)
            parts += [
                jnp.where(mine, volt_bf[:, 128 * j : 128 * j + 128], jnp.zeros((), BF16))
                for j in range(PER // 2)
            ]
        both = held[pl.ds(2 * i, 2)].reshape(2 * NODES, NODES)
        out_ref[...] += jnp.dot(jnp.concatenate(parts, axis=1), both, preferred_element_type=F32)
        return carry

    lax.fori_loop(0, count // 2, body, 0)
    means = jnp.zeros((16, CELLS), F32)
    for j in range(PER // 2):
        weights = jnp.where(expander(16, j), 1.0 / BLOCK, 0.0).astype(BF16)
        for part in split2(out_ref[:, 128 * j : 128 * j + 128]):
            means = means + lax.dot_general(weights, part.astype(BF16), NT, preferred_element_type=F32)
    total = jnp.zeros((CELLS, 256), F32)
    for k in range(PER):
        point = point_ref[k : k + 1, :]
        total = deposited(total, grid_row(point), point & 127, means[k : k + 1, :])
    deposit_ref[...] = total[:, 0:128] + total[:, 128:256]


CHUNKS = 4


def deposit_kernel(
    got_any, base_ref, slot_ref, phi_ref, deposit_ref, x_low_ref, x_high_ref, y_low_ref, y_high_ref, got_ref, sem
):
    rows = got_ref.shape[0] // CHUNKS
    copies = [
        pltpu.make_async_copy(got_any.at[pl.ds(rows * i, rows), :], got_ref.at[pl.ds(rows * i, rows), :], sem.at[i])
        for i in range(CHUNKS)
    ]
    for copy in copies:
        copy.start()
    lane = iota((16, 128), 1)
    weights = jnp.where(iota((16, 128), 0) == (lane >> 6), 1.0 / BLOCK, 0.0).astype(BF16)
    total = jnp.zeros((CELLS, 256), F32)
    for r in range(16):
        if r % (16 // CHUNKS) == 0:
            copies[r // (16 // CHUNKS)].wait()
        mean = jnp.zeros((16, 128), F32)
        for part in split2(got_ref[128 * r : 128 * r + 128, :]):
            mean = mean + lax.dot_general(weights, part.astype(BF16), NT, preferred_element_type=F32)

        def both(at):
            return jnp.concatenate([slot_ref[at + r : at + r + 1, :], slot_ref[at + 16 + r : at + 17 + r, :]], axis=1)

        total = deposited(total, both(0), both(32), jnp.concatenate([mean[0:1, :], mean[1:2, :]], axis=1))
    deposit_ref[...] = base_ref[...] - (total[:, 0:128] + total[:, 128:256])
    for array, at, across in ((phi_ref, 0, 0), (deposit_ref, HALO, TILE)):
        for t in range(TILES):
            start = TILE * t
            x_low_ref[8 * t + at : 8 * t + at + HALO, :] = array[start : start + HALO, :]
            x_high_ref[8 * t + at : 8 * t + at + HALO, :] = array[start + TILE - HALO : start + TILE, :]
        y_low_ref[across : across + TILE, :] = array[0:TILE, :]
        y_high_ref[across : across + TILE, :] = array[TILE * (TILES - 1) :, :]


def collect_kernel(offset, index_ref, got_ref, base_ref, out_ref, *scratch):
    lower, upper, slots, sem = scratch[0:2], scratch[2:4], scratch[4:20], scratch[20]
    copies = start_slots(index_ref, slots, sem)
    for ref in (*lower, *upper):
        ref[...] = jnp.zeros_like(ref)
    for copy in copies:
        copy.wait()

    def body(i, carry):
        for u in range(2):
            d = 2 * i + u
            base = pl.multiple_of(d * 16, 16)
            for p in range(8):
                row = got_ref[pl.ds(base + (offset + p), 1), :]
                lower[p % 2][pl.ds(slots[p][0, d], 1), :] += row
                upper[p % 2][pl.ds(slots[p + 8][0, d], 1), :] += row
        return carry

    lax.fori_loop(0, DEVS // 2, body, 0)
    low = low_half(CELLS)
    for j in range(PER // 2):
        sums = []
        for k in (2 * j, 2 * j + 1):
            cut = slice(CELLS * k, CELLS * k + CELLS)
            both = jnp.where(low, lower[0][cut, :] + lower[1][cut, :], upper[0][cut, :] + upper[1][cut, :])
            sums.append(both + pltpu.roll(both, 64, 1))
        cut = slice(128 * j, 128 * j + 128)
        out_ref[:, cut] = base_ref[:, cut] - jnp.where(low, sums[0], sums[1])


def frame_kernel(before_ref, after_ref, y_low_ref, y_high_ref, low_ref, high_ref):
    for middle_ref, out_ref, at in ((y_low_ref, low_ref, 0), (y_high_ref, high_ref, 8 * (TILES - 1))):
        out_ref[0:8, :] = before_ref[at : at + 8, :]
        out_ref[8:72, :] = middle_ref[...]
        out_ref[72:80, :] = after_ref[at : at + 8, :]


ROWS = TILE + 2 * HALO
LEAD = 8


def sweep_kernel(last, *refs):
    place_ref, phi_ref, deposit_ref, x_before_ref, x_after_ref, y_before_ref, y_after_ref = refs[:7]
    current_ref, volt_ref, point_ref = refs[7:10]
    if last:
        volt_out, phi_out, wide_phi, wide_deposit, found_ref = refs[10:]
    else:
        recov_ref, into_ref, into_scale_ref, own_ref, own_scale_ref = refs[10:15]
        volt_out, phi_out, recov_out, send_out, wide_phi, wide_deposit, found_ref, rows_ref = refs[15:23]
        own_slots, into_slots, own_sem, into_sem = refs[23:39], refs[39:55], refs[55], refs[56]
        copies = start_slots(own_ref, own_slots, own_sem) + start_slots(into_ref, into_slots, into_sem)
    end = LEAD + ROWS
    high = LEAD + HALO + TILE
    for wide, array, at, across in ((wide_phi, phi_ref, 0, 0), (wide_deposit, deposit_ref, HALO, TILE)):
        for t in range(TILES):
            wide[t + 1, LEAD : LEAD + HALO, :] = x_before_ref[8 * t + at : 8 * t + at + HALO, :]
            wide[t + 1, LEAD + HALO : high, :] = array[TILE * t : TILE * t + TILE, :]
            wide[t + 1, high:end, :] = x_after_ref[8 * t + at : 8 * t + at + HALO, :]
        for t, came in ((0, y_before_ref), (TILES + 1, y_after_ref)):
            wide[t, LEAD : LEAD + HALO, :] = came[at : at + HALO, :]
            wide[t, LEAD + HALO : high, :] = came[8 + across : 8 + across + TILE, :]
            wide[t, high:end, :] = came[72 + at : 72 + at + HALO, :]
    shape = (ROWS, 128)
    row = iota(shape, 0)
    lane = iota(shape, 1)
    depth = lane & (TILE - 1)
    first_row = jnp.where(place_ref[0] == 0, HALO, 0)
    last_row = jnp.where(place_ref[0] == place_ref[2] - 1, HALO + TILE, ROWS)
    inside = (row >= first_row) & (row < last_row)
    first_tile = jnp.where(place_ref[1] == 0, 1, 0)
    last_tile = jnp.where(place_ref[1] == place_ref[3] - 1, TILES + 1, TILES + 2)
    scale = jnp.where(inside, 1.0 / 6.5, 0.0)
    side = [jnp.where((t >= first_tile) & (t < last_tile), 1.0, 0.0) for t in (0, TILES + 1)]
    edge = {0: scale * side[0], TILES + 1: scale * side[1]}
    for t in range(TILES + 2):
        wide_phi[t, 0:LEAD, :] = jnp.zeros((LEAD, 128), F32)
        wide_phi[t, end : end + 8, :] = jnp.zeros((8, 128), F32)
        keep = jnp.where(inside, side[0 if t == 0 else 1], 0.0) if t in edge else jnp.where(inside, 1.0, 0.0)
        wide_phi[t, LEAD:end, :] = jnp.where(keep > 0.0, wide_phi[t, LEAD:end, :], 0.0)
    nothing = jnp.zeros(shape, F32)
    for _ in range(SWEEPS):
        middle = [wide_phi[t, LEAD:end, :] for t in range(TILES + 2)]
        fresh = []
        ups = [pltpu.roll(x, 32, 1) for x in middle]
        downs = [pltpu.roll(x, 96, 1) for x in middle]
        for t in range(TILES + 2):
            total = wide_deposit[t, LEAD:end, :]
            total = total + wide_phi[t, LEAD - 1 : end - 1, :] + wide_phi[t, LEAD + 1 : end + 1, :]
            total = total + jnp.where(lane < 32, ups[t - 1] if t else nothing, ups[t])
            total = total + jnp.where(lane >= 96, downs[t + 1] if t <= TILES else nothing, downs[t])
            total = total + jnp.where(depth == 0, 0.0, pltpu.roll(middle[t], 1, 1))
            total = total + jnp.where(depth == TILE - 1, 0.0, pltpu.roll(middle[t], 127, 1))
            fresh.append(jnp.where(edge.get(t, scale) > 0.0, total * (1.0 / 6.5), 0.0))
        for t in range(TILES + 2):
            wide_phi[t, LEAD:end, :] = fresh[t]
    tiles = [wide_phi[t + 1, LEAD + HALO : high, :] for t in range(TILES)]
    if last:
        for t in range(TILES):
            for y in range(4):
                turned = tiles[t] if y == 0 else pltpu.roll(tiles[t], 128 - 32 * y, 1)
                phi_out[pl.ds(4 * t + y, TILE, stride=TILE), :] = turned[:, 0:TILE]
    else:
        for t in range(TILES):
            phi_out[TILE * t : TILE * t + TILE, :] = tiles[t]
    turned = jnp.concatenate(tiles, axis=0).T
    pieces = jnp.concatenate(split2(turned), axis=0).astype(BF16)
    row_of = iota((CELLS, CELLS), 0)
    column_of = iota((128, CELLS), 0)
    found_ref[...] = jnp.zeros_like(found_ref)
    for k in range(PER):
        point = point_ref[k : k + 1, :]
        hit = flag(grid_row(point) == row_of)
        found = jnp.dot(pieces, hit, preferred_element_type=F32)
        found = found[0:128, :] + found[128:256, :]
        here = (point & 127) == column_of
        found_ref[k : k + 1, :] = jnp.sum(jnp.where(here, found, 0.0), axis=0, keepdims=True)
    found = jnp.concatenate(split2(found_ref[...]), axis=0).astype(BF16)
    low = low_half(CELLS)
    for j in range(PER // 2):
        cut = slice(128 * j, 128 * j + 128)
        at_node = lax.dot_general(found, flag(expander(32, j)), TN, preferred_element_type=F32)
        volt = volt_ref[:, cut]
        fresh = volt - 0.05 * (current_ref[:, cut] + at_node)
        volt_out[:, cut] = fresh
        if not last:
            recov = recov_ref[:, cut]
            recov_out[:, cut] = recov + 0.05 * 0.08 * (volt + 0.7 - 0.8 * recov)
            turned = pltpu.roll(fresh, 64, 1)
            rows_ref[512 * j : 512 * j + 256, :] = jnp.where(low, fresh, turned)
            rows_ref[512 * j + 256 : 512 * j + 512, :] = jnp.where(low, turned, fresh)
    if not last:
        for copy in copies:
            copy.wait()
        gather_rows(rows_ref, own_slots, own_scale_ref, send_out, 0, 16)
        gather_rows(rows_ref, into_slots, into_scale_ref, send_out, 8, 16)


def shaped(*shape, dtype=F32):
    return jax.ShapeDtypeStruct(shape, dtype)


def exchange(x):
    return lax.all_to_all(x, AXES, split_axis=0, concat_axis=0, tiled=True)


def shift(x, axis, by):
    size = lax.axis_size(axis)
    return lax.ppermute(x, axis, [(i, (i + by) % size) for i in range(size)])


def on_device(
    potential,
    gating,
    ecs_start,
    templates,
    template_id,
    patch_src,
    patch_dev,
    patch_dst,
    patch_conduct,
    memb_point,
):
    flat = (8, 128)
    table = pl.pallas_call(
        setup_kernel,
        out_shape=shaped(128, 128),
        in_specs=[VMEM] * 4,
        out_specs=VMEM,
        compiler_params=PARAMS,
        name="setup",
    )(
        patch_dev.reshape(flat),
        patch_src.reshape(flat),
        patch_dst.reshape(flat),
        patch_conduct.reshape(flat),
    )
    got_table = exchange(table)
    rows_scratch = pltpu.VMEM((PER * CELLS, 128), F32)
    slot_scratch = [pltpu.SMEM((1, 128), I32)] * CAP
    slot_sem = pltpu.SemaphoreType.DMA((CAP,))
    small = shaped(16, 128, dtype=I32)
    tables_out = (small, small, shaped(16, 128), shaped(DEVS * 8, 128))
    gather_scratch = [rows_scratch, pltpu.VMEM((128, 128), F32)] + slot_scratch + [slot_sem]
    sent, own, own_number, own_conduct, own_scale = pl.pallas_call(
        functools.partial(gather_kernel, False),
        out_shape=(shaped(DEVS * 8, 128),) + tables_out,
        in_specs=[VMEM] * 2,
        out_specs=(VMEM,) * 5,
        scratch_shapes=gather_scratch,
        compiler_params=PARAMS,
        name="gather_source",
    )(table, potential)
    outgoing, into, into_number, into_conduct, into_scale = pl.pallas_call(
        functools.partial(gather_kernel, True),
        out_shape=(shaped(DEVS * 16, 128),) + tables_out,
        in_specs=[VMEM] * 3,
        out_specs=(VMEM,) * 5,
        scratch_shapes=gather_scratch,
        compiler_params=PARAMS,
        name="gather_target",
    )(got_table, potential, sent)
    points = memb_point.reshape(CELLS, PER).T
    degree, id_wide, phi, slot_points = pl.pallas_call(
        prepare_kernel,
        out_shape=(shaped(CELLS, NODES), shaped(CELLS, 128), shaped(TILE * TILES, 128), shaped(64, 128, dtype=I32)),
        in_specs=[VMEM] * 7,
        out_specs=(VMEM,) * 4,
        scratch_shapes=[pltpu.VMEM((32, CELLS), F32), pltpu.VMEM((64, 128), F32)],
        compiler_params=PARAMS,
        name="prepare",
    )(
        into_number,
        into_conduct,
        own_number,
        own_conduct,
        template_id.reshape(2, 128),
        ecs_start.reshape(TILE * TILE, TILE),
        points,
    )

    place = jnp.stack([lax.axis_index("tx"), lax.axis_index("ty"), lax.axis_size("tx"), lax.axis_size("ty")])
    place = place.astype(I32)
    volt = potential
    recov = gating
    anywhere = pl.BlockSpec(memory_space=pl.ANY)
    for step in range(STEPS):
        last = step == STEPS - 1
        got = exchange(outgoing.reshape(DEVS, 16, 128)).reshape(DEVS * 16, 128)
        base, deposit_base = pl.pallas_call(
            base_kernel,
            out_shape=(shaped(CELLS, NODES), shaped(TILE * TILES, 128)),
            in_specs=[VMEM] * 5 + [anywhere],
            out_specs=(VMEM,) * 2,
            scratch_shapes=[
                pltpu.VMEM((CELLS, NODES), BF16),
                pltpu.VMEM(templates.shape, BF16),
                pltpu.SemaphoreType.DMA((templates.shape[0],)),
            ],
            cost_estimate=pl.CostEstimate(flops=3_000_000_000, bytes_accessed=14_000_000, transcendentals=0),
            compiler_params=PARAMS,
            name="base",
        )(volt, recov, id_wide, degree, points, templates)
        deposit, x_low, x_high, y_low, y_high = pl.pallas_call(
            deposit_kernel,
            out_shape=(shaped(TILE * TILES, 128),) + (shaped(64, 128),) * 4,
            in_specs=[anywhere] + [VMEM] * 3,
            out_specs=(VMEM,) * 5,
            scratch_shapes=[pltpu.VMEM((DEVS * 16, 128), F32), pltpu.SemaphoreType.DMA((CHUNKS,))],
            compiler_params=PARAMS,
            name="deposit",
        )(got, deposit_base, slot_points, phi)

        def collect(offset, index, start):
            return pl.pallas_call(
                functools.partial(collect_kernel, offset),
                out_shape=shaped(CELLS, NODES),
                in_specs=[VMEM] * 3,
                out_specs=VMEM,
                scratch_shapes=[rows_scratch] * 4 + slot_scratch + [slot_sem],
                cost_estimate=pl.CostEstimate(flops=1_000_000_000, bytes_accessed=10_000_000, transcendentals=0),
                compiler_params=PARAMS,
                name="collect_own" if offset else "collect_into",
            )(index, got, start)

        x_before = shift(x_high, "tx", 1)
        x_after = shift(x_low, "tx", -1)
        current = collect(0, into, base)
        y_low, y_high = pl.pallas_call(
            frame_kernel,
            out_shape=(shaped(80, 128),) * 2,
            in_specs=[VMEM] * 4,
            out_specs=(VMEM,) * 2,
            compiler_params=PARAMS,
            name="frame",
        )(x_before, x_after, y_low, y_high)
        y_before = shift(y_high, "ty", 1)
        y_after = shift(y_low, "ty", -1)
        current = collect(8, own, current)
        operands = [place, phi, deposit, x_before, x_after, y_before, y_after, current, volt, points]
        specs = [SMEM] + [VMEM] * 9
        wide = [pltpu.VMEM((TILES + 2, LEAD + ROWS + 8, 128), F32)] * 2 + [pltpu.VMEM((16, CELLS), F32)]
        if last:
            volt, phi = pl.pallas_call(
                functools.partial(sweep_kernel, True),
                out_shape=(shaped(CELLS, NODES), shaped(TILE * TILE, TILE)),
                in_specs=specs,
                out_specs=(VMEM,) * 2,
                scratch_shapes=wide,
                compiler_params=PARAMS,
                name="sweep_last",
            )(*operands)
        else:
            volt, phi, recov, outgoing = pl.pallas_call(
                functools.partial(sweep_kernel, False),
                out_shape=(
                    shaped(CELLS, NODES),
                    shaped(TILE * TILES, 128),
                    shaped(CELLS, NODES),
                    shaped(DEVS * 16, 128),
                ),
                in_specs=specs + [VMEM] * 5,
                out_specs=(VMEM,) * 4,
                scratch_shapes=wide + [rows_scratch] + slot_scratch * 2 + [slot_sem] * 2,
                compiler_params=PARAMS,
                name="sweep",
            )(*operands, recov, into, into_scale, own, own_scale)
    return (volt, phi.reshape(TILE, TILE, TILE))


def solution(mesh):
    return jax.shard_map(
        on_device,
        mesh=mesh,
        in_specs=(
            P(("tx", "ty"), None),
            P(("tx", "ty"), None),
            P("tx", "ty", None),
            P(),
            P(("tx", "ty")),
            P(("tx", "ty")),
            P(("tx", "ty"), None),
            P(("tx", "ty")),
            P(("tx", "ty")),
            P(("tx", "ty")),
        ),
        out_specs=(P(("tx", "ty"), None), P("tx", "ty", None)),
        check_vma=False,
    )
```

```python
import functools

import jax
import jax.numpy as jnp
from jax import lax
from jax.experimental import pallas as pl
from jax.experimental.pallas import tpu as pltpu
from jax.sharding import PartitionSpec as P

BLOCK = 64
SWEEPS = 4
STEPS = 2
CELLS = 256
NODES = 768
PER = 12
DEVS = 128
CAP = 16
TILE = 32
HALO = 4
CHUNKS = 4
TILES = 8
F32 = jnp.float32
BF16 = jnp.bfloat16
I32 = jnp.int32
AXES = ("tx", "ty")
VMEM = pl.BlockSpec(memory_space=pltpu.VMEM)
SMEM = pl.BlockSpec(memory_space=pltpu.SMEM)
NT = (((1,), (1,)), ((), ()))
TN = (((0,), (0,)), ((), ()))
PARAMS = pltpu.CompilerParams(vmem_limit_bytes=67_043_328)


def iota(shape, dim):
    return lax.broadcasted_iota(I32, shape, dim)


def low_half(rows):
    return iota((rows, 128), 1) < 64


def flag(condition):
    return condition.astype(F32).astype(BF16)


def marks(row, count):
    places = iota((count, row.shape[1]), 0).astype(F32).astype(BF16)
    return jnp.where(row.astype(F32).astype(BF16) == places, jnp.ones((), BF16), jnp.zeros((), BF16))


def regroup(number):
    value = number.astype(F32)
    cell = jnp.floor((value + 0.5) * (1.0 / PER))
    return (value - PER * cell) * CELLS + cell


def split2(x):
    hi = x.astype(BF16).astype(F32)
    return hi, x - hi


def setup_kernel(dev_ref, src_ref, dst_ref, conduct_ref, table_ref):
    device = iota((128, 128), 0)
    before = flag(device < iota((128, 128), 1))
    slots = iota((16, 128), 0)
    count = jnp.zeros((128, 1), F32)
    table = jnp.zeros((128, 128), F32)
    for q in range(8):
        hit = (dev_ref[q : q + 1, :] == device).astype(F32)
        hit_bf = hit.astype(BF16)
        running = jnp.dot(hit_bf, before, preferred_element_type=F32) + count
        rank = jnp.sum(hit * running, axis=0, keepdims=True)
        count = count + jnp.sum(hit, axis=1, keepdims=True)
        here = rank.astype(I32) == slots
        parts = []
        for ref in (dst_ref, src_ref):
            number = regroup(ref[q : q + 1, :])
            hi = jnp.floor(number * (1.0 / 64.0))
            parts += [hi, number - 64.0 * hi]
        first, rest = split2(conduct_ref[q : q + 1, :])
        second, third = split2(rest)
        parts += [first, second, third, jnp.zeros((1, 128), F32)]
        values = jnp.concatenate([jnp.where(here, part, 0.0) for part in parts], axis=0)
        table = table + lax.dot_general(hit_bf, values.astype(BF16), NT, preferred_element_type=F32)
    table_ref[...] = table


def decode(table, first_lane, scratch):
    scratch[...] = table
    lane = iota((16, 128), 1)
    out = jnp.zeros((16, 128), F32)
    for dl in range(8):
        rows = scratch[pl.ds(dl, 16, stride=8), :]
        out = jnp.where((lane >> 4) == dl, pltpu.roll(rows, (16 * dl - first_lane) % 128, 1), out)
    return out


def doubled(volt, rows_ref):
    low = low_half(CELLS)
    for j in range(PER // 2):
        pair = volt[:, 128 * j : 128 * j + 128]
        turned = pltpu.roll(pair, 64, 1)
        rows_ref[512 * j : 512 * j + 256, :] = jnp.where(low, pair, turned)
        rows_ref[512 * j + 256 : 512 * j + 512, :] = jnp.where(low, turned, pair)


def start_slots(index_ref, slots, sem):
    copies = [
        pltpu.make_async_copy(index_ref.at[pl.ds(s, 1), :], slot, sem.at[s]) for s, slot in enumerate(slots)
    ]
    for copy in copies:
        copy.start()
    return copies


def start_copies(pairs, sem):
    copies = [pltpu.make_async_copy(source, target, sem.at[i]) for i, (source, target) in enumerate(pairs)]
    for copy in copies:
        copy.start()
    return copies


def gather_rows(rows_ref, sides, out_ref, target_of, sem):
    low = low_half(1)
    copies = []
    for chunk in range(CHUNKS):
        count = DEVS // CHUNKS

        def body(i, carry, chunk=chunk, count=count):
            d = count * chunk + i
            scale_base = pl.multiple_of(d * 8, 8)
            for slots, scale_ref, first in sides:
                for p in range(8):
                    a = slots[p][0, d]
                    b = slots[p + 8][0, d]
                    row = jnp.where(low, rows_ref[pl.ds(a, 1), :], rows_ref[pl.ds(b, 1), :])
                    out_ref[d, first + p : first + p + 1, :] = row * scale_ref[pl.ds(scale_base + p, 1), :]
            return carry

        lax.fori_loop(0, count, body, 0, unroll=2)
        mine = pl.ds(count * chunk, count)
        copy = pltpu.make_async_copy(out_ref.at[mine], target_of(mine), sem.at[chunk])
        copy.start()
        copies.append(copy)
    return copies


def gather_kernel(incoming, *refs):
    if incoming:
        table_ref, volt_any, _, out_any = refs[:4]
        refs = refs[4:]
    else:
        table_ref, volt_any, out_any = refs[:3]
        refs = refs[3:]
    index_ref, number_ref, conduct_ref, scale_any, rows_ref, scratch, volt_ref, out_ref, scale_ref = refs[:9]
    slots, sem, data_sem, out_sem = refs[9:25], refs[25], refs[26], refs[27]
    (volt_copy,) = start_copies([(volt_any, volt_ref)], data_sem)
    first = 0 if incoming else 32
    table = table_ref[...]
    numbers = 64.0 * table + pltpu.roll(table, 112, 1)
    index_ref[...] = numbers.T[first : first + 16, :].astype(I32)
    copies = start_slots(index_ref, slots, sem)
    number_ref[...] = decode(numbers, first, scratch).astype(I32)
    conducts = table + pltpu.roll(table, 112, 1) + pltpu.roll(table, 96, 1)
    conduct_ref[...] = decode(conducts, 64, scratch)
    part = iota((128, 1024), 0)
    lane = iota((128, 1024), 1)
    slot = (lane >> 7) + 8 * ((lane >> 6) & 1)
    spread = flag((part >= 64) & (part < 112) & ((part & 15) == slot))
    scale = jnp.dot(table.astype(BF16), spread, preferred_element_type=F32)
    for p in range(8):
        scale_ref[pl.ds(p, DEVS, stride=8), :] = scale[:, 128 * p : 128 * p + 128]
    scale_copy = pltpu.make_async_copy(scale_ref, scale_any, data_sem.at[1])
    scale_copy.start()
    volt_copy.wait()
    doubled(volt_ref[...], rows_ref)
    for copy in copies:
        copy.wait()
    at = pl.ds(8 if incoming else 0, 8)
    done = gather_rows(rows_ref, ((slots, scale_ref, 0),), out_ref, lambda mine: out_any.at[mine, at], out_sem)
    for copy in (scale_copy, *done):
        copy.wait()


def expander(rows, j):
    return (iota((rows, 128), 0) & 15) == 2 * j + (iota((rows, 128), 1) >> 6)


def grid_row(point):
    return ((point >> 7) & 7) * TILE + (point >> 10)


def prepare_kernel(
    into_ref,
    into_conduct_ref,
    own_ref,
    own_conduct_ref,
    id_ref,
    ecs_ref,
    point_ref,
    degree_ref,
    id_out,
    phi_out,
    slot_out,
    place_ref,
    found_ref,
):
    kind = iota((16, 128), 0)
    place_ref[...] = jnp.zeros_like(place_ref)
    place_ref[0:PER, :] = grid_row(point_ref[...]).astype(F32)
    place_ref[16 : 16 + PER, :] = (point_ref[...] & 127).astype(F32)
    places = place_ref[...].astype(BF16)
    total = jnp.zeros((48, CELLS), F32)
    for side, (index_ref, conduct_ref) in enumerate(((into_ref, into_conduct_ref), (own_ref, own_conduct_ref))):
        for s in range(16):
            number = index_ref[s : s + 1, :]
            hit = marks(number & 255, CELLS)
            here = (number >> 8) == kind
            first, rest = split2(conduct_ref[s : s + 1, :])
            second, third = split2(rest)
            values = jnp.concatenate([jnp.where(here, x, 0.0) for x in (first, second, third)], axis=0)
            total = total + lax.dot_general(values.astype(BF16), hit, NT, preferred_element_type=F32)
            found = jnp.dot(places, hit, preferred_element_type=F32)
            for part in range(2):
                picked = jnp.where(here, found[16 * part : 16 * part + 16, :], 0.0)
                at = 32 * part + 16 * side + s
                found_ref[at : at + 1, :] = jnp.sum(picked, axis=0, keepdims=True)
    upper = (iota((16, 128), 1) & 8) != 0
    for part in range(2):
        into = found_ref[32 * part : 32 * part + 16, :]
        own = found_ref[32 * part + 16 : 32 * part + 32, :]
        slot_out[32 * part : 32 * part + 16, :] = jnp.where(upper, pltpu.roll(own, 8, 1), into).astype(I32)
        slot_out[32 * part + 16 : 32 * part + 32, :] = jnp.where(upper, own, pltpu.roll(into, 120, 1)).astype(I32)
    total = total[0:16, :] + total[16:32, :] + total[32:48, :]
    first, rest = split2(total)
    second, third = split2(rest)
    pieces = jnp.concatenate([first, second, third], axis=0).astype(BF16)
    for j in range(PER // 2):
        degree_ref[:, 128 * j : 128 * j + 128] = lax.dot_general(
            pieces, flag(expander(48, j)), TN, preferred_element_type=F32
        )
    number = iota((16, 128), 0).astype(F32).astype(BF16)
    for half in range(2):
        hit = flag(id_ref[half : half + 1, :] == kind)
        id_out[128 * half : 128 * half + 128, :] = lax.dot_general(hit, number, TN, preferred_element_type=F32)
    for t in range(TILES):
        for y in range(4):
            rows = ecs_ref[pl.ds(4 * t + y, TILE, stride=TILE), :]
            phi_out[TILE * t : TILE * t + TILE, 32 * y : 32 * y + 32] = rows


def deposited(total, row, column, mean):
    hit = marks(row, CELLS)
    here = marks(column, 128)
    spread = jnp.concatenate([here * x.astype(BF16) for x in split2(mean)], axis=0)
    return total + lax.dot_general(hit, spread, NT, preferred_element_type=F32)


def base_kernel(volt_ref, recov_ref, id_ref, degree_ref, point_ref, template_ref, out_ref, deposit_ref, volt_bf, held, sem):
    count = held.shape[0]
    copies = [pltpu.make_async_copy(template_ref.at[i], held.at[i], sem.at[i]) for i in range(count)]
    for copy in copies:
        copy.start()
    volt = volt_ref[...]
    volt_bf[...] = volt.astype(BF16)
    out_ref[...] = degree_ref[...] * volt - (volt - volt * volt * volt * (1.0 / 3.0) - recov_ref[...])

    def body(i, carry):
        parts = []
        for u in range(2):
            index = 2 * i + u
            pltpu.make_async_copy(template_ref.at[index], held.at[index], sem.at[index]).wait()
            mine = id_ref[...] == index.astype(F32)
            parts += [
                jnp.where(mine, volt_bf[:, 128 * j : 128 * j + 128], jnp.zeros((), BF16))
                for j in range(PER // 2)
            ]
        both = held[pl.ds(2 * i, 2)].reshape(2 * NODES, NODES)
        out_ref[...] += jnp.dot(jnp.concatenate(parts, axis=1), both, preferred_element_type=F32)
        return carry

    lax.fori_loop(0, count // 2, body, 0)
    means = jnp.zeros((16, CELLS), F32)
    for j in range(PER // 2):
        weights = jnp.where(expander(16, j), 1.0 / BLOCK, 0.0).astype(BF16)
        parts = jnp.concatenate(split2(out_ref[:, 128 * j : 128 * j + 128]), axis=1).astype(BF16)
        weights = jnp.concatenate([weights, weights], axis=1)
        means = means + lax.dot_general(weights, parts, NT, preferred_element_type=F32)
    total = jnp.zeros((CELLS, 256), F32)
    for k in range(PER):
        point = point_ref[k : k + 1, :]
        total = deposited(total, grid_row(point), point & 127, means[k : k + 1, :])
    deposit_ref[...] = total[:, 0:128] + total[:, 128:256]


def deposit_kernel(
    got_any, base_ref, slot_ref, phi_ref, deposit_ref, x_low_ref, x_high_ref, y_low_ref, y_high_ref, got_ref, sem
):
    rows = got_ref.shape[0] // CHUNKS
    copies = [
        pltpu.make_async_copy(got_any.at[pl.ds(rows * i, rows), :], got_ref.at[pl.ds(rows * i, rows), :], sem.at[i])
        for i in range(CHUNKS)
    ]
    for copy in copies:
        copy.start()
    half = (iota((16, 256), 1) >> 6) & 1
    weights = jnp.where(iota((16, 256), 0) == half, 1.0 / BLOCK, 0.0).astype(BF16)
    total = jnp.zeros((CELLS, 256), F32)
    for r in range(16):
        if r % (16 // CHUNKS) == 0:
            copies[r // (16 // CHUNKS)].wait()
        if r % 2 == 0:
            parts = jnp.concatenate(split2(got_ref[128 * r : 128 * r + 256, :]), axis=1).astype(BF16)
            pair = lax.dot_general(weights, parts, NT, preferred_element_type=F32)
        mean = pair[:, 128 * (r % 2) : 128 * (r % 2) + 128]

        def both(at):
            return jnp.concatenate([slot_ref[at + r : at + r + 1, :], slot_ref[at + 16 + r : at + 17 + r, :]], axis=1)

        total = deposited(total, both(0), both(32), jnp.concatenate([mean[0:1, :], mean[1:2, :]], axis=1))
    deposit_ref[...] = base_ref[...] - (total[:, 0:128] + total[:, 128:256])
    for array, at, across in ((phi_ref, 0, 0), (deposit_ref, HALO, TILE)):
        for t in range(TILES):
            start = TILE * t
            x_low_ref[8 * t + at : 8 * t + at + HALO, :] = array[start : start + HALO, :]
            x_high_ref[8 * t + at : 8 * t + at + HALO, :] = array[start + TILE - HALO : start + TILE, :]
        y_low_ref[across : across + TILE, :] = array[0:TILE, :]
        y_high_ref[across : across + TILE, :] = array[TILE * (TILES - 1) :, :]


def collect_kernel(into_ref, own_ref, got_any, base_any, out_any, *scratch):
    sums, into_slots, own_slots = scratch[0:8], scratch[8:24], scratch[24:40]
    got_ref, base_ref, into_sem, own_sem, data_sem, out_sem = scratch[40:]
    copies = start_slots(into_ref, into_slots, into_sem) + start_slots(own_ref, own_slots, own_sem)
    count = DEVS // CHUNKS
    pieces = [pl.ds(16 * count * i, 16 * count) for i in range(CHUNKS)]
    got_copies = start_copies(
        [(got_any.at[piece], got_ref.at[piece]) for piece in pieces] + [(base_any, base_ref)], data_sem
    )
    for ref in sums:
        ref[...] = jnp.zeros_like(ref)
    for copy in copies:
        copy.wait()
    for chunk in range(CHUNKS):
        got_copies[chunk].wait()

        def body(i, carry, chunk=chunk):
            d = count * chunk + i
            base = pl.multiple_of(d * 16, 16)
            for p in range(8):
                for side, slots in ((0, into_slots), (1, own_slots)):
                    row = got_ref[pl.ds(base + (8 * side + p), 1), :]
                    for half in (0, 1):
                        ref = sums[4 * (p % 2) + 2 * side + half]
                        ref[pl.ds(slots[p + 8 * half][0, d], 1), :] += row
            return carry

        lax.fori_loop(0, count, body, 0, unroll=2)
    got_copies[CHUNKS].wait()
    low = low_half(CELLS)
    out_copies = []
    for j in range(PER // 2):
        both = []
        for k in (2 * j, 2 * j + 1):
            cut = slice(CELLS * k, CELLS * k + CELLS)
            halves = [sum(ref[cut, :] for ref in sums[half::2]) for half in (0, 1)]
            rows = jnp.where(low, *halves)
            both.append(rows + pltpu.roll(rows, 64, 1))
        cut = slice(128 * j, 128 * j + 128)
        base_ref[:, cut] = base_ref[:, cut] - jnp.where(low, both[0], both[1])
        cut = pl.ds(128 * j, 128)
        copy = pltpu.make_async_copy(base_ref.at[:, cut], out_any.at[:, cut], out_sem.at[j])
        copy.start()
        out_copies.append(copy)
    for copy in out_copies:
        copy.wait()


def frame_kernel(before_ref, after_ref, y_low_ref, y_high_ref, low_ref, high_ref):
    for middle_ref, out_ref, at in ((y_low_ref, low_ref, 0), (y_high_ref, high_ref, 8 * (TILES - 1))):
        out_ref[0:8, :] = before_ref[at : at + 8, :]
        out_ref[8:72, :] = middle_ref[...]
        out_ref[72:80, :] = after_ref[at : at + 8, :]


ROWS = TILE + 2 * HALO
LEAD = 8


def sweep_kernel(last, *refs):
    place_ref, phi_ref, deposit_ref, x_before_ref, x_after_ref, y_before_ref, y_after_ref = refs[:7]
    current_any, volt_any, point_ref = refs[7:10]
    if last:
        volt_out, phi_out, wide_phi, wide_deposit, found_ref, current_ref, volt_ref, phi_held = refs[10:18]
        data_sem, out_sem = refs[18:]
        fetched = start_copies([(current_any, current_ref), (volt_any, volt_ref)], data_sem)
    else:
        recov_any, into_ref, into_scale_any, own_ref, own_scale_any = refs[10:15]
        volt_out, phi_out, recov_out, send_any = refs[15:19]
        wide_phi, wide_deposit, found_ref, current_ref, volt_ref, recov_ref = refs[19:25]
        own_scale_ref, into_scale_ref, send_ref, rows_ref = refs[25:29]
        own_slots, into_slots = refs[29:45], refs[45:61]
        own_sem, into_sem, data_sem, out_sem = refs[61:]
        copies = start_slots(own_ref, own_slots, own_sem) + start_slots(into_ref, into_slots, into_sem)
        fetched = start_copies(
            [
                (current_any, current_ref),
                (volt_any, volt_ref),
                (recov_any, recov_ref),
                (own_scale_any, own_scale_ref),
                (into_scale_any, into_scale_ref),
            ],
            data_sem,
        )
    end = LEAD + ROWS
    high = LEAD + HALO + TILE
    for wide, array, at, across in ((wide_phi, phi_ref, 0, 0), (wide_deposit, deposit_ref, HALO, TILE)):
        for t in range(TILES):
            wide[t + 1, LEAD : LEAD + HALO, :] = x_before_ref[8 * t + at : 8 * t + at + HALO, :]
            wide[t + 1, LEAD + HALO : high, :] = array[TILE * t : TILE * t + TILE, :]
            wide[t + 1, high:end, :] = x_after_ref[8 * t + at : 8 * t + at + HALO, :]
        for t, came in ((0, y_before_ref), (TILES + 1, y_after_ref)):
            wide[t, LEAD : LEAD + HALO, :] = came[at : at + HALO, :]
            wide[t, LEAD + HALO : high, :] = came[8 + across : 8 + across + TILE, :]
            wide[t, high:end, :] = came[72 + at : 72 + at + HALO, :]
    shape = (ROWS, 128)
    row = iota(shape, 0)
    lane = iota(shape, 1)
    depth = lane & (TILE - 1)
    first_row = jnp.where(place_ref[0] == 0, HALO, 0)
    last_row = jnp.where(place_ref[0] == place_ref[2] - 1, HALO + TILE, ROWS)
    inside = (row >= first_row) & (row < last_row)
    first_tile = jnp.where(place_ref[1] == 0, 1, 0)
    last_tile = jnp.where(place_ref[1] == place_ref[3] - 1, TILES + 1, TILES + 2)
    scale = jnp.where(inside, 1.0 / 6.5, 0.0)
    side = [jnp.where((t >= first_tile) & (t < last_tile), 1.0, 0.0) for t in (0, TILES + 1)]
    edge = {0: scale * side[0], TILES + 1: scale * side[1]}
    for t in range(TILES + 2):
        wide_phi[t, 0:LEAD, :] = jnp.zeros((LEAD, 128), F32)
        wide_phi[t, end : end + 8, :] = jnp.zeros((8, 128), F32)
        keep = jnp.where(inside, side[0 if t == 0 else 1], 0.0) if t in edge else jnp.where(inside, 1.0, 0.0)
        wide_phi[t, LEAD:end, :] = jnp.where(keep > 0.0, wide_phi[t, LEAD:end, :], 0.0)
    nothing = jnp.zeros(shape, F32)
    for _ in range(SWEEPS):
        middle = [wide_phi[t, LEAD:end, :] for t in range(TILES + 2)]
        fresh = []
        ups = [pltpu.roll(x, 32, 1) for x in middle]
        downs = [pltpu.roll(x, 96, 1) for x in middle]
        for t in range(TILES + 2):
            total = wide_deposit[t, LEAD:end, :]
            total = total + wide_phi[t, LEAD - 1 : end - 1, :] + wide_phi[t, LEAD + 1 : end + 1, :]
            total = total + jnp.where(lane < 32, ups[t - 1] if t else nothing, ups[t])
            total = total + jnp.where(lane >= 96, downs[t + 1] if t <= TILES else nothing, downs[t])
            total = total + jnp.where(depth == 0, 0.0, pltpu.roll(middle[t], 1, 1))
            total = total + jnp.where(depth == TILE - 1, 0.0, pltpu.roll(middle[t], 127, 1))
            fresh.append(jnp.where(edge.get(t, scale) > 0.0, total * (1.0 / 6.5), 0.0))
        for t in range(TILES + 2):
            wide_phi[t, LEAD:end, :] = fresh[t]
    tiles = [wide_phi[t + 1, LEAD + HALO : high, :] for t in range(TILES)]
    if last:
        for t in range(TILES):
            for y in range(4):
                turned = tiles[t] if y == 0 else pltpu.roll(tiles[t], 128 - 32 * y, 1)
                phi_held[pl.ds(4 * t + y, TILE, stride=TILE), :] = turned[:, 0:TILE]
        phi_copy = pltpu.make_async_copy(phi_held, phi_out, out_sem.at[PER // 2])
        phi_copy.start()
    else:
        for t in range(TILES):
            phi_out[TILE * t : TILE * t + TILE, :] = tiles[t]
    turned = jnp.concatenate(tiles, axis=0).T
    pieces = jnp.concatenate(split2(turned), axis=0).astype(BF16)
    column_of = iota((128, CELLS), 0)
    found_ref[...] = jnp.zeros_like(found_ref)
    for k in range(PER):
        point = point_ref[k : k + 1, :]
        hit = marks(grid_row(point), CELLS)
        found = jnp.dot(pieces, hit, preferred_element_type=F32)
        found = found[0:128, :] + found[128:256, :]
        here = (point & 127) == column_of
        found_ref[k : k + 1, :] = jnp.sum(jnp.where(here, found, 0.0), axis=0, keepdims=True)
    found = jnp.concatenate(split2(found_ref[...]), axis=0).astype(BF16)
    low = low_half(CELLS)
    for copy in fetched:
        copy.wait()
    done = []
    for j in range(PER // 2):
        cut = slice(128 * j, 128 * j + 128)
        at_node = lax.dot_general(found, flag(expander(32, j)), TN, preferred_element_type=F32)
        volt = volt_ref[:, cut]
        fresh = volt - 0.05 * (current_ref[:, cut] + at_node)
        volt_ref[:, cut] = fresh
        if last:
            part = pl.ds(128 * j, 128)
            done.append(pltpu.make_async_copy(volt_ref.at[:, part], volt_out.at[:, part], out_sem.at[j]))
            done[-1].start()
        else:
            recov = recov_ref[:, cut]
            recov_ref[:, cut] = recov + 0.05 * 0.08 * (volt + 0.7 - 0.8 * recov)
            turned = pltpu.roll(fresh, 64, 1)
            rows_ref[512 * j : 512 * j + 256, :] = jnp.where(low, fresh, turned)
            rows_ref[512 * j + 256 : 512 * j + 512, :] = jnp.where(low, turned, fresh)
    if last:
        done.append(phi_copy)
    else:
        for i, (held, target) in enumerate(((volt_ref, volt_out), (recov_ref, recov_out))):
            done.append(pltpu.make_async_copy(held, target, out_sem.at[CHUNKS + i]))
            done[-1].start()
        for copy in copies:
            copy.wait()
        sides = ((own_slots, own_scale_ref, 0), (into_slots, into_scale_ref, 8))
        done += gather_rows(rows_ref, sides, send_ref, lambda mine: send_any.at[mine], out_sem)
    for copy in done:
        copy.wait()


def shaped(*shape, dtype=F32):
    return jax.ShapeDtypeStruct(shape, dtype)


def exchange(x):
    return lax.all_to_all(x, AXES, split_axis=0, concat_axis=0, tiled=True)


def shift(x, axis, by):
    size = lax.axis_size(axis)
    return lax.ppermute(x, axis, [(i, (i + by) % size) for i in range(size)])


def on_device(
    potential,
    gating,
    ecs_start,
    templates,
    template_id,
    patch_src,
    patch_dev,
    patch_dst,
    patch_conduct,
    memb_point,
):
    flat = (8, 128)
    table = pl.pallas_call(
        setup_kernel,
        out_shape=shaped(128, 128),
        in_specs=[VMEM] * 4,
        out_specs=VMEM,
        compiler_params=PARAMS,
        name="setup",
    )(
        patch_dev.reshape(flat),
        patch_src.reshape(flat),
        patch_dst.reshape(flat),
        patch_conduct.reshape(flat),
    )
    got_table = exchange(table)
    rows_scratch = pltpu.VMEM((PER * CELLS, 128), F32)
    slot_scratch = [pltpu.SMEM((1, 128), I32)] * CAP
    slot_sem = pltpu.SemaphoreType.DMA((CAP,))
    small = shaped(16, 128, dtype=I32)
    tables_out = (small, small, shaped(16, 128), shaped(DEVS * 8, 128))
    plane = pltpu.VMEM((CELLS, NODES), F32)
    scale_scratch = pltpu.VMEM((DEVS * 8, 128), F32)
    gather_scratch = [
        rows_scratch,
        pltpu.VMEM((128, 128), F32),
        plane,
        pltpu.VMEM((DEVS, 8, 128), F32),
        scale_scratch,
        *slot_scratch,
        slot_sem,
        pltpu.SemaphoreType.DMA((2,)),
        pltpu.SemaphoreType.DMA((CHUNKS,)),
    ]
    anywhere = pl.BlockSpec(memory_space=pl.ANY)
    message = shaped(DEVS, 16, 128)
    outgoing, own, own_number, own_conduct, own_scale = pl.pallas_call(
        functools.partial(gather_kernel, False),
        out_shape=(message,) + tables_out,
        in_specs=[VMEM, anywhere],
        out_specs=(anywhere,) + (VMEM,) * 3 + (anywhere,),
        scratch_shapes=gather_scratch,
        compiler_params=PARAMS,
        name="gather_source",
    )(table, potential)
    outgoing, into, into_number, into_conduct, into_scale = pl.pallas_call(
        functools.partial(gather_kernel, True),
        out_shape=(message,) + tables_out,
        in_specs=[VMEM, anywhere, anywhere],
        out_specs=(anywhere,) + (VMEM,) * 3 + (anywhere,),
        scratch_shapes=gather_scratch,
        input_output_aliases={2: 0},
        compiler_params=PARAMS,
        name="gather_target",
    )(got_table, potential, outgoing)
    points = memb_point.reshape(CELLS, PER).T
    degree, id_wide, phi, slot_points = pl.pallas_call(
        prepare_kernel,
        out_shape=(shaped(CELLS, NODES), shaped(CELLS, 128), shaped(TILE * TILES, 128), shaped(64, 128, dtype=I32)),
        in_specs=[VMEM] * 7,
        out_specs=(VMEM,) * 4,
        scratch_shapes=[pltpu.VMEM((32, CELLS), F32), pltpu.VMEM((64, 128), F32)],
        compiler_params=PARAMS,
        name="prepare",
    )(
        into_number,
        into_conduct,
        own_number,
        own_conduct,
        template_id.reshape(2, 128),
        ecs_start.reshape(TILE * TILE, TILE),
        points,
    )

    place = jnp.stack([lax.axis_index("tx"), lax.axis_index("ty"), lax.axis_size("tx"), lax.axis_size("ty")])
    place = place.astype(I32)
    volt = potential
    recov = gating
    for step in range(STEPS):
        last = step == STEPS - 1
        got = exchange(outgoing).reshape(DEVS * 16, 128)
        base, deposit_base = pl.pallas_call(
            base_kernel,
            out_shape=(shaped(CELLS, NODES), shaped(TILE * TILES, 128)),
            in_specs=[VMEM] * 5 + [anywhere],
            out_specs=(VMEM,) * 2,
            scratch_shapes=[
                pltpu.VMEM((CELLS, NODES), BF16),
                pltpu.VMEM(templates.shape, BF16),
                pltpu.SemaphoreType.DMA((templates.shape[0],)),
            ],
            cost_estimate=pl.CostEstimate(flops=3_000_000_000, bytes_accessed=14_000_000, transcendentals=0),
            compiler_params=PARAMS,
            name="base",
        )(volt, recov, id_wide, degree, points, templates)
        deposit, x_low, x_high, y_low, y_high = pl.pallas_call(
            deposit_kernel,
            out_shape=(shaped(TILE * TILES, 128),) + (shaped(64, 128),) * 4,
            in_specs=[anywhere] + [VMEM] * 3,
            out_specs=(VMEM,) * 5,
            scratch_shapes=[pltpu.VMEM((DEVS * 16, 128), F32), pltpu.SemaphoreType.DMA((CHUNKS,))],
            compiler_params=PARAMS,
            name="deposit",
        )(got, deposit_base, slot_points, phi)

        x_before = shift(x_high, "tx", 1)
        x_after = shift(x_low, "tx", -1)
        y_low, y_high = pl.pallas_call(
            frame_kernel,
            out_shape=(shaped(80, 128),) * 2,
            in_specs=[VMEM] * 4,
            out_specs=(VMEM,) * 2,
            compiler_params=PARAMS,
            name="frame",
        )(x_before, x_after, y_low, y_high)
        y_before = shift(y_high, "ty", 1)
        y_after = shift(y_low, "ty", -1)
        current = pl.pallas_call(
            collect_kernel,
            out_shape=shaped(CELLS, NODES),
            in_specs=[VMEM] * 2 + [anywhere] * 2,
            out_specs=anywhere,
            scratch_shapes=[
                *[rows_scratch] * 8,
                *slot_scratch * 2,
                pltpu.VMEM((DEVS * 16, 128), F32),
                plane,
                slot_sem,
                slot_sem,
                pltpu.SemaphoreType.DMA((CHUNKS + 1,)),
                pltpu.SemaphoreType.DMA((PER // 2,)),
            ],
            cost_estimate=pl.CostEstimate(flops=1_000_000_000, bytes_accessed=10_000_000, transcendentals=0),
            compiler_params=PARAMS,
            name="collect",
        )(into, own, got, base)
        operands = [place, phi, deposit, x_before, x_after, y_before, y_after, current, volt, points]
        specs = [SMEM] + [VMEM] * 6 + [anywhere] * 2 + [VMEM]
        wide = [pltpu.VMEM((TILES + 2, LEAD + ROWS + 8, 128), F32)] * 2 + [pltpu.VMEM((16, CELLS), F32)]
        if last:
            volt, phi = pl.pallas_call(
                functools.partial(sweep_kernel, True),
                out_shape=(shaped(CELLS, NODES), shaped(TILE * TILE, TILE)),
                in_specs=specs,
                out_specs=(anywhere,) * 2,
                scratch_shapes=wide
                + [plane] * 2
                + [
                    pltpu.VMEM((TILE * TILE, TILE), F32),
                    pltpu.SemaphoreType.DMA((2,)),
                    pltpu.SemaphoreType.DMA((PER // 2 + 1,)),
                ],
                compiler_params=PARAMS,
                name="sweep_last",
            )(*operands)
        else:
            volt, phi, recov, outgoing = pl.pallas_call(
                functools.partial(sweep_kernel, False),
                out_shape=(shaped(CELLS, NODES), shaped(TILE * TILES, 128), shaped(CELLS, NODES), message),
                in_specs=specs + [anywhere, VMEM, anywhere, VMEM, anywhere],
                out_specs=(anywhere, VMEM, anywhere, anywhere),
                scratch_shapes=wide
                + [plane] * 3
                + [scale_scratch] * 2
                + [pltpu.VMEM((DEVS, 16, 128), F32), rows_scratch]
                + slot_scratch * 2
                + [
                    slot_sem,
                    slot_sem,
                    pltpu.SemaphoreType.DMA((5,)),
                    pltpu.SemaphoreType.DMA((CHUNKS + 2,)),
                ],
                compiler_params=PARAMS,
                name="sweep",
            )(*operands, recov, into, into_scale, own, own_scale)
    return (volt, phi.reshape(TILE, TILE, TILE))


def solution(mesh):
    return jax.shard_map(
        on_device,
        mesh=mesh,
        in_specs=(
            P(("tx", "ty"), None),
            P(("tx", "ty"), None),
            P("tx", "ty", None),
            P(),
            P(("tx", "ty")),
            P(("tx", "ty")),
            P(("tx", "ty"), None),
            P(("tx", "ty")),
            P(("tx", "ty")),
            P(("tx", "ty")),
        ),
        out_specs=(P(("tx", "ty"), None), P("tx", "ty", None)),
        check_vma=False,
    )
```

```python
import functools

import jax
import jax.numpy as jnp
from jax import lax
from jax.experimental import pallas as pl
from jax.experimental.pallas import tpu as pltpu
from jax.sharding import PartitionSpec as P

BLOCK = 64
SWEEPS = 4
STEPS = 2
CELLS = 256
NODES = 768
PER = 12
DEVS = 128
CAP = 16
TILE = 32
HALO = 4
CHUNKS = 4
TILES = 8
F32 = jnp.float32
BF16 = jnp.bfloat16
I32 = jnp.int32
AXES = ("tx", "ty")
VMEM = pl.BlockSpec(memory_space=pltpu.VMEM)
SMEM = pl.BlockSpec(memory_space=pltpu.SMEM)
NT = (((1,), (1,)), ((), ()))
TN = (((0,), (0,)), ((), ()))
PARAMS = pltpu.CompilerParams(vmem_limit_bytes=67_043_328)


def iota(shape, dim):
    return lax.broadcasted_iota(I32, shape, dim)


def low_half(rows):
    return iota((rows, 128), 1) < 64


def flag(condition):
    return condition.astype(F32).astype(BF16)


def marks(row, count):
    places = iota((count, row.shape[1]), 0).astype(F32).astype(BF16)
    return jnp.where(row.astype(F32).astype(BF16) == places, jnp.ones((), BF16), jnp.zeros((), BF16))


def regroup(number):
    value = number.astype(F32)
    cell = jnp.floor((value + 0.5) * (1.0 / PER))
    return (value - PER * cell) * CELLS + cell


def split2(x):
    hi = x.astype(BF16).astype(F32)
    return hi, x - hi


def setup_kernel(dev_ref, src_ref, dst_ref, conduct_ref, table_ref):
    device = iota((128, 128), 0)
    before = flag(device < iota((128, 128), 1))
    slots = iota((16, 128), 0)
    count = jnp.zeros((128, 1), F32)
    table = jnp.zeros((128, 128), F32)
    for q in range(8):
        hit = (dev_ref[q : q + 1, :] == device).astype(F32)
        hit_bf = hit.astype(BF16)
        running = jnp.dot(hit_bf, before, preferred_element_type=F32) + count
        rank = jnp.sum(hit * running, axis=0, keepdims=True)
        count = count + jnp.sum(hit, axis=1, keepdims=True)
        here = rank.astype(I32) == slots
        parts = []
        for ref in (dst_ref, src_ref):
            number = regroup(ref[q : q + 1, :])
            hi = jnp.floor(number * (1.0 / 64.0))
            parts += [hi, number - 64.0 * hi]
        first, rest = split2(conduct_ref[q : q + 1, :])
        second, third = split2(rest)
        parts += [first, second, third, jnp.zeros((1, 128), F32)]
        values = jnp.concatenate([jnp.where(here, part, 0.0) for part in parts], axis=0)
        table = table + lax.dot_general(hit_bf, values.astype(BF16), NT, preferred_element_type=F32)
    table_ref[...] = table


def decode(table, first_lane, scratch):
    scratch[...] = table
    lane = iota((16, 128), 1)
    out = jnp.zeros((16, 128), F32)
    for dl in range(8):
        rows = scratch[pl.ds(dl, 16, stride=8), :]
        out = jnp.where((lane >> 4) == dl, pltpu.roll(rows, (16 * dl - first_lane) % 128, 1), out)
    return out


def doubled(volt, rows_ref):
    low = low_half(CELLS)
    for j in range(PER // 2):
        pair = volt[:, 128 * j : 128 * j + 128]
        turned = pltpu.roll(pair, 64, 1)
        rows_ref[512 * j : 512 * j + 256, :] = jnp.where(low, pair, turned)
        rows_ref[512 * j + 256 : 512 * j + 512, :] = jnp.where(low, turned, pair)


def start_slots(index_ref, slots, sem):
    copies = [
        pltpu.make_async_copy(index_ref.at[pl.ds(s, 1), :], slot, sem.at[s]) for s, slot in enumerate(slots)
    ]
    for copy in copies:
        copy.start()
    return copies


def start_copies(pairs, sem):
    copies = [pltpu.make_async_copy(source, target, sem.at[i]) for i, (source, target) in enumerate(pairs)]
    for copy in copies:
        copy.start()
    return copies


def gather_rows(rows_ref, sides, out_ref, target_of, sem):
    low = low_half(1)
    copies = []
    for chunk in range(CHUNKS):
        count = DEVS // CHUNKS

        def body(i, carry, chunk=chunk, count=count):
            d = count * chunk + i
            scale_base = pl.multiple_of(d * 8, 8)
            for slots, scale_ref, first in sides:
                for p in range(8):
                    a = slots[p][0, d]
                    b = slots[p + 8][0, d]
                    row = jnp.where(low, rows_ref[pl.ds(a, 1), :], rows_ref[pl.ds(b, 1), :])
                    out_ref[d, first + p : first + p + 1, :] = row * scale_ref[pl.ds(scale_base + p, 1), :]
            return carry

        lax.fori_loop(0, count, body, 0, unroll=2)
        mine = pl.ds(count * chunk, count)
        copy = pltpu.make_async_copy(out_ref.at[mine], target_of(mine), sem.at[chunk])
        copy.start()
        copies.append(copy)
    return copies


def gather_kernel(incoming, *refs):
    if incoming:
        table_ref, volt_any, _, out_any = refs[:4]
        refs = refs[4:]
    else:
        table_ref, volt_any, out_any = refs[:3]
        refs = refs[3:]
    index_ref, scale_any, rows_ref, volt_ref, out_ref, scale_ref = refs[:6]
    slots, sem, data_sem, out_sem = refs[6:22], refs[22], refs[23], refs[24]
    (volt_copy,) = start_copies([(volt_any, volt_ref)], data_sem)
    first = 0 if incoming else 32
    table = table_ref[...]
    numbers = 64.0 * table + pltpu.roll(table, 112, 1)
    index_ref[...] = numbers.T[first : first + 16, :].astype(I32)
    copies = start_slots(index_ref, slots, sem)
    part = iota((128, 1024), 0)
    lane = iota((128, 1024), 1)
    slot = (lane >> 7) + 8 * ((lane >> 6) & 1)
    spread = flag((part >= 64) & (part < 112) & ((part & 15) == slot))
    scale = jnp.dot(table.astype(BF16), spread, preferred_element_type=F32)
    for p in range(8):
        scale_ref[pl.ds(p, DEVS, stride=8), :] = scale[:, 128 * p : 128 * p + 128]
    scale_copy = pltpu.make_async_copy(scale_ref, scale_any, data_sem.at[1])
    scale_copy.start()
    volt_copy.wait()
    doubled(volt_ref[...], rows_ref)
    for copy in copies:
        copy.wait()
    at = pl.ds(8 if incoming else 0, 8)
    done = gather_rows(rows_ref, ((slots, scale_ref, 0),), out_ref, lambda mine: out_any.at[mine, at], out_sem)
    for copy in (scale_copy, *done):
        copy.wait()


def expander(rows, j):
    return (iota((rows, 128), 0) & 15) == 2 * j + (iota((rows, 128), 1) >> 6)


def grid_row(point):
    return ((point >> 7) & 7) * TILE + (point >> 10)


def prepare_kernel(
    got_table_ref,
    table_ref,
    id_ref,
    ecs_ref,
    point_ref,
    degree_ref,
    id_out,
    phi_out,
    slot_out,
    place_ref,
    found_ref,
    scratch,
):
    kind = iota((16, 128), 0)
    place_ref[...] = jnp.zeros_like(place_ref)
    place_ref[0:PER, :] = grid_row(point_ref[...]).astype(F32)
    place_ref[16 : 16 + PER, :] = (point_ref[...] & 127).astype(F32)
    places = place_ref[...].astype(BF16)
    total = jnp.zeros((48, CELLS), F32)
    for side, ref in enumerate((got_table_ref, table_ref)):
        table = ref[...]
        index = decode(64.0 * table + pltpu.roll(table, 112, 1), 32 * side, scratch).astype(I32)
        conducts = decode(table + pltpu.roll(table, 112, 1) + pltpu.roll(table, 96, 1), 64, scratch)
        for s in range(16):
            number = index[s : s + 1, :]
            hit = marks(number & 255, CELLS)
            here = (number >> 8) == kind
            first, rest = split2(conducts[s : s + 1, :])
            second, third = split2(rest)
            values = jnp.concatenate([jnp.where(here, x, 0.0) for x in (first, second, third)], axis=0)
            total = total + lax.dot_general(values.astype(BF16), hit, NT, preferred_element_type=F32)
            found = jnp.dot(places, hit, preferred_element_type=F32)
            for part in range(2):
                picked = jnp.where(here, found[16 * part : 16 * part + 16, :], 0.0)
                at = 32 * part + 16 * side + s
                found_ref[at : at + 1, :] = jnp.sum(picked, axis=0, keepdims=True)
    upper = (iota((16, 128), 1) & 8) != 0
    for part in range(2):
        into = found_ref[32 * part : 32 * part + 16, :]
        own = found_ref[32 * part + 16 : 32 * part + 32, :]
        slot_out[32 * part : 32 * part + 16, :] = jnp.where(upper, pltpu.roll(own, 8, 1), into).astype(I32)
        slot_out[32 * part + 16 : 32 * part + 32, :] = jnp.where(upper, own, pltpu.roll(into, 120, 1)).astype(I32)
    total = total[0:16, :] + total[16:32, :] + total[32:48, :]
    first, rest = split2(total)
    second, third = split2(rest)
    pieces = jnp.concatenate([first, second, third], axis=0).astype(BF16)
    for j in range(PER // 2):
        degree_ref[:, 128 * j : 128 * j + 128] = lax.dot_general(
            pieces, flag(expander(48, j)), TN, preferred_element_type=F32
        )
    number = iota((16, 128), 0).astype(F32).astype(BF16)
    for half in range(2):
        hit = flag(id_ref[half : half + 1, :] == kind)
        id_out[128 * half : 128 * half + 128, :] = lax.dot_general(hit, number, TN, preferred_element_type=F32)
    for t in range(TILES):
        for y in range(4):
            rows = ecs_ref[pl.ds(4 * t + y, TILE, stride=TILE), :]
            phi_out[TILE * t : TILE * t + TILE, 32 * y : 32 * y + 32] = rows


def deposited(total, row, column, mean):
    hit = marks(row, CELLS)
    here = marks(column, 128)
    spread = jnp.concatenate([here * x.astype(BF16) for x in split2(mean)], axis=0)
    return total + lax.dot_general(hit, spread, NT, preferred_element_type=F32)


def base_kernel(volt_ref, recov_ref, id_ref, degree_ref, point_ref, template_ref, out_ref, deposit_ref, volt_bf, held, sem):
    count = held.shape[0]
    copies = [pltpu.make_async_copy(template_ref.at[i], held.at[i], sem.at[i]) for i in range(count)]
    for copy in copies:
        copy.start()
    volt = volt_ref[...]
    volt_bf[...] = volt.astype(BF16)
    out_ref[...] = degree_ref[...] * volt - (volt - volt * volt * volt * (1.0 / 3.0) - recov_ref[...])

    def body(i, carry):
        parts = []
        for u in range(2):
            index = 2 * i + u
            pltpu.make_async_copy(template_ref.at[index], held.at[index], sem.at[index]).wait()
            mine = id_ref[...] == index.astype(F32)
            parts += [
                jnp.where(mine, volt_bf[:, 128 * j : 128 * j + 128], jnp.zeros((), BF16))
                for j in range(PER // 2)
            ]
        both = held[pl.ds(2 * i, 2)].reshape(2 * NODES, NODES)
        out_ref[...] += jnp.dot(jnp.concatenate(parts, axis=1), both, preferred_element_type=F32)
        return carry

    lax.fori_loop(0, count // 2, body, 0)
    means = jnp.zeros((16, CELLS), F32)
    for j in range(PER // 2):
        weights = jnp.where(expander(16, j), 1.0 / BLOCK, 0.0).astype(BF16)
        parts = jnp.concatenate(split2(out_ref[:, 128 * j : 128 * j + 128]), axis=1).astype(BF16)
        weights = jnp.concatenate([weights, weights], axis=1)
        means = means + lax.dot_general(weights, parts, NT, preferred_element_type=F32)
    total = jnp.zeros((CELLS, 256), F32)
    for k in range(PER):
        point = point_ref[k : k + 1, :]
        total = deposited(total, grid_row(point), point & 127, means[k : k + 1, :])
    deposit_ref[...] = total[:, 0:128] + total[:, 128:256]


def odd_of(place_ref, axis):
    return place_ref[axis] & 1


def deposit_kernel(
    place_ref, got_any, base_any, slot_any, phi_any, deposit_ref, x_near_ref, x_far_ref, y_near_ref, y_far_ref, *scratch
):
    got_ref, base_ref, slot_ref, phi_ref, sem = scratch
    rows = got_ref.shape[0] // CHUNKS
    pieces = [pl.ds(rows * i, rows) for i in range(CHUNKS)]
    copies = start_copies(
        [(slot_any, slot_ref)]
        + [(got_any.at[piece], got_ref.at[piece]) for piece in pieces]
        + [(base_any, base_ref), (phi_any, phi_ref)],
        sem,
    )
    copies[0].wait()
    half = (iota((16, 256), 1) >> 6) & 1
    weights = jnp.where(iota((16, 256), 0) == half, 1.0 / BLOCK, 0.0).astype(BF16)
    total = jnp.zeros((CELLS, 256), F32)
    for r in range(16):
        if r % (16 // CHUNKS) == 0:
            copies[1 + r // (16 // CHUNKS)].wait()
        if r % 2 == 0:
            parts = jnp.concatenate(split2(got_ref[128 * r : 128 * r + 256, :]), axis=1).astype(BF16)
            pair = lax.dot_general(weights, parts, NT, preferred_element_type=F32)
        mean = pair[:, 128 * (r % 2) : 128 * (r % 2) + 128]

        def both(at):
            return jnp.concatenate([slot_ref[at + r : at + r + 1, :], slot_ref[at + 16 + r : at + 17 + r, :]], axis=1)

        total = deposited(total, both(0), both(32), jnp.concatenate([mean[0:1, :], mean[1:2, :]], axis=1))
    for copy in copies[1 + CHUNKS :]:
        copy.wait()
    deposit_ref[...] = base_ref[...] - (total[:, 0:128] + total[:, 128:256])
    odd_x = odd_of(place_ref, 0)
    odd_y = odd_of(place_ref, 1)
    for array, at, across in ((phi_ref, 0, 0), (deposit_ref, HALO, TILE)):
        for t in range(TILES):
            low = array[TILE * t : TILE * t + HALO, :]
            high = array[TILE * t + TILE - HALO : TILE * t + TILE, :]
            place = slice(8 * t + at, 8 * t + at + HALO)
            x_near_ref[place, :] = jnp.where(jnp.full(low.shape, odd_x) == 0, high, low)
            x_far_ref[place, :] = jnp.where(jnp.full(low.shape, odd_x) == 0, low, high)
        near = pl.multiple_of((1 - odd_y) * (TILE * (TILES - 1)), TILE)
        far = pl.multiple_of(odd_y * (TILE * (TILES - 1)), TILE)
        y_near_ref[across : across + TILE, :] = array[pl.ds(near, TILE), :]
        y_far_ref[across : across + TILE, :] = array[pl.ds(far, TILE), :]


def collect_kernel(into_ref, own_ref, got_any, base_any, out_any, *scratch):
    sums, into_slots, own_slots = scratch[0:8], scratch[8:24], scratch[24:40]
    got_ref, base_ref, into_sem, own_sem, data_sem, out_sem = scratch[40:]
    copies = start_slots(into_ref, into_slots, into_sem) + start_slots(own_ref, own_slots, own_sem)
    count = DEVS // CHUNKS
    pieces = [pl.ds(16 * count * i, 16 * count) for i in range(CHUNKS)]
    got_copies = start_copies(
        [(got_any.at[piece], got_ref.at[piece]) for piece in pieces] + [(base_any, base_ref)], data_sem
    )
    for ref in sums:
        ref[...] = jnp.zeros_like(ref)
    for copy in copies:
        copy.wait()
    for chunk in range(CHUNKS):
        got_copies[chunk].wait()

        def body(i, carry, chunk=chunk):
            d = count * chunk + i
            base = pl.multiple_of(d * 16, 16)
            for p in range(8):
                for side, slots in ((0, into_slots), (1, own_slots)):
                    row = got_ref[pl.ds(base + (8 * side + p), 1), :]
                    for half in (0, 1):
                        ref = sums[4 * (p % 2) + 2 * side + half]
                        ref[pl.ds(slots[p + 8 * half][0, d], 1), :] += row
            return carry

        lax.fori_loop(0, count, body, 0, unroll=2)
    got_copies[CHUNKS].wait()
    low = low_half(CELLS)
    out_copies = []
    for j in range(PER // 2):
        both = []
        for k in (2 * j, 2 * j + 1):
            cut = slice(CELLS * k, CELLS * k + CELLS)
            halves = [sum(ref[cut, :] for ref in sums[half::2]) for half in (0, 1)]
            rows = jnp.where(low, *halves)
            both.append(rows + pltpu.roll(rows, 64, 1))
        cut = slice(128 * j, 128 * j + 128)
        base_ref[:, cut] = base_ref[:, cut] - jnp.where(low, both[0], both[1])
        cut = pl.ds(128 * j, 128)
        copy = pltpu.make_async_copy(base_ref.at[:, cut], out_any.at[:, cut], out_sem.at[j])
        copy.start()
        out_copies.append(copy)
    for copy in out_copies:
        copy.wait()


def ordered(odd, near, far):
    is_even = jnp.full(near.shape, odd) == 0
    return jnp.where(is_even, far, near), jnp.where(is_even, near, far)


def frame_kernel(place_ref, x_near_ref, x_far_ref, y_near_ref, y_far_ref, near_ref, far_ref):
    odd_y = odd_of(place_ref, 1)
    for middle_ref, out_ref, at in ((y_near_ref, near_ref, 1 - odd_y), (y_far_ref, far_ref, odd_y)):
        rows = pl.ds(pl.multiple_of(at * (8 * (TILES - 1)), 8), 8)
        before, after = ordered(odd_of(place_ref, 0), x_near_ref[rows, :], x_far_ref[rows, :])
        out_ref[0:8, :] = before
        out_ref[8:72, :] = middle_ref[...]
        out_ref[72:80, :] = after


ROWS = TILE + 2 * HALO
LEAD = 8


def sweep_kernel(last, *refs):
    place_ref, phi_ref, deposit_ref, x_near_ref, x_far_ref, y_near_ref, y_far_ref = refs[:7]
    current_any, volt_any, point_ref = refs[7:10]
    if last:
        volt_out, phi_out, wide_phi, wide_deposit, found_ref, current_ref, volt_ref, phi_held = refs[10:18]
        data_sem, out_sem = refs[18:]
        fetched = start_copies([(current_any, current_ref), (volt_any, volt_ref)], data_sem)
    else:
        recov_any, into_ref, into_scale_any, own_ref, own_scale_any = refs[10:15]
        volt_out, phi_out, recov_out, send_any = refs[15:19]
        wide_phi, wide_deposit, found_ref, current_ref, volt_ref, recov_ref = refs[19:25]
        own_scale_ref, into_scale_ref, send_ref, rows_ref = refs[25:29]
        own_slots, into_slots = refs[29:45], refs[45:61]
        own_sem, into_sem, data_sem, out_sem = refs[61:]
        copies = start_slots(own_ref, own_slots, own_sem) + start_slots(into_ref, into_slots, into_sem)
        fetched = start_copies(
            [
                (current_any, current_ref),
                (volt_any, volt_ref),
                (recov_any, recov_ref),
                (own_scale_any, own_scale_ref),
                (into_scale_any, into_scale_ref),
            ],
            data_sem,
        )
    end = LEAD + ROWS
    high = LEAD + HALO + TILE
    x_before, x_after = ordered(odd_of(place_ref, 0), x_near_ref[...], x_far_ref[...])
    y_before, y_after = ordered(odd_of(place_ref, 1), y_near_ref[...], y_far_ref[...])
    for wide, array, at, across in ((wide_phi, phi_ref, 0, 0), (wide_deposit, deposit_ref, HALO, TILE)):
        for t in range(TILES):
            wide[t + 1, LEAD : LEAD + HALO, :] = x_before[8 * t + at : 8 * t + at + HALO, :]
            wide[t + 1, LEAD + HALO : high, :] = array[TILE * t : TILE * t + TILE, :]
            wide[t + 1, high:end, :] = x_after[8 * t + at : 8 * t + at + HALO, :]
        for t, came in ((0, y_before), (TILES + 1, y_after)):
            wide[t, LEAD : LEAD + HALO, :] = came[at : at + HALO, :]
            wide[t, LEAD + HALO : high, :] = came[8 + across : 8 + across + TILE, :]
            wide[t, high:end, :] = came[72 + at : 72 + at + HALO, :]
    shape = (ROWS, 128)
    row = iota(shape, 0)
    lane = iota(shape, 1)
    depth = lane & (TILE - 1)
    first_row = jnp.where(place_ref[0] == 0, HALO, 0)
    last_row = jnp.where(place_ref[0] == place_ref[2] - 1, HALO + TILE, ROWS)
    inside = (row >= first_row) & (row < last_row)
    first_tile = jnp.where(place_ref[1] == 0, 1, 0)
    last_tile = jnp.where(place_ref[1] == place_ref[3] - 1, TILES + 1, TILES + 2)
    scale = jnp.where(inside, 1.0 / 6.5, 0.0)
    side = [jnp.where((t >= first_tile) & (t < last_tile), 1.0, 0.0) for t in (0, TILES + 1)]
    edge = {0: scale * side[0], TILES + 1: scale * side[1]}
    for t in range(TILES + 2):
        wide_phi[t, 0:LEAD, :] = jnp.zeros((LEAD, 128), F32)
        wide_phi[t, end : end + 8, :] = jnp.zeros((8, 128), F32)
        keep = jnp.where(inside, side[0 if t == 0 else 1], 0.0) if t in edge else jnp.where(inside, 1.0, 0.0)
        wide_phi[t, LEAD:end, :] = jnp.where(keep > 0.0, wide_phi[t, LEAD:end, :], 0.0)
    nothing = jnp.zeros(shape, F32)
    for _ in range(SWEEPS):
        middle = [wide_phi[t, LEAD:end, :] for t in range(TILES + 2)]
        fresh = []
        ups = [pltpu.roll(x, 32, 1) for x in middle]
        downs = [pltpu.roll(x, 96, 1) for x in middle]
        for t in range(TILES + 2):
            total = wide_deposit[t, LEAD:end, :]
            total = total + wide_phi[t, LEAD - 1 : end - 1, :] + wide_phi[t, LEAD + 1 : end + 1, :]
            total = total + jnp.where(lane < 32, ups[t - 1] if t else nothing, ups[t])
            total = total + jnp.where(lane >= 96, downs[t + 1] if t <= TILES else nothing, downs[t])
            total = total + jnp.where(depth == 0, 0.0, pltpu.roll(middle[t], 1, 1))
            total = total + jnp.where(depth == TILE - 1, 0.0, pltpu.roll(middle[t], 127, 1))
            fresh.append(jnp.where(edge.get(t, scale) > 0.0, total * (1.0 / 6.5), 0.0))
        for t in range(TILES + 2):
            wide_phi[t, LEAD:end, :] = fresh[t]
    tiles = [wide_phi[t + 1, LEAD + HALO : high, :] for t in range(TILES)]
    if last:
        for t in range(TILES):
            for y in range(4):
                turned = tiles[t] if y == 0 else pltpu.roll(tiles[t], 128 - 32 * y, 1)
                phi_held[pl.ds(4 * t + y, TILE, stride=TILE), :] = turned[:, 0:TILE]
        phi_copy = pltpu.make_async_copy(phi_held, phi_out, out_sem.at[PER // 2])
        phi_copy.start()
    else:
        for t in range(TILES):
            phi_out[TILE * t : TILE * t + TILE, :] = tiles[t]
    turned = jnp.concatenate(tiles, axis=0).T
    pieces = jnp.concatenate(split2(turned), axis=0).astype(BF16)
    column_of = iota((128, CELLS), 0)
    found_ref[...] = jnp.zeros_like(found_ref)
    for k in range(PER):
        point = point_ref[k : k + 1, :]
        hit = marks(grid_row(point), CELLS)
        found = jnp.dot(pieces, hit, preferred_element_type=F32)
        found = found[0:128, :] + found[128:256, :]
        here = (point & 127) == column_of
        found_ref[k : k + 1, :] = jnp.sum(jnp.where(here, found, 0.0), axis=0, keepdims=True)
    found = jnp.concatenate(split2(found_ref[...]), axis=0).astype(BF16)
    low = low_half(CELLS)
    for copy in fetched:
        copy.wait()
    done = []
    for j in range(PER // 2):
        cut = slice(128 * j, 128 * j + 128)
        at_node = lax.dot_general(found, flag(expander(32, j)), TN, preferred_element_type=F32)
        volt = volt_ref[:, cut]
        fresh = volt - 0.05 * (current_ref[:, cut] + at_node)
        volt_ref[:, cut] = fresh
        if last:
            part = pl.ds(128 * j, 128)
            done.append(pltpu.make_async_copy(volt_ref.at[:, part], volt_out.at[:, part], out_sem.at[j]))
            done[-1].start()
        else:
            recov = recov_ref[:, cut]
            recov_ref[:, cut] = recov + 0.05 * 0.08 * (volt + 0.7 - 0.8 * recov)
            turned = pltpu.roll(fresh, 64, 1)
            rows_ref[512 * j : 512 * j + 256, :] = jnp.where(low, fresh, turned)
            rows_ref[512 * j + 256 : 512 * j + 512, :] = jnp.where(low, turned, fresh)
    if last:
        done.append(phi_copy)
    else:
        for i, (held, target) in enumerate(((volt_ref, volt_out), (recov_ref, recov_out))):
            done.append(pltpu.make_async_copy(held, target, out_sem.at[CHUNKS + i]))
            done[-1].start()
        for copy in copies:
            copy.wait()
        sides = ((own_slots, own_scale_ref, 0), (into_slots, into_scale_ref, 8))
        done += gather_rows(rows_ref, sides, send_ref, lambda mine: send_any.at[mine], out_sem)
    for copy in done:
        copy.wait()


def shaped(*shape, dtype=F32):
    return jax.ShapeDtypeStruct(shape, dtype)


def exchange(x):
    return lax.all_to_all(x, AXES, split_axis=0, concat_axis=0, tiled=True)


def swap(x, axis, first):
    size = lax.axis_size(axis)
    pairs = [((first + i) % size, (first + i + 1) % size) for i in range(0, size, 2)]
    return lax.ppermute(x, axis, pairs + [(j, i) for i, j in pairs])


def on_device(
    potential,
    gating,
    ecs_start,
    templates,
    template_id,
    patch_src,
    patch_dev,
    patch_dst,
    patch_conduct,
    memb_point,
):
    flat = (8, 128)
    table = pl.pallas_call(
        setup_kernel,
        out_shape=shaped(128, 128),
        in_specs=[VMEM] * 4,
        out_specs=VMEM,
        compiler_params=PARAMS,
        name="setup",
    )(
        patch_dev.reshape(flat),
        patch_src.reshape(flat),
        patch_dst.reshape(flat),
        patch_conduct.reshape(flat),
    )
    got_table = exchange(table)
    rows_scratch = pltpu.VMEM((PER * CELLS, 128), F32)
    slot_scratch = [pltpu.SMEM((1, 128), I32)] * CAP
    slot_sem = pltpu.SemaphoreType.DMA((CAP,))
    small = shaped(16, 128, dtype=I32)
    tables_out = (small, shaped(DEVS * 8, 128))
    plane = pltpu.VMEM((CELLS, NODES), F32)
    scale_scratch = pltpu.VMEM((DEVS * 8, 128), F32)
    gather_scratch = [
        rows_scratch,
        plane,
        pltpu.VMEM((DEVS, 8, 128), F32),
        scale_scratch,
        *slot_scratch,
        slot_sem,
        pltpu.SemaphoreType.DMA((2,)),
        pltpu.SemaphoreType.DMA((CHUNKS,)),
    ]
    anywhere = pl.BlockSpec(memory_space=pl.ANY)
    message = shaped(DEVS, 16, 128)
    outgoing, own, own_scale = pl.pallas_call(
        functools.partial(gather_kernel, False),
        out_shape=(message,) + tables_out,
        in_specs=[VMEM, anywhere],
        out_specs=(anywhere, VMEM, anywhere),
        scratch_shapes=gather_scratch,
        compiler_params=PARAMS,
        name="gather_source",
    )(table, potential)
    outgoing, into, into_scale = pl.pallas_call(
        functools.partial(gather_kernel, True),
        out_shape=(message,) + tables_out,
        in_specs=[VMEM, anywhere, anywhere],
        out_specs=(anywhere, VMEM, anywhere),
        scratch_shapes=gather_scratch,
        input_output_aliases={2: 0},
        compiler_params=PARAMS,
        name="gather_target",
    )(got_table, potential, outgoing)
    points = memb_point.reshape(CELLS, PER).T
    degree, id_wide, phi, slot_points = pl.pallas_call(
        prepare_kernel,
        out_shape=(shaped(CELLS, NODES), shaped(CELLS, 128), shaped(TILE * TILES, 128), shaped(64, 128, dtype=I32)),
        in_specs=[VMEM] * 5,
        out_specs=(VMEM,) * 4,
        scratch_shapes=[pltpu.VMEM((32, CELLS), F32), pltpu.VMEM((64, 128), F32), pltpu.VMEM((128, 128), F32)],
        compiler_params=PARAMS,
        name="prepare",
    )(
        got_table,
        table,
        template_id.reshape(2, 128),
        ecs_start.reshape(TILE * TILE, TILE),
        points,
    )

    place = jnp.stack([lax.axis_index("tx"), lax.axis_index("ty"), lax.axis_size("tx"), lax.axis_size("ty")])
    place = place.astype(I32)
    volt = potential
    recov = gating
    for step in range(STEPS):
        last = step == STEPS - 1
        got = exchange(outgoing).reshape(DEVS * 16, 128)
        base, deposit_base = pl.pallas_call(
            base_kernel,
            out_shape=(shaped(CELLS, NODES), shaped(TILE * TILES, 128)),
            in_specs=[VMEM] * 5 + [anywhere],
            out_specs=(VMEM,) * 2,
            scratch_shapes=[
                pltpu.VMEM((CELLS, NODES), BF16),
                pltpu.VMEM(templates.shape, BF16),
                pltpu.SemaphoreType.DMA((templates.shape[0],)),
            ],
            cost_estimate=pl.CostEstimate(flops=3_000_000_000, bytes_accessed=14_000_000, transcendentals=0),
            compiler_params=PARAMS,
            name="base",
        )(volt, recov, id_wide, degree, points, templates)
        deposit, x_near, x_far, y_near, y_far = pl.pallas_call(
            deposit_kernel,
            out_shape=(shaped(TILE * TILES, 128),) + (shaped(64, 128),) * 4,
            in_specs=[SMEM] + [anywhere] * 4,
            out_specs=(VMEM,) * 5,
            scratch_shapes=[
                pltpu.VMEM((DEVS * 16, 128), F32),
                pltpu.VMEM((TILE * TILES, 128), F32),
                pltpu.VMEM((64, 128), I32),
                pltpu.VMEM((TILE * TILES, 128), F32),
                pltpu.SemaphoreType.DMA((CHUNKS + 3,)),
            ],
            compiler_params=PARAMS,
            name="deposit",
        )(place, got, deposit_base, slot_points, phi)

        x_far = swap(x_far, "tx", 1)
        x_near = swap(x_near, "tx", 0)
        y_near, y_far = pl.pallas_call(
            frame_kernel,
            out_shape=(shaped(80, 128),) * 2,
            in_specs=[SMEM] + [VMEM] * 4,
            out_specs=(VMEM,) * 2,
            compiler_params=PARAMS,
            name="frame",
        )(place, x_near, x_far, y_near, y_far)
        y_far = swap(y_far, "ty", 1)
        y_near = swap(y_near, "ty", 0)
        current = pl.pallas_call(
            collect_kernel,
            out_shape=shaped(CELLS, NODES),
            in_specs=[VMEM] * 2 + [anywhere] * 2,
            out_specs=anywhere,
            scratch_shapes=[
                *[rows_scratch] * 8,
                *slot_scratch * 2,
                pltpu.VMEM((DEVS * 16, 128), F32),
                plane,
                slot_sem,
                slot_sem,
                pltpu.SemaphoreType.DMA((CHUNKS + 1,)),
                pltpu.SemaphoreType.DMA((PER // 2,)),
            ],
            cost_estimate=pl.CostEstimate(flops=1_000_000_000, bytes_accessed=10_000_000, transcendentals=0),
            compiler_params=PARAMS,
            name="collect",
        )(into, own, got, base)
        operands = [place, phi, deposit, x_near, x_far, y_near, y_far, current, volt, points]
        specs = [SMEM] + [VMEM] * 6 + [anywhere] * 2 + [VMEM]
        wide = [pltpu.VMEM((TILES + 2, LEAD + ROWS + 8, 128), F32)] * 2 + [pltpu.VMEM((16, CELLS), F32)]
        if last:
            volt, phi = pl.pallas_call(
                functools.partial(sweep_kernel, True),
                out_shape=(shaped(CELLS, NODES), shaped(TILE * TILE, TILE)),
                in_specs=specs,
                out_specs=(anywhere,) * 2,
                scratch_shapes=wide
                + [plane] * 2
                + [
                    pltpu.VMEM((TILE * TILE, TILE), F32),
                    pltpu.SemaphoreType.DMA((2,)),
                    pltpu.SemaphoreType.DMA((PER // 2 + 1,)),
                ],
                compiler_params=PARAMS,
                name="sweep_last",
            )(*operands)
        else:
            volt, phi, recov, outgoing = pl.pallas_call(
                functools.partial(sweep_kernel, False),
                out_shape=(shaped(CELLS, NODES), shaped(TILE * TILES, 128), shaped(CELLS, NODES), message),
                in_specs=specs + [anywhere, VMEM, anywhere, VMEM, anywhere],
                out_specs=(anywhere, VMEM, anywhere, anywhere),
                scratch_shapes=wide
                + [plane] * 3
                + [scale_scratch] * 2
                + [pltpu.VMEM((DEVS, 16, 128), F32), rows_scratch]
                + slot_scratch * 2
                + [
                    slot_sem,
                    slot_sem,
                    pltpu.SemaphoreType.DMA((5,)),
                    pltpu.SemaphoreType.DMA((CHUNKS + 2,)),
                ],
                compiler_params=PARAMS,
                name="sweep",
            )(*operands, recov, into, into_scale, own, own_scale)
    return (volt, phi.reshape(TILE, TILE, TILE))


def solution(mesh):
    return jax.shard_map(
        on_device,
        mesh=mesh,
        in_specs=(
            P(("tx", "ty"), None),
            P(("tx", "ty"), None),
            P("tx", "ty", None),
            P(),
            P(("tx", "ty")),
            P(("tx", "ty")),
            P(("tx", "ty"), None),
            P(("tx", "ty")),
            P(("tx", "ty")),
            P(("tx", "ty")),
        ),
        out_specs=(P(("tx", "ty"), None), P("tx", "ty", None)),
        check_vma=False,
    )
```

```python
import functools

import jax
import jax.numpy as jnp
from jax import lax
from jax.experimental import pallas as pl
from jax.experimental.pallas import tpu as pltpu
from jax.sharding import PartitionSpec as P

BLOCK = 64
SWEEPS = 4
STEPS = 2
CELLS = 256
NODES = 768
PER = 12
DEVS = 128
CAP = 16
TILE = 32
HALO = 4
CHUNKS = 4
TILES = 8
F32 = jnp.float32
BF16 = jnp.bfloat16
I32 = jnp.int32
AXES = ("tx", "ty")
VMEM = pl.BlockSpec(memory_space=pltpu.VMEM)
NT = (((1,), (1,)), ((), ()))
TN = (((0,), (0,)), ((), ()))
PARAMS = pltpu.CompilerParams(vmem_limit_bytes=67_043_328)


def iota(shape, dim):
    return lax.broadcasted_iota(I32, shape, dim)


def low_half(rows):
    return iota((rows, 128), 1) < 64


def flag(condition):
    return condition.astype(F32).astype(BF16)


def marks(row, count):
    places = iota((count, row.shape[1]), 0).astype(F32).astype(BF16)
    return jnp.where(row.astype(F32).astype(BF16) == places, jnp.ones((), BF16), jnp.zeros((), BF16))


def regroup(number):
    value = number.astype(F32)
    cell = jnp.floor((value + 0.5) * (1.0 / PER))
    return (value - PER * cell) * CELLS + cell


def split2(x):
    hi = x.astype(BF16).astype(F32)
    return hi, x - hi


def setup_kernel(dev_ref, src_ref, dst_ref, conduct_ref, table_ref):
    device = iota((128, 128), 0)
    before = flag(device < iota((128, 128), 1))
    slots = iota((16, 128), 0)
    count = jnp.zeros((128, 1), F32)
    table = jnp.zeros((128, 128), F32)
    for q in range(8):
        hit = (dev_ref[q : q + 1, :] == device).astype(F32)
        hit_bf = hit.astype(BF16)
        running = jnp.dot(hit_bf, before, preferred_element_type=F32) + count
        rank = jnp.sum(hit * running, axis=0, keepdims=True)
        count = count + jnp.sum(hit, axis=1, keepdims=True)
        here = rank.astype(I32) == slots
        parts = []
        for ref in (dst_ref, src_ref):
            number = regroup(ref[q : q + 1, :])
            hi = jnp.floor(number * (1.0 / 64.0))
            parts += [hi, number - 64.0 * hi]
        first, rest = split2(conduct_ref[q : q + 1, :])
        second, third = split2(rest)
        parts += [first, second, third, jnp.zeros((1, 128), F32)]
        values = jnp.concatenate([jnp.where(here, part, 0.0) for part in parts], axis=0)
        table = table + lax.dot_general(hit_bf, values.astype(BF16), NT, preferred_element_type=F32)
    table_ref[...] = table


def decode(table, first_lane, scratch):
    scratch[...] = table
    lane = iota((16, 128), 1)
    out = jnp.zeros((16, 128), F32)
    for dl in range(8):
        rows = scratch[pl.ds(dl, 16, stride=8), :]
        out = jnp.where((lane >> 4) == dl, pltpu.roll(rows, (16 * dl - first_lane) % 128, 1), out)
    return out


def doubled(volt, rows_ref):
    low = low_half(CELLS)
    for j in range(PER // 2):
        pair = volt[:, 128 * j : 128 * j + 128]
        turned = pltpu.roll(pair, 64, 1)
        rows_ref[512 * j : 512 * j + 256, :] = jnp.where(low, pair, turned)
        rows_ref[512 * j + 256 : 512 * j + 512, :] = jnp.where(low, turned, pair)


def start_slots(index_ref, slots, sem):
    copies = [
        pltpu.make_async_copy(index_ref.at[pl.ds(s, 1), :], slot, sem.at[s]) for s, slot in enumerate(slots)
    ]
    for copy in copies:
        copy.start()
    return copies


def start_copies(pairs, sem):
    copies = [pltpu.make_async_copy(source, target, sem.at[i]) for i, (source, target) in enumerate(pairs)]
    for copy in copies:
        copy.start()
    return copies


def gather_rows(rows_ref, sides, out_ref, target_of, sem):
    low = low_half(1)
    copies = []
    for chunk in range(CHUNKS):
        count = DEVS // CHUNKS

        def body(i, carry, chunk=chunk, count=count):
            d = count * chunk + i
            scale_base = pl.multiple_of(d * 8, 8)
            for slots, scale_ref, first in sides:
                for p in range(8):
                    a = slots[p][0, d]
                    b = slots[p + 8][0, d]
                    row = jnp.where(low, rows_ref[pl.ds(a, 1), :], rows_ref[pl.ds(b, 1), :])
                    out_ref[d, first + p : first + p + 1, :] = row * scale_ref[pl.ds(scale_base + p, 1), :]
            return carry

        lax.fori_loop(0, count, body, 0, unroll=2)
        mine = pl.ds(count * chunk, count)
        copy = pltpu.make_async_copy(out_ref.at[mine], target_of(mine), sem.at[chunk])
        copy.start()
        copies.append(copy)
    return copies


def gather_kernel(incoming, *refs):
    if incoming:
        table_ref, volt_any, _, out_any = refs[:4]
        refs = refs[4:]
    else:
        table_ref, volt_any, out_any = refs[:3]
        refs = refs[3:]
    index_ref, scale_any, rows_ref, volt_ref, out_ref, scale_ref = refs[:6]
    slots, sem, data_sem, out_sem = refs[6:22], refs[22], refs[23], refs[24]
    (volt_copy,) = start_copies([(volt_any, volt_ref)], data_sem)
    first = 0 if incoming else 32
    table = table_ref[...]
    numbers = 64.0 * table + pltpu.roll(table, 112, 1)
    index_ref[...] = numbers.T[first : first + 16, :].astype(I32)
    copies = start_slots(index_ref, slots, sem)
    part = iota((128, 1024), 0)
    lane = iota((128, 1024), 1)
    slot = (lane >> 7) + 8 * ((lane >> 6) & 1)
    spread = flag((part >= 64) & (part < 112) & ((part & 15) == slot))
    scale = jnp.dot(table.astype(BF16), spread, preferred_element_type=F32)
    for p in range(8):
        scale_ref[pl.ds(p, DEVS, stride=8), :] = scale[:, 128 * p : 128 * p + 128]
    scale_copy = pltpu.make_async_copy(scale_ref, scale_any, data_sem.at[1])
    scale_copy.start()
    volt_copy.wait()
    doubled(volt_ref[...], rows_ref)
    for copy in copies:
        copy.wait()
    at = pl.ds(8 if incoming else 0, 8)
    done = gather_rows(rows_ref, ((slots, scale_ref, 0),), out_ref, lambda mine: out_any.at[mine, at], out_sem)
    for copy in (scale_copy, *done):
        copy.wait()


def expander(rows, j):
    return (iota((rows, 128), 0) & 15) == 2 * j + (iota((rows, 128), 1) >> 6)


def grid_row(point):
    return ((point >> 7) & 7) * TILE + (point >> 10)


def prepare_kernel(
    got_table_ref,
    table_ref,
    id_ref,
    ecs_ref,
    point_ref,
    degree_ref,
    id_out,
    phi_out,
    slot_out,
    place_ref,
    found_ref,
    scratch,
):
    kind = iota((16, 128), 0)
    place_ref[...] = jnp.zeros_like(place_ref)
    place_ref[0:PER, :] = grid_row(point_ref[...]).astype(F32)
    place_ref[16 : 16 + PER, :] = (point_ref[...] & 127).astype(F32)
    places = place_ref[...].astype(BF16)
    total = jnp.zeros((48, CELLS), F32)
    for side, ref in enumerate((got_table_ref, table_ref)):
        table = ref[...]
        index = decode(64.0 * table + pltpu.roll(table, 112, 1), 32 * side, scratch).astype(I32)
        conducts = decode(table + pltpu.roll(table, 112, 1) + pltpu.roll(table, 96, 1), 64, scratch)
        for s in range(16):
            number = index[s : s + 1, :]
            hit = marks(number & 255, CELLS)
            here = (number >> 8) == kind
            first, rest = split2(conducts[s : s + 1, :])
            second, third = split2(rest)
            values = jnp.concatenate([jnp.where(here, x, 0.0) for x in (first, second, third)], axis=0)
            total = total + lax.dot_general(values.astype(BF16), hit, NT, preferred_element_type=F32)
            found = jnp.dot(places, hit, preferred_element_type=F32)
            for part in range(2):
                picked = jnp.where(here, found[16 * part : 16 * part + 16, :], 0.0)
                at = 32 * part + 16 * side + s
                found_ref[at : at + 1, :] = jnp.sum(picked, axis=0, keepdims=True)
    upper = (iota((16, 128), 1) & 8) != 0
    for part in range(2):
        into = found_ref[32 * part : 32 * part + 16, :]
        own = found_ref[32 * part + 16 : 32 * part + 32, :]
        slot_out[32 * part : 32 * part + 16, :] = jnp.where(upper, pltpu.roll(own, 8, 1), into).astype(I32)
        slot_out[32 * part + 16 : 32 * part + 32, :] = jnp.where(upper, own, pltpu.roll(into, 120, 1)).astype(I32)
    total = total[0:16, :] + total[16:32, :] + total[32:48, :]
    first, rest = split2(total)
    second, third = split2(rest)
    pieces = jnp.concatenate([first, second, third], axis=0).astype(BF16)
    for j in range(PER // 2):
        degree_ref[:, 128 * j : 128 * j + 128] = lax.dot_general(
            pieces, flag(expander(48, j)), TN, preferred_element_type=F32
        )
    number = iota((16, 128), 0).astype(F32).astype(BF16)
    for half in range(2):
        hit = flag(id_ref[half : half + 1, :] == kind)
        id_out[128 * half : 128 * half + 128, :] = lax.dot_general(hit, number, TN, preferred_element_type=F32)
    for t in range(TILES):
        for y in range(4):
            rows = ecs_ref[pl.ds(4 * t + y, TILE, stride=TILE), :]
            phi_out[TILE * t : TILE * t + TILE, 32 * y : 32 * y + 32] = rows


def deposited(total, row, column, mean):
    hit = marks(row, CELLS)
    here = marks(column, 128)
    spread = jnp.concatenate([here * x.astype(BF16) for x in split2(mean)], axis=0)
    return total + lax.dot_general(hit, spread, NT, preferred_element_type=F32)


def base_kernel(volt_ref, recov_ref, id_ref, degree_ref, point_ref, template_ref, out_ref, deposit_ref, volt_bf, held, sem):
    count = held.shape[0]
    copies = [pltpu.make_async_copy(template_ref.at[i], held.at[i], sem.at[i]) for i in range(count)]
    for copy in copies:
        copy.start()
    volt = volt_ref[...]
    volt_bf[...] = volt.astype(BF16)
    out_ref[...] = degree_ref[...] * volt - (volt - volt * volt * volt * (1.0 / 3.0) - recov_ref[...])

    def body(i, carry):
        parts = []
        for u in range(2):
            index = 2 * i + u
            pltpu.make_async_copy(template_ref.at[index], held.at[index], sem.at[index]).wait()
            mine = id_ref[...] == index.astype(F32)
            parts += [
                jnp.where(mine, volt_bf[:, 128 * j : 128 * j + 128], jnp.zeros((), BF16))
                for j in range(PER // 2)
            ]
        both = held[pl.ds(2 * i, 2)].reshape(2 * NODES, NODES)
        out_ref[...] += jnp.dot(jnp.concatenate(parts, axis=1), both, preferred_element_type=F32)
        return carry

    lax.fori_loop(0, count // 2, body, 0)
    means = jnp.zeros((16, CELLS), F32)
    for j in range(PER // 2):
        weights = jnp.where(expander(16, j), 1.0 / BLOCK, 0.0).astype(BF16)
        parts = jnp.concatenate(split2(out_ref[:, 128 * j : 128 * j + 128]), axis=1).astype(BF16)
        weights = jnp.concatenate([weights, weights], axis=1)
        means = means + lax.dot_general(weights, parts, NT, preferred_element_type=F32)
    total = jnp.zeros((CELLS, 256), F32)
    for k in range(PER):
        point = point_ref[k : k + 1, :]
        total = deposited(total, grid_row(point), point & 127, means[k : k + 1, :])
    deposit_ref[...] = total[:, 0:128] + total[:, 128:256]


def odd_of(axis):
    return lax.axis_index(axis) & 1


def deposit_kernel(
    got_any, base_any, slot_any, phi_any, deposit_ref, x_near_ref, x_far_ref, y_near_ref, y_far_ref, *scratch
):
    got_ref, base_ref, slot_ref, phi_ref, sem = scratch
    rows = got_ref.shape[0] // CHUNKS
    pieces = [pl.ds(rows * i, rows) for i in range(CHUNKS)]
    copies = start_copies(
        [(slot_any, slot_ref)]
        + [(got_any.at[piece], got_ref.at[piece]) for piece in pieces]
        + [(base_any, base_ref), (phi_any, phi_ref)],
        sem,
    )
    copies[0].wait()
    half = (iota((16, 256), 1) >> 6) & 1
    weights = jnp.where(iota((16, 256), 0) == half, 1.0 / BLOCK, 0.0).astype(BF16)
    total = jnp.zeros((CELLS, 256), F32)
    for r in range(16):
        if r % (16 // CHUNKS) == 0:
            copies[1 + r // (16 // CHUNKS)].wait()
        if r % 2 == 0:
            parts = jnp.concatenate(split2(got_ref[128 * r : 128 * r + 256, :]), axis=1).astype(BF16)
            pair = lax.dot_general(weights, parts, NT, preferred_element_type=F32)
        mean = pair[:, 128 * (r % 2) : 128 * (r % 2) + 128]

        def both(at):
            return jnp.concatenate([slot_ref[at + r : at + r + 1, :], slot_ref[at + 16 + r : at + 17 + r, :]], axis=1)

        total = deposited(total, both(0), both(32), jnp.concatenate([mean[0:1, :], mean[1:2, :]], axis=1))
    for copy in copies[1 + CHUNKS :]:
        copy.wait()
    deposit_ref[...] = base_ref[...] - (total[:, 0:128] + total[:, 128:256])
    odd_x = odd_of("tx")
    odd_y = odd_of("ty")
    for array, at, across in ((phi_ref, 0, 0), (deposit_ref, HALO, TILE)):
        for t in range(TILES):
            low = array[TILE * t : TILE * t + HALO, :]
            high = array[TILE * t + TILE - HALO : TILE * t + TILE, :]
            place = slice(8 * t + at, 8 * t + at + HALO)
            x_near_ref[place, :] = jnp.where(jnp.full(low.shape, odd_x) == 0, high, low)
            x_far_ref[place, :] = jnp.where(jnp.full(low.shape, odd_x) == 0, low, high)
        near = pl.multiple_of((1 - odd_y) * (TILE * (TILES - 1)), TILE)
        far = pl.multiple_of(odd_y * (TILE * (TILES - 1)), TILE)
        y_near_ref[across : across + TILE, :] = array[pl.ds(near, TILE), :]
        y_far_ref[across : across + TILE, :] = array[pl.ds(far, TILE), :]


def collect_kernel(into_ref, own_ref, got_any, base_any, out_any, *scratch):
    sums, into_slots, own_slots = scratch[0:8], scratch[8:24], scratch[24:40]
    got_ref, base_ref, into_sem, own_sem, data_sem, out_sem = scratch[40:]
    copies = start_slots(into_ref, into_slots, into_sem) + start_slots(own_ref, own_slots, own_sem)
    count = DEVS // CHUNKS
    pieces = [pl.ds(16 * count * i, 16 * count) for i in range(CHUNKS)]
    got_copies = start_copies(
        [(got_any.at[piece], got_ref.at[piece]) for piece in pieces] + [(base_any, base_ref)], data_sem
    )
    for ref in sums:
        ref[...] = jnp.zeros_like(ref)
    for copy in copies:
        copy.wait()
    for chunk in range(CHUNKS):
        got_copies[chunk].wait()

        def body(i, carry, chunk=chunk):
            d = count * chunk + i
            base = pl.multiple_of(d * 16, 16)
            for p in range(8):
                for side, slots in ((0, into_slots), (1, own_slots)):
                    row = got_ref[pl.ds(base + (8 * side + p), 1), :]
                    for half in (0, 1):
                        ref = sums[4 * (p % 2) + 2 * side + half]
                        ref[pl.ds(slots[p + 8 * half][0, d], 1), :] += row
            return carry

        lax.fori_loop(0, count, body, 0, unroll=2)
    got_copies[CHUNKS].wait()
    low = low_half(CELLS)
    out_copies = []
    for j in range(PER // 2):
        both = []
        for k in (2 * j, 2 * j + 1):
            cut = slice(CELLS * k, CELLS * k + CELLS)
            halves = [sum(ref[cut, :] for ref in sums[half::2]) for half in (0, 1)]
            rows = jnp.where(low, *halves)
            both.append(rows + pltpu.roll(rows, 64, 1))
        cut = slice(128 * j, 128 * j + 128)
        base_ref[:, cut] = base_ref[:, cut] - jnp.where(low, both[0], both[1])
        cut = pl.ds(128 * j, 128)
        copy = pltpu.make_async_copy(base_ref.at[:, cut], out_any.at[:, cut], out_sem.at[j])
        copy.start()
        out_copies.append(copy)
    for copy in out_copies:
        copy.wait()


def ordered(odd, near, far):
    is_even = jnp.full(near.shape, odd) == 0
    return jnp.where(is_even, far, near), jnp.where(is_even, near, far)


def frame_kernel(y_near_ref, y_far_ref, x_near_ref, x_far_ref, near_ref, far_ref):
    odd_x = odd_of("tx")
    for middle_ref, out_ref, high in ((x_near_ref, near_ref, 1 - odd_x), (x_far_ref, far_ref, odd_x)):
        out_ref[0:64, :] = middle_ref[...]
        for at, across in ((0, 0), (HALO, TILE)):
            rows = pl.ds(pl.multiple_of(high * (TILE - HALO) + across, HALO), HALO)
            before, after = ordered(odd_of("ty"), y_near_ref[rows, :], y_far_ref[rows, :])
            out_ref[64 + at : 64 + at + HALO, :] = before
            out_ref[72 + at : 72 + at + HALO, :] = after


ROWS = TILE + 2 * HALO
LEAD = 8


def sweep_kernel(last, *refs):
    phi_ref, deposit_ref, x_near_ref, x_far_ref, y_near_ref, y_far_ref = refs[:6]
    current_any, volt_any, point_ref = refs[6:9]
    refs = refs[9:]
    if last:
        volt_out, phi_out, wide_phi, wide_deposit, found_ref, current_ref, volt_ref, phi_held = refs[:8]
        data_sem, out_sem = refs[8:]
        fetched = start_copies([(current_any, current_ref), (volt_any, volt_ref)], data_sem)
    else:
        recov_any, into_ref, into_scale_any, own_ref, own_scale_any = refs[:5]
        volt_out, phi_out, recov_out, send_any = refs[5:9]
        wide_phi, wide_deposit, found_ref, current_ref, volt_ref, recov_ref = refs[9:15]
        own_scale_ref, into_scale_ref, send_ref, rows_ref = refs[15:19]
        own_slots, into_slots = refs[19:35], refs[35:51]
        own_sem, into_sem, data_sem, out_sem = refs[51:]
        copies = start_slots(own_ref, own_slots, own_sem) + start_slots(into_ref, into_slots, into_sem)
        fetched = start_copies(
            [
                (current_any, current_ref),
                (volt_any, volt_ref),
                (recov_any, recov_ref),
                (own_scale_any, own_scale_ref),
                (into_scale_any, into_scale_ref),
            ],
            data_sem,
        )
    end = LEAD + ROWS
    high = LEAD + HALO + TILE
    x_before, x_after = ordered(odd_of("tx"), x_near_ref[...], x_far_ref[...])
    y_before, y_after = ordered(odd_of("ty"), y_near_ref[...], y_far_ref[...])
    for wide, array, at, across in ((wide_phi, phi_ref, 0, 0), (wide_deposit, deposit_ref, HALO, TILE)):
        for t in range(TILES):
            wide[t + 1, LEAD : LEAD + HALO, :] = x_before[8 * t + at : 8 * t + at + HALO, :]
            wide[t + 1, LEAD + HALO : high, :] = array[TILE * t : TILE * t + TILE, :]
            wide[t + 1, high:end, :] = x_after[8 * t + at : 8 * t + at + HALO, :]
        for t, came, corner in ((0, y_before, 64 + at), (TILES + 1, y_after, 72 + at)):
            wide[t, LEAD : LEAD + HALO, :] = x_before[corner : corner + HALO, :]
            wide[t, LEAD + HALO : high, :] = came[across : across + TILE, :]
            wide[t, high:end, :] = x_after[corner : corner + HALO, :]
    shape = (ROWS, 128)
    row = iota(shape, 0)
    lane = iota(shape, 1)
    depth = lane & (TILE - 1)
    first_row = jnp.where(lax.axis_index("tx") == 0, HALO, 0)
    last_row = jnp.where(lax.axis_index("tx") == lax.axis_size("tx") - 1, HALO + TILE, ROWS)
    inside = (row >= first_row) & (row < last_row)
    first_tile = jnp.where(lax.axis_index("ty") == 0, 1, 0)
    last_tile = jnp.where(lax.axis_index("ty") == lax.axis_size("ty") - 1, TILES + 1, TILES + 2)
    scale = jnp.where(inside, 1.0 / 6.5, 0.0)
    side = [jnp.where((t >= first_tile) & (t < last_tile), 1.0, 0.0) for t in (0, TILES + 1)]
    edge = {0: scale * side[0], TILES + 1: scale * side[1]}
    for t in range(TILES + 2):
        wide_phi[t, 0:LEAD, :] = jnp.zeros((LEAD, 128), F32)
        wide_phi[t, end : end + 8, :] = jnp.zeros((8, 128), F32)
        keep = jnp.where(inside, side[0 if t == 0 else 1], 0.0) if t in edge else jnp.where(inside, 1.0, 0.0)
        wide_phi[t, LEAD:end, :] = jnp.where(keep > 0.0, wide_phi[t, LEAD:end, :], 0.0)
    nothing = jnp.zeros(shape, F32)
    for _ in range(SWEEPS):
        middle = [wide_phi[t, LEAD:end, :] for t in range(TILES + 2)]
        fresh = []
        ups = [pltpu.roll(x, 32, 1) for x in middle]
        downs = [pltpu.roll(x, 96, 1) for x in middle]
        for t in range(TILES + 2):
            total = wide_deposit[t, LEAD:end, :]
            total = total + wide_phi[t, LEAD - 1 : end - 1, :] + wide_phi[t, LEAD + 1 : end + 1, :]
            total = total + jnp.where(lane < 32, ups[t - 1] if t else nothing, ups[t])
            total = total + jnp.where(lane >= 96, downs[t + 1] if t <= TILES else nothing, downs[t])
            total = total + jnp.where(depth == 0, 0.0, pltpu.roll(middle[t], 1, 1))
            total = total + jnp.where(depth == TILE - 1, 0.0, pltpu.roll(middle[t], 127, 1))
            fresh.append(jnp.where(edge.get(t, scale) > 0.0, total * (1.0 / 6.5), 0.0))
        for t in range(TILES + 2):
            wide_phi[t, LEAD:end, :] = fresh[t]
    tiles = [wide_phi[t + 1, LEAD + HALO : high, :] for t in range(TILES)]
    if last:
        for t in range(TILES):
            for y in range(4):
                turned = tiles[t] if y == 0 else pltpu.roll(tiles[t], 128 - 32 * y, 1)
                phi_held[pl.ds(4 * t + y, TILE, stride=TILE), :] = turned[:, 0:TILE]
        phi_copy = pltpu.make_async_copy(phi_held, phi_out, out_sem.at[PER // 2])
        phi_copy.start()
    else:
        for t in range(TILES):
            phi_out[TILE * t : TILE * t + TILE, :] = tiles[t]
    turned = jnp.concatenate(tiles, axis=0).T
    pieces = jnp.concatenate(split2(turned), axis=0).astype(BF16)
    column_of = iota((128, CELLS), 0)
    found_ref[...] = jnp.zeros_like(found_ref)
    for k in range(PER):
        point = point_ref[k : k + 1, :]
        hit = marks(grid_row(point), CELLS)
        found = jnp.dot(pieces, hit, preferred_element_type=F32)
        found = found[0:128, :] + found[128:256, :]
        here = (point & 127) == column_of
        found_ref[k : k + 1, :] = jnp.sum(jnp.where(here, found, 0.0), axis=0, keepdims=True)
    found = jnp.concatenate(split2(found_ref[...]), axis=0).astype(BF16)
    low = low_half(CELLS)
    for copy in fetched:
        copy.wait()
    done = []
    for j in range(PER // 2):
        cut = slice(128 * j, 128 * j + 128)
        at_node = lax.dot_general(found, flag(expander(32, j)), TN, preferred_element_type=F32)
        volt = volt_ref[:, cut]
        fresh = volt - 0.05 * (current_ref[:, cut] + at_node)
        volt_ref[:, cut] = fresh
        if last:
            part = pl.ds(128 * j, 128)
            done.append(pltpu.make_async_copy(volt_ref.at[:, part], volt_out.at[:, part], out_sem.at[j]))
            done[-1].start()
        else:
            recov = recov_ref[:, cut]
            recov_ref[:, cut] = recov + 0.05 * 0.08 * (volt + 0.7 - 0.8 * recov)
            turned = pltpu.roll(fresh, 64, 1)
            rows_ref[512 * j : 512 * j + 256, :] = jnp.where(low, fresh, turned)
            rows_ref[512 * j + 256 : 512 * j + 512, :] = jnp.where(low, turned, fresh)
    if last:
        done.append(phi_copy)
    else:
        for i, (held, target) in enumerate(((volt_ref, volt_out), (recov_ref, recov_out))):
            done.append(pltpu.make_async_copy(held, target, out_sem.at[CHUNKS + i]))
            done[-1].start()
        for copy in copies:
            copy.wait()
        sides = ((own_slots, own_scale_ref, 0), (into_slots, into_scale_ref, 8))
        done += gather_rows(rows_ref, sides, send_ref, lambda mine: send_any.at[mine], out_sem)
    for copy in done:
        copy.wait()


def shaped(*shape, dtype=F32):
    return jax.ShapeDtypeStruct(shape, dtype)


def exchange(x):
    return lax.all_to_all(x, AXES, split_axis=0, concat_axis=0, tiled=True)


def swap(x, axis, first):
    size = lax.axis_size(axis)
    pairs = [(i, i + 1) for i in range(first, size - 1, 2)]
    ends = [(i, i) for i in range(size) if not any(i in pair for pair in pairs)]
    return lax.ppermute(x, axis, pairs + [(j, i) for i, j in pairs] + ends)


def on_device(
    potential,
    gating,
    ecs_start,
    templates,
    template_id,
    patch_src,
    patch_dev,
    patch_dst,
    patch_conduct,
    memb_point,
):
    flat = (8, 128)
    table = pl.pallas_call(
        setup_kernel,
        out_shape=shaped(128, 128),
        in_specs=[VMEM] * 4,
        out_specs=VMEM,
        compiler_params=PARAMS,
        name="setup",
    )(
        patch_dev.reshape(flat),
        patch_src.reshape(flat),
        patch_dst.reshape(flat),
        patch_conduct.reshape(flat),
    )
    got_table = exchange(table)
    rows_scratch = pltpu.VMEM((PER * CELLS, 128), F32)
    slot_scratch = [pltpu.SMEM((1, 128), I32)] * CAP
    slot_sem = pltpu.SemaphoreType.DMA((CAP,))
    small = shaped(16, 128, dtype=I32)
    tables_out = (small, shaped(DEVS * 8, 128))
    plane = pltpu.VMEM((CELLS, NODES), F32)
    scale_scratch = pltpu.VMEM((DEVS * 8, 128), F32)
    gather_scratch = [
        rows_scratch,
        plane,
        pltpu.VMEM((DEVS, 8, 128), F32),
        scale_scratch,
        *slot_scratch,
        slot_sem,
        pltpu.SemaphoreType.DMA((2,)),
        pltpu.SemaphoreType.DMA((CHUNKS,)),
    ]
    anywhere = pl.BlockSpec(memory_space=pl.ANY)
    message = shaped(DEVS, 16, 128)
    outgoing, own, own_scale = pl.pallas_call(
        functools.partial(gather_kernel, False),
        out_shape=(message,) + tables_out,
        in_specs=[VMEM, anywhere],
        out_specs=(anywhere, VMEM, anywhere),
        scratch_shapes=gather_scratch,
        compiler_params=PARAMS,
        name="gather_source",
    )(table, potential)
    outgoing, into, into_scale = pl.pallas_call(
        functools.partial(gather_kernel, True),
        out_shape=(message,) + tables_out,
        in_specs=[VMEM, anywhere, anywhere],
        out_specs=(anywhere, VMEM, anywhere),
        scratch_shapes=gather_scratch,
        input_output_aliases={2: 0},
        compiler_params=PARAMS,
        name="gather_target",
    )(got_table, potential, outgoing)
    points = memb_point.reshape(CELLS, PER).T
    degree, id_wide, phi, slot_points = pl.pallas_call(
        prepare_kernel,
        out_shape=(shaped(CELLS, NODES), shaped(CELLS, 128), shaped(TILE * TILES, 128), shaped(64, 128, dtype=I32)),
        in_specs=[VMEM] * 5,
        out_specs=(VMEM,) * 4,
        scratch_shapes=[pltpu.VMEM((32, CELLS), F32), pltpu.VMEM((64, 128), F32), pltpu.VMEM((128, 128), F32)],
        compiler_params=PARAMS,
        name="prepare",
    )(
        got_table,
        table,
        template_id.reshape(2, 128),
        ecs_start.reshape(TILE * TILE, TILE),
        points,
    )

    volt = potential
    recov = gating
    for step in range(STEPS):
        last = step == STEPS - 1
        got = exchange(outgoing).reshape(DEVS * 16, 128)
        base, deposit_base = pl.pallas_call(
            base_kernel,
            out_shape=(shaped(CELLS, NODES), shaped(TILE * TILES, 128)),
            in_specs=[VMEM] * 5 + [anywhere],
            out_specs=(VMEM,) * 2,
            scratch_shapes=[
                pltpu.VMEM((CELLS, NODES), BF16),
                pltpu.VMEM(templates.shape, BF16),
                pltpu.SemaphoreType.DMA((templates.shape[0],)),
            ],
            cost_estimate=pl.CostEstimate(flops=3_000_000_000, bytes_accessed=14_000_000, transcendentals=0),
            compiler_params=PARAMS,
            name="base",
        )(volt, recov, id_wide, degree, points, templates)
        deposit, x_near, x_far, y_near, y_far = pl.pallas_call(
            deposit_kernel,
            out_shape=(shaped(TILE * TILES, 128),) + (shaped(64, 128),) * 4,
            in_specs=[anywhere] * 4,
            out_specs=(VMEM,) * 5,
            scratch_shapes=[
                pltpu.VMEM((DEVS * 16, 128), F32),
                pltpu.VMEM((TILE * TILES, 128), F32),
                pltpu.VMEM((64, 128), I32),
                pltpu.VMEM((TILE * TILES, 128), F32),
                pltpu.SemaphoreType.DMA((CHUNKS + 3,)),
            ],
            compiler_params=PARAMS,
            name="deposit",
        )(got, deposit_base, slot_points, phi)

        y_far = swap(y_far, "ty", 1)
        y_near = swap(y_near, "ty", 0)
        x_near, x_far = pl.pallas_call(
            frame_kernel,
            out_shape=(shaped(80, 128),) * 2,
            in_specs=[VMEM] * 4,
            out_specs=(VMEM,) * 2,
            compiler_params=PARAMS,
            name="frame",
        )(y_near, y_far, x_near, x_far)
        x_far = swap(x_far, "tx", 1)
        x_near = swap(x_near, "tx", 0)
        current = pl.pallas_call(
            collect_kernel,
            out_shape=shaped(CELLS, NODES),
            in_specs=[VMEM] * 2 + [anywhere] * 2,
            out_specs=anywhere,
            scratch_shapes=[
                *[rows_scratch] * 8,
                *slot_scratch * 2,
                pltpu.VMEM((DEVS * 16, 128), F32),
                plane,
                slot_sem,
                slot_sem,
                pltpu.SemaphoreType.DMA((CHUNKS + 1,)),
                pltpu.SemaphoreType.DMA((PER // 2,)),
            ],
            cost_estimate=pl.CostEstimate(flops=1_000_000_000, bytes_accessed=10_000_000, transcendentals=0),
            compiler_params=PARAMS,
            name="collect",
        )(into, own, got, base)
        operands = [phi, deposit, x_near, x_far, y_near, y_far, current, volt, points]
        specs = [VMEM] * 6 + [anywhere] * 2 + [VMEM]
        wide = [pltpu.VMEM((TILES + 2, LEAD + ROWS + 8, 128), F32)] * 2 + [pltpu.VMEM((16, CELLS), F32)]
        if last:
            volt, phi = pl.pallas_call(
                functools.partial(sweep_kernel, True),
                out_shape=(shaped(CELLS, NODES), shaped(TILE * TILE, TILE)),
                in_specs=specs,
                out_specs=(anywhere,) * 2,
                scratch_shapes=wide
                + [plane] * 2
                + [
                    pltpu.VMEM((TILE * TILE, TILE), F32),
                    pltpu.SemaphoreType.DMA((2,)),
                    pltpu.SemaphoreType.DMA((PER // 2 + 1,)),
                ],
                compiler_params=PARAMS,
                name="sweep_last",
            )(*operands)
        else:
            volt, phi, recov, outgoing = pl.pallas_call(
                functools.partial(sweep_kernel, False),
                out_shape=(shaped(CELLS, NODES), shaped(TILE * TILES, 128), shaped(CELLS, NODES), message),
                in_specs=specs + [anywhere, VMEM, anywhere, VMEM, anywhere],
                out_specs=(anywhere, VMEM, anywhere, anywhere),
                scratch_shapes=wide
                + [plane] * 3
                + [scale_scratch] * 2
                + [pltpu.VMEM((DEVS, 16, 128), F32), rows_scratch]
                + slot_scratch * 2
                + [
                    slot_sem,
                    slot_sem,
                    pltpu.SemaphoreType.DMA((5,)),
                    pltpu.SemaphoreType.DMA((CHUNKS + 2,)),
                ],
                compiler_params=PARAMS,
                name="sweep",
            )(*operands, recov, into, into_scale, own, own_scale)
    return (volt, phi.reshape(TILE, TILE, TILE))


def solution(mesh):
    return jax.shard_map(
        on_device,
        mesh=mesh,
        in_specs=(
            P(("tx", "ty"), None),
            P(("tx", "ty"), None),
            P("tx", "ty", None),
            P(),
            P(("tx", "ty")),
            P(("tx", "ty")),
            P(("tx", "ty"), None),
            P(("tx", "ty")),
            P(("tx", "ty")),
            P(("tx", "ty")),
        ),
        out_specs=(P(("tx", "ty"), None), P("tx", "ty", None)),
        check_vma=False,
    )
```

```python
import functools

import jax
import jax.numpy as jnp
from jax import lax
from jax.experimental import pallas as pl
from jax.experimental.pallas import tpu as pltpu
from jax.sharding import PartitionSpec as P

BLOCK = 64
SWEEPS = 4
STEPS = 2
CELLS = 256
NODES = 768
PER = 12
DEVS = 128
CAP = 16
TILE = 32
HALO = 4
CHUNKS = 4
TILES = 8
F32 = jnp.float32
BF16 = jnp.bfloat16
I32 = jnp.int32
AXES = ("tx", "ty")
VMEM = pl.BlockSpec(memory_space=pltpu.VMEM)
NT = (((1,), (1,)), ((), ()))
TN = (((0,), (0,)), ((), ()))
PARAMS = pltpu.CompilerParams(vmem_limit_bytes=67_043_328)


def iota(shape, dim):
    return lax.broadcasted_iota(I32, shape, dim)


def low_half(rows):
    return iota((rows, 128), 1) < 64


def flag(condition):
    return condition.astype(F32).astype(BF16)


def marks(row, count):
    places = iota((count, row.shape[1]), 0).astype(F32).astype(BF16)
    return jnp.where(row.astype(F32).astype(BF16) == places, jnp.ones((), BF16), jnp.zeros((), BF16))


def regroup(number):
    value = number.astype(F32)
    cell = jnp.floor((value + 0.5) * (1.0 / PER))
    return (value - PER * cell) * CELLS + cell


def split2(x):
    hi = x.astype(BF16).astype(F32)
    return hi, x - hi


def setup_kernel(dev_ref, src_ref, dst_ref, conduct_ref, table_ref):
    device = iota((128, 128), 0)
    before = flag(device < iota((128, 128), 1))
    slots = iota((16, 128), 0)
    count = jnp.zeros((128, 1), F32)
    table = jnp.zeros((128, 128), F32)
    for q in range(8):
        hit = (dev_ref[q : q + 1, :] == device).astype(F32)
        hit_bf = hit.astype(BF16)
        running = jnp.dot(hit_bf, before, preferred_element_type=F32) + count
        rank = jnp.sum(hit * running, axis=0, keepdims=True)
        count = count + jnp.sum(hit, axis=1, keepdims=True)
        here = rank.astype(I32) == slots
        parts = []
        for ref in (dst_ref, src_ref):
            number = regroup(ref[q : q + 1, :])
            hi = jnp.floor(number * (1.0 / 64.0))
            parts += [hi, number - 64.0 * hi]
        first, rest = split2(conduct_ref[q : q + 1, :])
        second, third = split2(rest)
        parts += [first, second, third, jnp.zeros((1, 128), F32)]
        values = jnp.concatenate([jnp.where(here, part, 0.0) for part in parts], axis=0)
        table = table + lax.dot_general(hit_bf, values.astype(BF16), NT, preferred_element_type=F32)
    table_ref[...] = table


def decode(table, first_lane, scratch):
    scratch[...] = table
    lane = iota((16, 128), 1)
    out = jnp.zeros((16, 128), F32)
    for dl in range(8):
        rows = scratch[pl.ds(dl, 16, stride=8), :]
        out = jnp.where((lane >> 4) == dl, pltpu.roll(rows, (16 * dl - first_lane) % 128, 1), out)
    return out


def doubled(volt, rows_ref):
    low = low_half(CELLS)
    for j in range(PER // 2):
        pair = volt[:, 128 * j : 128 * j + 128]
        turned = pltpu.roll(pair, 64, 1)
        rows_ref[512 * j : 512 * j + 256, :] = jnp.where(low, pair, turned)
        rows_ref[512 * j + 256 : 512 * j + 512, :] = jnp.where(low, turned, pair)


def start_slots(index_ref, slots, sem):
    copies = [
        pltpu.make_async_copy(index_ref.at[pl.ds(s, 1), :], slot, sem.at[s]) for s, slot in enumerate(slots)
    ]
    for copy in copies:
        copy.start()
    return copies


def start_copies(pairs, sem):
    copies = [pltpu.make_async_copy(source, target, sem.at[i]) for i, (source, target) in enumerate(pairs)]
    for copy in copies:
        copy.start()
    return copies


def gather_rows(rows_ref, sides, out_ref, target_of, sem):
    low = low_half(1)
    copies = []
    for chunk in range(CHUNKS):
        count = DEVS // CHUNKS

        def body(i, carry, chunk=chunk, count=count):
            d = count * chunk + i
            scale_base = pl.multiple_of(d * 8, 8)
            for slots, scale_ref, first in sides:
                for p in range(8):
                    a = slots[p][0, d]
                    b = slots[p + 8][0, d]
                    row = jnp.where(low, rows_ref[pl.ds(a, 1), :], rows_ref[pl.ds(b, 1), :])
                    out_ref[d, first + p : first + p + 1, :] = row * scale_ref[pl.ds(scale_base + p, 1), :]
            return carry

        lax.fori_loop(0, count, body, 0, unroll=2)
        mine = pl.ds(count * chunk, count)
        copy = pltpu.make_async_copy(out_ref.at[mine], target_of(mine), sem.at[chunk])
        copy.start()
        copies.append(copy)
    return copies


def gather_kernel(incoming, *refs):
    if incoming:
        table_ref, volt_any, _, out_any = refs[:4]
        refs = refs[4:]
    else:
        table_ref, volt_any, out_any = refs[:3]
        refs = refs[3:]
    index_ref, scale_any, rows_ref, volt_ref, out_ref, scale_ref = refs[:6]
    slots, sem, data_sem, out_sem = refs[6:22], refs[22], refs[23], refs[24]
    (volt_copy,) = start_copies([(volt_any, volt_ref)], data_sem)
    first = 0 if incoming else 32
    table = table_ref[...]
    numbers = 64.0 * table + pltpu.roll(table, 112, 1)
    index_ref[...] = numbers.T[first : first + 16, :].astype(I32)
    copies = start_slots(index_ref, slots, sem)
    part = iota((128, 1024), 0)
    lane = iota((128, 1024), 1)
    slot = (lane >> 7) + 8 * ((lane >> 6) & 1)
    spread = flag((part >= 64) & (part < 112) & ((part & 15) == slot))
    scale = jnp.dot(table.astype(BF16), spread, preferred_element_type=F32)
    for p in range(8):
        scale_ref[pl.ds(p, DEVS, stride=8), :] = scale[:, 128 * p : 128 * p + 128]
    scale_copy = pltpu.make_async_copy(scale_ref, scale_any, data_sem.at[1])
    scale_copy.start()
    volt_copy.wait()
    doubled(volt_ref[...], rows_ref)
    for copy in copies:
        copy.wait()
    at = pl.ds(8 if incoming else 0, 8)
    done = gather_rows(rows_ref, ((slots, scale_ref, 0),), out_ref, lambda mine: out_any.at[mine, at], out_sem)
    for copy in (scale_copy, *done):
        copy.wait()


def expander(rows, j):
    return (iota((rows, 128), 0) & 15) == 2 * j + (iota((rows, 128), 1) >> 6)


def grid_row(point):
    return ((point >> 7) & 7) * TILE + (point >> 10)


def prepare_kernel(
    got_table_ref,
    table_ref,
    id_ref,
    ecs_ref,
    point_ref,
    degree_ref,
    id_out,
    phi_out,
    slot_out,
    place_ref,
    found_ref,
    scratch,
):
    kind = iota((16, 128), 0)
    place_ref[...] = jnp.zeros_like(place_ref)
    place_ref[0:PER, :] = grid_row(point_ref[...]).astype(F32)
    place_ref[16 : 16 + PER, :] = (point_ref[...] & 127).astype(F32)
    places = place_ref[...].astype(BF16)
    total = jnp.zeros((48, CELLS), F32)
    for side, ref in enumerate((got_table_ref, table_ref)):
        table = ref[...]
        index = decode(64.0 * table + pltpu.roll(table, 112, 1), 32 * side, scratch).astype(I32)
        conducts = decode(table + pltpu.roll(table, 112, 1) + pltpu.roll(table, 96, 1), 64, scratch)
        for s in range(16):
            number = index[s : s + 1, :]
            hit = marks(number & 255, CELLS)
            here = (number >> 8) == kind
            first, rest = split2(conducts[s : s + 1, :])
            second, third = split2(rest)
            values = jnp.concatenate([jnp.where(here, x, 0.0) for x in (first, second, third)], axis=0)
            total = total + lax.dot_general(values.astype(BF16), hit, NT, preferred_element_type=F32)
            found = jnp.dot(places, hit, preferred_element_type=F32)
            for part in range(2):
                picked = jnp.where(here, found[16 * part : 16 * part + 16, :], 0.0)
                at = 32 * part + 16 * side + s
                found_ref[at : at + 1, :] = jnp.sum(picked, axis=0, keepdims=True)
    upper = (iota((16, 128), 1) & 8) != 0
    for part in range(2):
        into = found_ref[32 * part : 32 * part + 16, :]
        own = found_ref[32 * part + 16 : 32 * part + 32, :]
        slot_out[32 * part : 32 * part + 16, :] = jnp.where(upper, pltpu.roll(own, 8, 1), into).astype(I32)
        slot_out[32 * part + 16 : 32 * part + 32, :] = jnp.where(upper, own, pltpu.roll(into, 120, 1)).astype(I32)
    total = total[0:16, :] + total[16:32, :] + total[32:48, :]
    first, rest = split2(total)
    second, third = split2(rest)
    pieces = jnp.concatenate([first, second, third], axis=0).astype(BF16)
    for j in range(PER // 2):
        degree_ref[:, 128 * j : 128 * j + 128] = lax.dot_general(
            pieces, flag(expander(48, j)), TN, preferred_element_type=F32
        )
    number = iota((16, 128), 0).astype(F32).astype(BF16)
    for half in range(2):
        hit = flag(id_ref[half : half + 1, :] == kind)
        id_out[128 * half : 128 * half + 128, :] = lax.dot_general(hit, number, TN, preferred_element_type=F32)
    for t in range(TILES):
        for y in range(4):
            rows = ecs_ref[pl.ds(4 * t + y, TILE, stride=TILE), :]
            phi_out[TILE * t : TILE * t + TILE, 32 * y : 32 * y + 32] = rows


def deposited(total, row, column, mean):
    hit = marks(row, CELLS)
    here = marks(column, 128)
    spread = jnp.concatenate([here * x.astype(BF16) for x in split2(mean)], axis=0)
    return total + lax.dot_general(hit, spread, NT, preferred_element_type=F32)


def base_kernel(volt_ref, recov_ref, id_ref, degree_ref, point_ref, template_ref, out_ref, deposit_ref, volt_bf, held, sem):
    count = held.shape[0]
    copies = [pltpu.make_async_copy(template_ref.at[i], held.at[i], sem.at[i]) for i in range(count)]
    for copy in copies:
        copy.start()
    volt = volt_ref[...]
    volt_bf[...] = volt.astype(BF16)
    out_ref[...] = degree_ref[...] * volt - (volt - volt * volt * volt * (1.0 / 3.0) - recov_ref[...])

    def body(i, carry):
        parts = []
        for u in range(2):
            index = 2 * i + u
            pltpu.make_async_copy(template_ref.at[index], held.at[index], sem.at[index]).wait()
            mine = id_ref[...] == index.astype(F32)
            parts += [
                jnp.where(mine, volt_bf[:, 128 * j : 128 * j + 128], jnp.zeros((), BF16))
                for j in range(PER // 2)
            ]
        both = held[pl.ds(2 * i, 2)].reshape(2 * NODES, NODES)
        out_ref[...] += jnp.dot(jnp.concatenate(parts, axis=1), both, preferred_element_type=F32)
        return carry

    lax.fori_loop(0, count // 2, body, 0)
    means = jnp.zeros((16, CELLS), F32)
    for j in range(PER // 2):
        weights = jnp.where(expander(16, j), 1.0 / BLOCK, 0.0).astype(BF16)
        parts = jnp.concatenate(split2(out_ref[:, 128 * j : 128 * j + 128]), axis=1).astype(BF16)
        weights = jnp.concatenate([weights, weights], axis=1)
        means = means + lax.dot_general(weights, parts, NT, preferred_element_type=F32)
    total = jnp.zeros((CELLS, 256), F32)
    for k in range(PER):
        point = point_ref[k : k + 1, :]
        total = deposited(total, grid_row(point), point & 127, means[k : k + 1, :])
    deposit_ref[...] = total[:, 0:128] + total[:, 128:256]


def odd_of(axis):
    return lax.axis_index(axis) & 1


def deposit_kernel(
    got_any, base_any, slot_any, phi_any, deposit_ref, x_near_ref, x_far_ref, y_near_ref, y_far_ref, *scratch
):
    got_ref, base_ref, slot_ref, phi_ref, sem = scratch
    rows = got_ref.shape[0] // CHUNKS
    pieces = [pl.ds(rows * i, rows) for i in range(CHUNKS)]
    copies = start_copies(
        [(slot_any, slot_ref)]
        + [(got_any.at[piece], got_ref.at[piece]) for piece in pieces]
        + [(base_any, base_ref), (phi_any, phi_ref)],
        sem,
    )
    copies[0].wait()
    half = (iota((16, 256), 1) >> 6) & 1
    weights = jnp.where(iota((16, 256), 0) == half, 1.0 / BLOCK, 0.0).astype(BF16)
    total = jnp.zeros((CELLS, 256), F32)
    for r in range(16):
        if r % (16 // CHUNKS) == 0:
            copies[1 + r // (16 // CHUNKS)].wait()
        if r % 2 == 0:
            parts = jnp.concatenate(split2(got_ref[128 * r : 128 * r + 256, :]), axis=1).astype(BF16)
            pair = lax.dot_general(weights, parts, NT, preferred_element_type=F32)
        mean = pair[:, 128 * (r % 2) : 128 * (r % 2) + 128]

        def both(at):
            return jnp.concatenate([slot_ref[at + r : at + r + 1, :], slot_ref[at + 16 + r : at + 17 + r, :]], axis=1)

        total = deposited(total, both(0), both(32), jnp.concatenate([mean[0:1, :], mean[1:2, :]], axis=1))
    for copy in copies[1 + CHUNKS :]:
        copy.wait()
    deposit_ref[...] = base_ref[...] - (total[:, 0:128] + total[:, 128:256])
    odd_x = odd_of("tx")
    odd_y = odd_of("ty")
    for array, at, across in ((phi_ref, 0, 0), (deposit_ref, HALO, TILE)):
        for t in range(TILES):
            low = array[TILE * t : TILE * t + HALO, :]
            high = array[TILE * t + TILE - HALO : TILE * t + TILE, :]
            place = slice(8 * t + at, 8 * t + at + HALO)
            x_near_ref[place, :] = jnp.where(jnp.full(low.shape, odd_x) == 0, high, low)
            x_far_ref[place, :] = jnp.where(jnp.full(low.shape, odd_x) == 0, low, high)
        near = pl.multiple_of((1 - odd_y) * (TILE * (TILES - 1)), TILE)
        far = pl.multiple_of(odd_y * (TILE * (TILES - 1)), TILE)
        y_near_ref[across : across + TILE, :] = array[pl.ds(near, TILE), :]
        y_far_ref[across : across + TILE, :] = array[pl.ds(far, TILE), :]


def collect_kernel(into_ref, own_ref, got_any, base_any, out_any, *scratch):
    sums, into_slots, own_slots = scratch[0:8], scratch[8:24], scratch[24:40]
    got_ref, base_ref, into_sem, own_sem, data_sem, out_sem = scratch[40:]
    copies = start_slots(into_ref, into_slots, into_sem) + start_slots(own_ref, own_slots, own_sem)
    count = DEVS // CHUNKS
    pieces = [pl.ds(16 * count * i, 16 * count) for i in range(CHUNKS)]
    got_copies = start_copies(
        [(got_any.at[piece], got_ref.at[piece]) for piece in pieces] + [(base_any, base_ref)], data_sem
    )
    for ref in sums:
        ref[...] = jnp.zeros_like(ref)
    for copy in copies:
        copy.wait()
    for chunk in range(CHUNKS):
        got_copies[chunk].wait()

        def body(i, carry, chunk=chunk):
            d = count * chunk + i
            base = pl.multiple_of(d * 16, 16)
            for p in range(8):
                for side, slots in ((0, into_slots), (1, own_slots)):
                    row = got_ref[pl.ds(base + (8 * side + p), 1), :]
                    for half in (0, 1):
                        ref = sums[4 * (p % 2) + 2 * side + half]
                        ref[pl.ds(slots[p + 8 * half][0, d], 1), :] += row
            return carry

        lax.fori_loop(0, count, body, 0, unroll=2)
    got_copies[CHUNKS].wait()
    low = low_half(CELLS)
    out_copies = []
    for j in range(PER // 2):
        both = []
        for k in (2 * j, 2 * j + 1):
            cut = slice(CELLS * k, CELLS * k + CELLS)
            halves = [sum(ref[cut, :] for ref in sums[half::2]) for half in (0, 1)]
            rows = jnp.where(low, *halves)
            both.append(rows + pltpu.roll(rows, 64, 1))
        cut = slice(128 * j, 128 * j + 128)
        base_ref[:, cut] = base_ref[:, cut] - jnp.where(low, both[0], both[1])
        cut = pl.ds(128 * j, 128)
        copy = pltpu.make_async_copy(base_ref.at[:, cut], out_any.at[:, cut], out_sem.at[j])
        copy.start()
        out_copies.append(copy)
    for copy in out_copies:
        copy.wait()


def ordered(odd, near, far):
    is_even = jnp.full(near.shape, odd) == 0
    return jnp.where(is_even, far, near), jnp.where(is_even, near, far)


def frame_kernel(y_near_ref, y_far_ref, x_near_ref, x_far_ref, near_ref, far_ref):
    odd_x = odd_of("tx")
    for middle_ref, out_ref, high in ((x_near_ref, near_ref, 1 - odd_x), (x_far_ref, far_ref, odd_x)):
        out_ref[0:64, :] = middle_ref[...]
        for at, across in ((0, 0), (HALO, TILE)):
            rows = pl.ds(pl.multiple_of(high * (TILE - HALO) + across, HALO), HALO)
            before, after = ordered(odd_of("ty"), y_near_ref[rows, :], y_far_ref[rows, :])
            out_ref[64 + at : 64 + at + HALO, :] = before
            out_ref[72 + at : 72 + at + HALO, :] = after


ROWS = TILE + 2 * HALO
LEAD = 8


def sweep_kernel(last, *refs):
    phi_ref, deposit_ref, x_near_ref, x_far_ref, y_near_ref, y_far_ref = refs[:6]
    current_any, volt_any, point_ref = refs[6:9]
    refs = refs[9:]
    if last:
        volt_out, phi_out, wide_phi, wide_deposit, found_ref, current_ref, volt_ref, phi_held = refs[:8]
        data_sem, out_sem = refs[8:]
        fetched = start_copies([(current_any, current_ref), (volt_any, volt_ref)], data_sem)
    else:
        recov_any, into_ref, into_scale_any, own_ref, own_scale_any = refs[:5]
        volt_out, phi_out, recov_out, send_any = refs[5:9]
        wide_phi, wide_deposit, found_ref, current_ref, volt_ref, recov_ref = refs[9:15]
        own_scale_ref, into_scale_ref, send_ref, rows_ref = refs[15:19]
        own_slots, into_slots = refs[19:35], refs[35:51]
        own_sem, into_sem, data_sem, out_sem = refs[51:]
        copies = start_slots(own_ref, own_slots, own_sem) + start_slots(into_ref, into_slots, into_sem)
        fetched = start_copies(
            [
                (current_any, current_ref),
                (volt_any, volt_ref),
                (recov_any, recov_ref),
                (own_scale_any, own_scale_ref),
                (into_scale_any, into_scale_ref),
            ],
            data_sem,
        )
    end = LEAD + ROWS
    high = LEAD + HALO + TILE
    x_before, x_after = ordered(odd_of("tx"), x_near_ref[...], x_far_ref[...])
    y_before, y_after = ordered(odd_of("ty"), y_near_ref[...], y_far_ref[...])
    for wide, array, at, across in ((wide_phi, phi_ref, 0, 0), (wide_deposit, deposit_ref, HALO, TILE)):
        for t in range(TILES):
            wide[t + 1, LEAD : LEAD + HALO, :] = x_before[8 * t + at : 8 * t + at + HALO, :]
            wide[t + 1, LEAD + HALO : high, :] = array[TILE * t : TILE * t + TILE, :]
            wide[t + 1, high:end, :] = x_after[8 * t + at : 8 * t + at + HALO, :]
        for t, came, corner in ((0, y_before, 64 + at), (TILES + 1, y_after, 72 + at)):
            wide[t, LEAD : LEAD + HALO, :] = x_before[corner : corner + HALO, :]
            wide[t, LEAD + HALO : high, :] = came[across : across + TILE, :]
            wide[t, high:end, :] = x_after[corner : corner + HALO, :]
    shape = (ROWS, 128)
    row = iota(shape, 0)
    lane = iota(shape, 1)
    depth = lane & (TILE - 1)
    first_row = jnp.where(lax.axis_index("tx") == 0, HALO, 0)
    last_row = jnp.where(lax.axis_index("tx") == lax.axis_size("tx") - 1, HALO + TILE, ROWS)
    inside = (row >= first_row) & (row < last_row)
    first_tile = jnp.where(lax.axis_index("ty") == 0, 1, 0)
    last_tile = jnp.where(lax.axis_index("ty") == lax.axis_size("ty") - 1, TILES + 1, TILES + 2)
    scale = jnp.where(inside, 1.0 / 6.5, 0.0)
    side = [jnp.where((t >= first_tile) & (t < last_tile), 1.0, 0.0) for t in (0, TILES + 1)]
    edge = {0: scale * side[0], TILES + 1: scale * side[1]}
    for t in range(TILES + 2):
        wide_phi[t, 0:LEAD, :] = jnp.zeros((LEAD, 128), F32)
        wide_phi[t, end : end + 8, :] = jnp.zeros((8, 128), F32)
        keep = jnp.where(inside, side[0 if t == 0 else 1], 0.0) if t in edge else jnp.where(inside, 1.0, 0.0)
        wide_phi[t, LEAD:end, :] = jnp.where(keep > 0.0, wide_phi[t, LEAD:end, :], 0.0)
    nothing = jnp.zeros(shape, F32)
    for _ in range(SWEEPS):
        middle = [wide_phi[t, LEAD:end, :] for t in range(TILES + 2)]
        fresh = []
        ups = [pltpu.roll(x, 32, 1) for x in middle]
        downs = [pltpu.roll(x, 96, 1) for x in middle]
        for t in range(TILES + 2):
            total = wide_deposit[t, LEAD:end, :]
            total = total + wide_phi[t, LEAD - 1 : end - 1, :] + wide_phi[t, LEAD + 1 : end + 1, :]
            total = total + jnp.where(lane < 32, ups[t - 1] if t else nothing, ups[t])
            total = total + jnp.where(lane >= 96, downs[t + 1] if t <= TILES else nothing, downs[t])
            total = total + jnp.where(depth == 0, 0.0, pltpu.roll(middle[t], 1, 1))
            total = total + jnp.where(depth == TILE - 1, 0.0, pltpu.roll(middle[t], 127, 1))
            fresh.append(jnp.where(edge.get(t, scale) > 0.0, total * (1.0 / 6.5), 0.0))
        for t in range(TILES + 2):
            wide_phi[t, LEAD:end, :] = fresh[t]
    tiles = [wide_phi[t + 1, LEAD + HALO : high, :] for t in range(TILES)]
    if last:
        for t in range(TILES):
            for y in range(4):
                turned = tiles[t] if y == 0 else pltpu.roll(tiles[t], 128 - 32 * y, 1)
                phi_held[pl.ds(4 * t + y, TILE, stride=TILE), :] = turned[:, 0:TILE]
        phi_copy = pltpu.make_async_copy(phi_held, phi_out, out_sem.at[PER // 2])
        phi_copy.start()
    else:
        for t in range(TILES):
            phi_out[TILE * t : TILE * t + TILE, :] = tiles[t]
    turned = jnp.concatenate(tiles, axis=0).T
    pieces = jnp.concatenate(split2(turned), axis=0).astype(BF16)
    column_of = iota((128, CELLS), 0)
    found_ref[...] = jnp.zeros_like(found_ref)
    for k in range(PER):
        point = point_ref[k : k + 1, :]
        hit = marks(grid_row(point), CELLS)
        found = jnp.dot(pieces, hit, preferred_element_type=F32)
        found = found[0:128, :] + found[128:256, :]
        here = (point & 127) == column_of
        found_ref[k : k + 1, :] = jnp.sum(jnp.where(here, found, 0.0), axis=0, keepdims=True)
    found = jnp.concatenate(split2(found_ref[...]), axis=0).astype(BF16)
    low = low_half(CELLS)
    for copy in fetched:
        copy.wait()
    done = []
    for j in range(PER // 2):
        cut = slice(128 * j, 128 * j + 128)
        at_node = lax.dot_general(found, flag(expander(32, j)), TN, preferred_element_type=F32)
        volt = volt_ref[:, cut]
        fresh = volt - 0.05 * (current_ref[:, cut] + at_node)
        volt_ref[:, cut] = fresh
        if last:
            part = pl.ds(128 * j, 128)
            done.append(pltpu.make_async_copy(volt_ref.at[:, part], volt_out.at[:, part], out_sem.at[j]))
            done[-1].start()
        else:
            recov = recov_ref[:, cut]
            recov_ref[:, cut] = recov + 0.05 * 0.08 * (volt + 0.7 - 0.8 * recov)
            turned = pltpu.roll(fresh, 64, 1)
            rows_ref[512 * j : 512 * j + 256, :] = jnp.where(low, fresh, turned)
            rows_ref[512 * j + 256 : 512 * j + 512, :] = jnp.where(low, turned, fresh)
    if last:
        done.append(phi_copy)
    else:
        for i, (held, target) in enumerate(((volt_ref, volt_out), (recov_ref, recov_out))):
            done.append(pltpu.make_async_copy(held, target, out_sem.at[CHUNKS + i]))
            done[-1].start()
        for copy in copies:
            copy.wait()
        sides = ((own_slots, own_scale_ref, 0), (into_slots, into_scale_ref, 8))
        done += gather_rows(rows_ref, sides, send_ref, lambda mine: send_any.at[mine], out_sem)
    for copy in done:
        copy.wait()


def shaped(*shape, dtype=F32):
    return jax.ShapeDtypeStruct(shape, dtype)


def exchange(x):
    return lax.all_to_all(x, AXES, split_axis=0, concat_axis=0, tiled=True)


def swap(x, axis, first):
    size = lax.axis_size(axis)
    pairs = [((first + i) % size, (first + i + 1) % size) for i in range(0, size, 2)]
    return lax.ppermute(x, axis, pairs + [(j, i) for i, j in pairs])


def on_device(
    potential,
    gating,
    ecs_start,
    templates,
    template_id,
    patch_src,
    patch_dev,
    patch_dst,
    patch_conduct,
    memb_point,
):
    flat = (8, 128)
    table = pl.pallas_call(
        setup_kernel,
        out_shape=shaped(128, 128),
        in_specs=[VMEM] * 4,
        out_specs=VMEM,
        compiler_params=PARAMS,
        name="setup",
    )(
        patch_dev.reshape(flat),
        patch_src.reshape(flat),
        patch_dst.reshape(flat),
        patch_conduct.reshape(flat),
    )
    got_table = exchange(table)
    rows_scratch = pltpu.VMEM((PER * CELLS, 128), F32)
    slot_scratch = [pltpu.SMEM((1, 128), I32)] * CAP
    slot_sem = pltpu.SemaphoreType.DMA((CAP,))
    small = shaped(16, 128, dtype=I32)
    tables_out = (small, shaped(DEVS * 8, 128))
    plane = pltpu.VMEM((CELLS, NODES), F32)
    scale_scratch = pltpu.VMEM((DEVS * 8, 128), F32)
    gather_scratch = [
        rows_scratch,
        plane,
        pltpu.VMEM((DEVS, 8, 128), F32),
        scale_scratch,
        *slot_scratch,
        slot_sem,
        pltpu.SemaphoreType.DMA((2,)),
        pltpu.SemaphoreType.DMA((CHUNKS,)),
    ]
    anywhere = pl.BlockSpec(memory_space=pl.ANY)
    message = shaped(DEVS, 16, 128)
    outgoing, own, own_scale = pl.pallas_call(
        functools.partial(gather_kernel, False),
        out_shape=(message,) + tables_out,
        in_specs=[VMEM, anywhere],
        out_specs=(anywhere, VMEM, anywhere),
        scratch_shapes=gather_scratch,
        compiler_params=PARAMS,
        name="gather_source",
    )(table, potential)
    outgoing, into, into_scale = pl.pallas_call(
        functools.partial(gather_kernel, True),
        out_shape=(message,) + tables_out,
        in_specs=[VMEM, anywhere, anywhere],
        out_specs=(anywhere, VMEM, anywhere),
        scratch_shapes=gather_scratch,
        input_output_aliases={2: 0},
        compiler_params=PARAMS,
        name="gather_target",
    )(got_table, potential, outgoing)
    points = memb_point.reshape(CELLS, PER).T
    degree, id_wide, phi, slot_points = pl.pallas_call(
        prepare_kernel,
        out_shape=(shaped(CELLS, NODES), shaped(CELLS, 128), shaped(TILE * TILES, 128), shaped(64, 128, dtype=I32)),
        in_specs=[VMEM] * 5,
        out_specs=(VMEM,) * 4,
        scratch_shapes=[pltpu.VMEM((32, CELLS), F32), pltpu.VMEM((64, 128), F32), pltpu.VMEM((128, 128), F32)],
        compiler_params=PARAMS,
        name="prepare",
    )(
        got_table,
        table,
        template_id.reshape(2, 128),
        ecs_start.reshape(TILE * TILE, TILE),
        points,
    )

    volt = potential
    recov = gating
    for step in range(STEPS):
        last = step == STEPS - 1
        got = exchange(outgoing).reshape(DEVS * 16, 128)
        base, deposit_base = pl.pallas_call(
            base_kernel,
            out_shape=(shaped(CELLS, NODES), shaped(TILE * TILES, 128)),
            in_specs=[VMEM] * 5 + [anywhere],
            out_specs=(VMEM,) * 2,
            scratch_shapes=[
                pltpu.VMEM((CELLS, NODES), BF16),
                pltpu.VMEM(templates.shape, BF16),
                pltpu.SemaphoreType.DMA((templates.shape[0],)),
            ],
            cost_estimate=pl.CostEstimate(flops=3_000_000_000, bytes_accessed=14_000_000, transcendentals=0),
            compiler_params=PARAMS,
            name="base",
        )(volt, recov, id_wide, degree, points, templates)
        deposit, x_near, x_far, y_near, y_far = pl.pallas_call(
            deposit_kernel,
            out_shape=(shaped(TILE * TILES, 128),) + (shaped(64, 128),) * 4,
            in_specs=[anywhere] * 4,
            out_specs=(VMEM,) * 5,
            scratch_shapes=[
                pltpu.VMEM((DEVS * 16, 128), F32),
                pltpu.VMEM((TILE * TILES, 128), F32),
                pltpu.VMEM((64, 128), I32),
                pltpu.VMEM((TILE * TILES, 128), F32),
                pltpu.SemaphoreType.DMA((CHUNKS + 3,)),
            ],
            compiler_params=PARAMS,
            name="deposit",
        )(got, deposit_base, slot_points, phi)

        y_far = swap(y_far, "ty", 1)
        y_near = swap(y_near, "ty", 0)
        x_near, x_far = pl.pallas_call(
            frame_kernel,
            out_shape=(shaped(80, 128),) * 2,
            in_specs=[VMEM] * 4,
            out_specs=(VMEM,) * 2,
            compiler_params=PARAMS,
            name="frame",
        )(y_near, y_far, x_near, x_far)
        x_far = swap(x_far, "tx", 1)
        x_near = swap(x_near, "tx", 0)
        current = pl.pallas_call(
            collect_kernel,
            out_shape=shaped(CELLS, NODES),
            in_specs=[VMEM] * 2 + [anywhere] * 2,
            out_specs=anywhere,
            scratch_shapes=[
                *[rows_scratch] * 8,
                *slot_scratch * 2,
                pltpu.VMEM((DEVS * 16, 128), F32),
                plane,
                slot_sem,
                slot_sem,
                pltpu.SemaphoreType.DMA((CHUNKS + 1,)),
                pltpu.SemaphoreType.DMA((PER // 2,)),
            ],
            cost_estimate=pl.CostEstimate(flops=1_000_000_000, bytes_accessed=10_000_000, transcendentals=0),
            compiler_params=PARAMS,
            name="collect",
        )(into, own, got, base)
        operands = [phi, deposit, x_near, x_far, y_near, y_far, current, volt, points]
        specs = [VMEM] * 6 + [anywhere] * 2 + [VMEM]
        wide = [pltpu.VMEM((TILES + 2, LEAD + ROWS + 8, 128), F32)] * 2 + [pltpu.VMEM((16, CELLS), F32)]
        if last:
            volt, phi = pl.pallas_call(
                functools.partial(sweep_kernel, True),
                out_shape=(shaped(CELLS, NODES), shaped(TILE * TILE, TILE)),
                in_specs=specs,
                out_specs=(anywhere,) * 2,
                scratch_shapes=wide
                + [plane] * 2
                + [
                    pltpu.VMEM((TILE * TILE, TILE), F32),
                    pltpu.SemaphoreType.DMA((2,)),
                    pltpu.SemaphoreType.DMA((PER // 2 + 1,)),
                ],
                compiler_params=PARAMS,
                name="sweep_last",
            )(*operands)
        else:
            volt, phi, recov, outgoing = pl.pallas_call(
                functools.partial(sweep_kernel, False),
                out_shape=(shaped(CELLS, NODES), shaped(TILE * TILES, 128), shaped(CELLS, NODES), message),
                in_specs=specs + [anywhere, VMEM, anywhere, VMEM, anywhere],
                out_specs=(anywhere, VMEM, anywhere, anywhere),
                scratch_shapes=wide
                + [plane] * 3
                + [scale_scratch] * 2
                + [pltpu.VMEM((DEVS, 16, 128), F32), rows_scratch]
                + slot_scratch * 2
                + [
                    slot_sem,
                    slot_sem,
                    pltpu.SemaphoreType.DMA((5,)),
                    pltpu.SemaphoreType.DMA((CHUNKS + 2,)),
                ],
                compiler_params=PARAMS,
                name="sweep",
            )(*operands, recov, into, into_scale, own, own_scale)
    return (volt, phi.reshape(TILE, TILE, TILE))


def solution(mesh):
    return jax.shard_map(
        on_device,
        mesh=mesh,
        in_specs=(
            P(("tx", "ty"), None),
            P(("tx", "ty"), None),
            P("tx", "ty", None),
            P(),
            P(("tx", "ty")),
            P(("tx", "ty")),
            P(("tx", "ty"), None),
            P(("tx", "ty")),
            P(("tx", "ty")),
            P(("tx", "ty")),
        ),
        out_specs=(P(("tx", "ty"), None), P("tx", "ty", None)),
        check_vma=False,
    )
```
